32 devices in a mesh: groups: 2 (over x), tm: 8 (over z, y), space: 2 (over core).
Axes of the slice: x: 2, y: 2, z: 4, core: 2. Of those that a mesh axis runs over, the one named last changes fastest.
Arguments:
- video: bfloat16 [32, 16, 64, 1152], P(('groups', 'tm'), 'space'), parts along dimension 0, may hold values from -6 to 6
- w_query: bfloat16 [1152, 1152], replicated, may hold values from -0.1875 to 0.1875
- w_key: bfloat16 [1152, 1152], replicated, may hold values from -0.1875 to 0.1875
- w_value: bfloat16 [1152, 1152], replicated, may hold values from -0.1875 to 0.1875
- w_out: bfloat16 [1152, 1152], replicated, may hold values from -0.1875 to 0.1875
- w_latent: bfloat16 [1152, 128], replicated, may hold values from -0.1875 to 0.1875
- conv_weight: bfloat16 [3, 3, 128, 256], replicated, may hold values from -0.1875 to 0.1875
- conv_bias: float32 [256], replicated, may hold values from -3 to 3
Outputs:
- decoded: bfloat16 [32, 32, 128, 256], P('groups', 'space', 'tm'), parts along dimension 0
The draws below stay inside these ranges and needn't reach their ends.
There are 2 independent parts, one for each index of `groups`. The reference program is written for one: setup_inputs(seed, part) draws one part's arguments, and reference() takes and returns one part's arrays. A program takes and returns all parts, laid end to end along the dimension named above; an argument that names none is the same for every part. Nothing has to cross between parts.
All inputs are finite; a program needn't handle non-finite values.
Results may differ from the reference program's by a relative error of at most 0.008.
Values may be sent and summed in bfloat16 or wider, within the bound.
No kernel may reach another device: no remote copies, remote signals or barrier semaphores. Data moves between devices by JAX's collectives and lax.ppermute only.
A program may use at most 128 MiB of HBM per device.

```python
import jax
import jax.numpy as jnp
from jax import lax

HEADS = 9
HEAD = 128
D = 1152
C = 128
CO = 256
ROWS = 16
COLS = 64
FRAMES = 16


def steps_of(key, dims, pieces, least, high):
    factor_of = 1.0
    for dim, parts in pieces:
        steps = jax.random.uniform(jax.random.fold_in(jax.random.fold_in(key, 6), dim), (parts,), jnp.float32, least / len(pieces), high / len(pieces))
        factor_of = factor_of * jnp.repeat(jnp.exp(steps), dims[dim] // parts).reshape((-1,) + (1,) * (len(dims) - 1 - dim))
    return factor_of


def centred(own_key, dims, width, bound, split=(), kind=jnp.bfloat16):
    array = width * jax.random.normal(own_key, dims, jnp.float32)
    if split:
        array = array * steps_of(own_key, dims, split, -0.22, 0.18)
    return jnp.clip(array, -bound, bound).astype(kind)


def setup_inputs(seed: int = 0, part: int = 0) -> dict:
    key_list = jax.random.split(jax.random.key(seed), 9)
    part_keys = jax.random.split(jax.random.fold_in(key_list[8], part), 9)
    return {
        "video": centred(part_keys[0], (FRAMES, ROWS, COLS, D), 1.0, 6.0, ((0, 8), (1, 2))),
        "w_query": centred(key_list[1], (D, D), D ** -0.5, 0.1875),
        "w_key": centred(key_list[2], (D, D), D ** -0.5, 0.1875),
        "w_value": centred(key_list[3], (D, D), D ** -0.5, 0.1875),
        "w_out": centred(key_list[4], (D, D), D ** -0.5, 0.1875),
        "w_latent": centred(key_list[5], (D, C), D ** -0.5, 0.1875),
        "conv_weight": centred(key_list[6], (3, 3, C, CO), (9 * C) ** -0.5, 0.1875),
        "conv_bias": centred(key_list[7], (CO,), 0.5, 3.0, (), jnp.float32),
    }


def features(values):
    return (jax.nn.elu(values) + 1.0).astype(jnp.bfloat16)

def rms_scale(values):
    return values * lax.rsqrt(lax.optimization_barrier(jnp.mean(values * values, axis=-1, keepdims=True)) + 1e-06)

def reference(video, w_query, w_key, w_value, w_out, w_latent, conv_weight, conv_bias):
    frame_count = video.shape[0]
    flat_video = video.reshape(-1, video.shape[3])
    shaped = (frame_count, -1, HEADS, HEAD)
    query_feat = features(jnp.dot(flat_video, w_query, preferred_element_type=jnp.float32)).reshape(shaped)
    key_feat = features(jnp.dot(flat_video, w_key, preferred_element_type=jnp.float32)).reshape(shaped)
    value_rows = jnp.dot(flat_video, w_value, preferred_element_type=jnp.float32).astype(jnp.bfloat16).reshape(shaped)
    frame_states = jnp.einsum('fthi,fthj->fhij', key_feat.astype(jnp.float32), value_rows.astype(jnp.float32), precision=lax.Precision.HIGHEST)
    used_states = jnp.cumsum(frame_states, axis=0).astype(jnp.bfloat16)
    attended = jnp.einsum('fthi,fhij->fthj', query_feat.astype(jnp.float32), used_states.astype(jnp.float32), precision=lax.Precision.HIGHEST)
    head_out = rms_scale(attended).astype(jnp.bfloat16).reshape(flat_video.shape)
    residual_sum = flat_video.astype(jnp.float32) + jnp.dot(head_out, w_out, preferred_element_type=jnp.float32)
    normed = rms_scale(residual_sum).astype(jnp.bfloat16)
    latent = jnp.dot(normed, w_latent, preferred_element_type=jnp.float32).astype(jnp.bfloat16)
    latent = latent.reshape(frame_count, video.shape[1], video.shape[2], -1)
    enlarged = jnp.repeat(jnp.repeat(latent, 2, axis=1), 2, axis=2)
    padded = jnp.pad(enlarged, ((0, 0), (1, 1), (1, 1), (0, 0)))
    mapped = lax.conv_general_dilated(padded, conv_weight, (1, 1), 'VALID', dimension_numbers=('NHWC', 'HWIO', 'NHWC'), preferred_element_type=jnp.float32)
    return jax.nn.silu(mapped + conv_bias).astype(jnp.bfloat16)
```

```python
import functools

import jax
import jax.numpy as jnp
from jax import lax
from jax.experimental import pallas as pl
from jax.experimental.pallas import tpu as pltpu
from jax.sharding import PartitionSpec as P

HEAD = 128
SPACE = 2
EPS = 1e-06
BF16 = jnp.bfloat16
F32 = jnp.float32


IN_HBM = pl.BlockSpec(memory_space=pltpu.HBM)
IN_VMEM = pl.BlockSpec(memory_space=pltpu.VMEM)
IN_SMEM = pl.BlockSpec(memory_space=pltpu.SMEM)


def shape(dims, dtype):
    return jax.ShapeDtypeStruct(dims, dtype)


def params(megabytes):
    return pltpu.CompilerParams(vmem_limit_bytes=megabytes << 20)


def matmul(a, b):
    return jnp.dot(a, b, preferred_element_type=F32)


def features(x):
    return jnp.where(x > 0.0, x + 1.0, jnp.exp(jnp.minimum(x, 0.0)))


def states_kernel(
    frames, core, video_hbm, wk_hbm, wv_hbm,
    parts_out, mine_out, theirs_out,
    video, wk, wv, key, value, video_sem, wk_sem, wv_sem,
):
    per = video.shape[0] // frames
    heads = wk.shape[1] // HEAD
    half = HEAD // 2

    def weight_copies(h):
        cols = pl.ds(pl.multiple_of(h * HEAD, HEAD), HEAD)
        return (
            pltpu.make_async_copy(wk_hbm.at[:, cols], wk.at[:, cols], wk_sem.at[h]),
            pltpu.make_async_copy(wv_hbm.at[:, cols], wv.at[:, cols], wv_sem.at[h]),
        )

    def video_copy(f):
        rows = pl.ds(f * per, per)
        return pltpu.make_async_copy(video_hbm.at[rows], video.at[rows], video_sem.at[f])

    for c in weight_copies(0):
        c.start()
    for f in range(frames):
        video_copy(f).start()
    for h in range(1, heads):
        for c in weight_copies(h):
            c.start()
    for f in range(frames):
        video_copy(f).wait()

    def project(h, carry):
        for c in weight_copies(h):
            c.wait()
        cols = pl.ds(pl.multiple_of(h * HEAD, HEAD), HEAD)
        both = jnp.concatenate([wk[:, cols], wv[:, cols]], axis=1)
        for f in range(frames):
            rows = slice(f * per, (f + 1) * per)
            kv = matmul(video[rows, :], both)
            key[h, rows, :] = features(kv[:, :HEAD]).astype(BF16)
            value[h, rows, :] = kv[:, HEAD:].astype(BF16)
        return carry

    lax.fori_loop(0, heads, project, 0)
    low = core[0] == 0
    for h in range(heads):
        total = None
        for f in range(frames):
            rows = slice(f * per, (f + 1) * per)
            state = lax.dot_general(
                key[h, rows, :], value[h, rows, :], (((0,), (0,)), ((), ())),
                preferred_element_type=F32,
            )
            parts_out[f, h] = state.astype(BF16)
            total = state if total is None else total + state
        mine_out[h] = jnp.where(low, total[:half], total[half:])
        theirs_out[h] = jnp.where(low, total[half:], total[:half]).astype(BF16)


def states_call(core, video, wk, wv, frames):
    tokens, d = video.shape
    heads = d // HEAD
    half = (heads, HEAD // 2, HEAD)
    return pl.pallas_call(
        functools.partial(states_kernel, frames),
        out_shape=[
            shape((frames, heads, HEAD, HEAD), BF16),
            shape(half, F32),
            shape(half, BF16),
        ],
        in_specs=[IN_SMEM, IN_HBM, IN_HBM, IN_HBM],
        out_specs=[IN_VMEM] * 3,
        scratch_shapes=[
            pltpu.VMEM((tokens, d), BF16),
            pltpu.VMEM((d, d), BF16),
            pltpu.VMEM((d, d), BF16),
            pltpu.VMEM((heads, tokens, HEAD), BF16),
            pltpu.VMEM((heads, tokens, HEAD), BF16),
            pltpu.SemaphoreType.DMA((frames,)),
            pltpu.SemaphoreType.DMA((heads,)),
            pltpu.SemaphoreType.DMA((heads,)),
        ],
        name="states",
        compiler_params=params(28),
    )(core, video, wk, wv)


def query_kernel(video, w, out):
    out[...] = features(matmul(video[...], w[...])).astype(BF16)


def query_call(video, w, first, width):
    tokens, d = video.shape
    return pl.pallas_call(
        query_kernel,
        out_shape=shape((tokens, width), BF16),
        grid=(1,),
        in_specs=[
            pl.BlockSpec((tokens, d), lambda i: (0, 0)),
            pl.BlockSpec((d, width), lambda i: (0, first // width)),
        ],
        out_specs=pl.BlockSpec((tokens, width), lambda i: (0, 0)),
        name="query",
        compiler_params=params(24),
    )(video, w)


def latent_kernel(
    frames, columns, tiles, core, video, query_parts, parts, other_parts, carry, other_carry,
    w_out, w_latent, out, used, head_out, latent,
):
    tokens, d = video.shape
    per = tokens // frames
    heads = d // HEAD
    half = HEAD // 2
    low = core[0] == 0
    used[...] = jnp.zeros_like(used)
    for h in range(heads):
        mine, theirs = carry[h].astype(F32), other_carry[h].astype(F32)
        running = jnp.concatenate(
            [jnp.where(low, mine, theirs), jnp.where(low, theirs, mine)], axis=0
        )
        at = (h % 2) * HEAD
        for f in range(frames):
            running = running + parts[f, h].astype(F32) + other_parts[f, h].astype(F32)
            used[f, h // 2, at : at + HEAD, at : at + HEAD] = running.astype(BF16)

    for f in range(frames):
        rows = slice(f * per, (f + 1) * per)
        for p in range(pl.cdiv(heads, 2)):
            width = min(2, heads - 2 * p) * HEAD
            query = query_parts[p // 2 if len(query_parts) > 1 else 0]
            first = 2 * p * HEAD - (p // 2 * 4 * HEAD if len(query_parts) > 1 else 0)
            attended = matmul(
                query[rows, first : first + width], used[f, p, :width, :width]
            )
            for h in range(width // HEAD):
                one = attended[:, h * HEAD : (h + 1) * HEAD]
                scale = lax.rsqrt(jnp.mean(one * one, axis=1, keepdims=True) + EPS)
                at = (2 * p + h) * HEAD
                head_out[rows, at : at + HEAD] = (one * scale).astype(BF16)
        summed = video[rows, :].astype(F32) + matmul(head_out[rows, :], w_out[...])
        scale = lax.rsqrt(jnp.mean(summed * summed, axis=1, keepdims=True) + EPS)
        latent[rows, :] = matmul((summed * scale).astype(BF16), w_latent[...])

    own = columns // tiles
    grid_rows = per // columns
    main = grid_rows * frames * own
    for t in range(tiles):
        for r in range(grid_rows):
            block = [
                latent[pl.ds(f * per + r * columns + t * own, own), :] for f in range(frames)
            ]
            at = r * frames * own
            out[t, at : at + frames * own, :] = jnp.concatenate(block, axis=0).astype(BF16)
        sides = []
        for column in (t * own - 1, (t + 1) * own):
            for f in range(frames):
                if 0 <= column < columns:
                    at = f * per + column
                    sides.append(latent[pl.ds(at, grid_rows, stride=columns), :])
                else:
                    sides.append(jnp.zeros((grid_rows, out.shape[2]), F32))
        at = main
        out[t, main:, :] = jnp.concatenate(sides, axis=0).astype(BF16)


def latent_call(core, video, queries, parts, other_parts, carry, other_carry, w_out, w_latent,
                frames, columns, tiles):
    tokens, d = video.shape
    channels = w_latent.shape[1]
    heads = d // HEAD
    own = columns // tiles
    rows = tokens // columns * (own + 2)
    n = len(queries)

    def kernel(core, video, *refs):
        latent_kernel(frames, columns, tiles, core, video, refs[:n], *refs[n:])

    return pl.pallas_call(
        kernel,
        out_shape=shape((tiles, rows, channels), BF16),
        in_specs=[IN_SMEM] + [IN_VMEM] * (n + 7),
        out_specs=IN_VMEM,
        scratch_shapes=[
            pltpu.VMEM((frames, pl.cdiv(heads, 2), 2 * HEAD, 2 * HEAD), BF16),
            pltpu.VMEM((tokens, d), BF16),
            pltpu.VMEM((tokens, channels), F32),
        ],
        name="latent",
        compiler_params=params(36),
    )(core, video, *queries, parts, other_parts, carry, other_carry, w_out, w_latent)


def decode_kernel(
    frames, tiles, grid_rows, own, blocks, before, after, weight, bias,
    out, left, middle, right, taps, wide,
):
    group = frames * own
    main = grid_rows * group
    column = lax.broadcasted_iota(jnp.int32, (group, 1), 0) % own
    channels = weight.shape[2]

    def place(row, t, body, sides):
        at = slice(t * group, (t + 1) * group)
        first = jnp.concatenate(
            [jnp.broadcast_to(sides[f : f + 1], (own, channels)) for f in range(frames)], axis=0
        )
        last = jnp.concatenate(
            [jnp.broadcast_to(sides[frames + f : frames + f + 1], (own, channels))
             for f in range(frames)], axis=0
        )
        down = pltpu.roll(body, 1, 0)
        up = pltpu.roll(body, group - 1, 0)
        left[row, at, :] = jnp.where(column == 0, first, down).astype(BF16)
        middle[row, at, :] = body.astype(BF16)
        right[row, at, :] = jnp.where(column == own - 1, last, up).astype(BF16)

    for t in range(tiles):
        everything = blocks[t].astype(F32)
        for r in range(grid_rows):
            body = everything[r * group : (r + 1) * group]
            sides = [
                everything[main + s * grid_rows + r : main + s * grid_rows + r + 1]
                for s in range(2 * frames)
            ]
            place(r + 1, t, body, jnp.concatenate(sides, axis=0))
        for row, ref in ((0, before), (grid_rows + 1, after)):
            edge = ref[t].astype(F32)
            place(row, t, edge[:group], edge[group:])

    w = weight[...].astype(F32)
    row_sets = (((0,), (1, 2)), ((0, 1), (2,)))
    for a in range(2):
        for b in range(2):
            for i, rows in enumerate(row_sets[a]):
                for j, cols in enumerate(row_sets[b]):
                    tap = sum(w[r, c] for r in rows for c in cols)
                    at = (2 * i + j) * channels
                    taps[2 * a + b, at : at + channels, :] = tap.astype(BF16)

    views = ((left, middle), (middle, right))
    total = tiles * group
    for a in range(2):
        for b in range(2):
            lhs = jnp.concatenate(
                [v[a + i : a + i + grid_rows].reshape(grid_rows * total, channels)
                 for i in range(2) for v in views[b]], axis=1
            )
            mapped = matmul(lhs, taps[2 * a + b]) + bias[...]
            value = 0.5 * mapped * (1.0 + jnp.tanh(0.5 * mapped))
            for n in range(wide.shape[0]):
                wide[n, pl.ds(b, grid_rows * total, stride=2), :] = value[:, n * 128 : (n + 1) * 128]
        for n in range(wide.shape[0]):
            shaped = wide[n].reshape(grid_rows, tiles * frames, 2 * own, 128)
            for r in range(grid_rows):
                out[:, 2 * r + a, :, n * 128 : (n + 1) * 128] = shaped[r].astype(BF16)


def body(video, w_query, w_key, w_value, w_out, w_latent, conv_weight, conv_bias):
    frames, grid_rows, columns, d = video.shape
    tiles = lax.axis_size("tm")
    own = columns // tiles
    flat = video.reshape(-1, d)
    core_id = lax.axis_index("space")
    core = core_id.astype(jnp.int32).reshape(1)
    here = lax.axis_index("tm")

    parts, mine, theirs = states_call(core, flat, w_key, w_value, frames)
    swap = [(0, 1), (1, 0)]
    total = mine + lax.ppermute(theirs, "space", swap).astype(F32)
    other_parts = lax.ppermute(parts, "space", swap)

    queries = [query_call(flat, w_query, 0, d)]
    carry = jnp.zeros_like(total)
    step = 1
    while step < tiles:
        sent = total.astype(BF16)
        if 2 * step < tiles:
            pairs = [(i, i ^ step) for i in range(tiles)]
            got = lax.ppermute(sent, "tm", pairs).astype(F32)
            carry = carry + jnp.where((here & step) != 0, got, 0.0)
            total = total + got
        else:
            pairs = [(i, i + step) for i in range(step)]
            carry = carry + lax.ppermute(sent, "tm", pairs).astype(F32)
        step *= 2
    carry = carry.astype(BF16)
    other_carry = lax.ppermute(carry, "space", swap)

    blocks = latent_call(
        core, flat, queries, parts, other_parts, carry, other_carry, w_out, w_latent,
        frames, columns, tiles,
    )
    blocks = lax.all_to_all(blocks, "tm", 0, 0, tiled=True)

    return decode(blocks, conv_weight, conv_bias, frames, grid_rows, own, tiles)


def decode(blocks, conv_weight, conv_bias, frames, grid_rows, own, tiles):
    channels = conv_weight.shape[2]
    width = conv_weight.shape[3]
    group = frames * own
    main = grid_rows * group
    sides = blocks[:, main:].reshape(tiles, 2 * frames, grid_rows, channels)

    def edge(r):
        return jnp.concatenate([blocks[:, r * group : (r + 1) * group], sides[:, :, r]], axis=1)

    before = lax.ppermute(edge(grid_rows - 1), "space", [(0, 1)])
    after = lax.ppermute(edge(0), "space", [(1, 0)])
    total = tiles * group
    return pl.pallas_call(
        functools.partial(decode_kernel, frames, tiles, grid_rows, own),
        out_shape=shape((tiles * frames, 2 * grid_rows, 2 * own, width), BF16),
        in_specs=[IN_VMEM] * 5,
        out_specs=IN_VMEM,
        scratch_shapes=[pltpu.VMEM((grid_rows + 2, total, channels), BF16)] * 3
        + [
            pltpu.VMEM((4, 4 * channels, width), BF16),
            pltpu.VMEM((width // 128, 2 * grid_rows * total, 128), F32),
        ],
        name="decode",
        compiler_params=params(36),
    )(blocks, before, after, conv_weight, conv_bias.reshape(1, width))


def solution(mesh):
    placed = (P(("groups", "tm"), "space", None, None), P(), P(), P(), P(), P(), P(), P())
    return jax.shard_map(
        body,
        mesh=mesh,
        in_specs=placed,
        out_specs=P("groups", "space", "tm", None),
        check_vma=False,
    )
```

```python
import functools

import jax
import jax.numpy as jnp
from jax import lax
from jax.experimental import pallas as pl
from jax.experimental.pallas import tpu as pltpu
from jax.sharding import PartitionSpec as P


HEAD = 128
EPS = 1e-06
BF16 = jnp.bfloat16
F32 = jnp.float32


IN_HBM = pl.BlockSpec(memory_space=pltpu.HBM)
IN_VMEM = pl.BlockSpec(memory_space=pltpu.VMEM)
IN_SMEM = pl.BlockSpec(memory_space=pltpu.SMEM)


def shape(dims, dtype):
    return jax.ShapeDtypeStruct(dims, dtype)


def params(megabytes):
    return pltpu.CompilerParams(vmem_limit_bytes=megabytes << 20)


def in_hbm(x):
    return pltpu.with_memory_space_constraint(x, pltpu.HBM)


def matmul(a, b):
    return jnp.dot(a, b, preferred_element_type=F32)


def features(x):
    return jnp.where(x > 0.0, x + 1.0, jnp.exp(jnp.minimum(x, 0.0)))


def states_kernel(
    frames, first, load, core, video_in, wk_hbm, wv_hbm,
    parts_out, mine_out, theirs_out, *refs,
):
    if load:
        video, wk, wv, key, value, wk_sem, wv_sem, video_sem = refs
    else:
        wk, wv, key, value, wk_sem, wv_sem = refs
        video = video_in
    per = video.shape[0] // frames
    heads = wk.shape[1] // HEAD
    half = HEAD // 2

    def weight_copies(h):
        source = pl.ds(pl.multiple_of((first + h) * HEAD, HEAD), HEAD)
        cols = pl.ds(pl.multiple_of(h * HEAD, HEAD), HEAD)
        return (
            pltpu.make_async_copy(wk_hbm.at[:, source], wk.at[:, cols], wk_sem.at[h]),
            pltpu.make_async_copy(wv_hbm.at[:, source], wv.at[:, cols], wv_sem.at[h]),
        )

    def video_copy(f):
        rows = pl.ds(f * per, per)
        return pltpu.make_async_copy(video_in.at[rows], video.at[rows], video_sem.at[f])

    for c in weight_copies(0):
        c.start()
    if load:
        for f in range(frames):
            video_copy(f).start()
    for h in range(1, heads):
        for c in weight_copies(h):
            c.start()
    if load:
        for f in range(frames):
            video_copy(f).wait()

    def project(h, carry):
        for c in weight_copies(h):
            c.wait()
        cols = pl.ds(pl.multiple_of(h * HEAD, HEAD), HEAD)
        both = jnp.concatenate([wk[:, cols], wv[:, cols]], axis=1)
        for f in range(frames):
            rows = slice(f * per, (f + 1) * per)
            kv = matmul(video[rows, :], both)
            key[h, rows, :] = features(kv[:, :HEAD]).astype(BF16)
            value[h, rows, :] = kv[:, HEAD:].astype(BF16)
        return carry

    lax.fori_loop(0, heads, project, 0)
    low = core[0] == 0
    for h in range(heads):
        total = None
        for f in range(frames):
            rows = slice(f * per, (f + 1) * per)
            state = lax.dot_general(
                key[h, rows, :], value[h, rows, :], (((0,), (0,)), ((), ())),
                preferred_element_type=F32,
            )
            parts_out[f, h] = state.astype(BF16)
            total = state if total is None else total + state
        mine_out[h] = jnp.where(low, total[:half], total[half:])
        theirs_out[h] = jnp.where(low, total[half:], total[:half]).astype(BF16)


def states_call(core, video, wk, wv, frames, first, heads, load):
    tokens, d = video.shape
    width = heads * HEAD
    half = (heads, HEAD // 2, HEAD)
    out_shape = [
        shape((frames, heads, HEAD, HEAD), BF16),
        shape(half, F32),
        shape(half, BF16),
    ]
    scratch = [
        pltpu.VMEM((d, width), BF16),
        pltpu.VMEM((d, width), BF16),
        pltpu.VMEM((heads, tokens, HEAD), BF16),
        pltpu.VMEM((heads, tokens, HEAD), BF16),
        pltpu.SemaphoreType.DMA((heads,)),
        pltpu.SemaphoreType.DMA((heads,)),
    ]
    if load:
        out_shape.append(shape((tokens, d), BF16))
        scratch.append(pltpu.SemaphoreType.DMA((frames,)))
        video = in_hbm(video)
    return pl.pallas_call(
        functools.partial(states_kernel, frames, first, load),
        out_shape=out_shape,
        in_specs=[IN_SMEM, IN_HBM if load else IN_VMEM, IN_HBM, IN_HBM],
        out_specs=[IN_VMEM] * len(out_shape),
        scratch_shapes=scratch,
        name="states",
        compiler_params=params(20),
    )(core, video, in_hbm(wk), in_hbm(wv))


def query_call(video, w, first, width):
    def kernel(video, w, out):
        out[...] = features(matmul(video[...], w[:, first : first + width])).astype(BF16)

    return pl.pallas_call(
        kernel,
        out_shape=shape((video.shape[0], width), BF16),
        in_specs=[IN_VMEM] * 2,
        out_specs=IN_VMEM,
        name="query",
        compiler_params=params(16),
    )(video, w)


def attend(frames, core, query, parts, other_parts, carry, other_carry, used, head_out):
    heads = carry.shape[0]
    per = query.shape[0] // frames
    low = core[0] == 0
    used[...] = jnp.zeros_like(used)
    for h in range(heads):
        mine, theirs = carry[h].astype(F32), other_carry[h].astype(F32)
        running = jnp.concatenate(
            [jnp.where(low, mine, theirs), jnp.where(low, theirs, mine)], axis=0
        )
        at = (h % 2) * HEAD
        for f in range(frames):
            running = running + parts[f, h].astype(F32) + other_parts[f, h].astype(F32)
            used[f, h // 2, at : at + HEAD, at : at + HEAD] = running.astype(BF16)
    for f in range(frames):
        rows = slice(f * per, (f + 1) * per)
        for p in range(pl.cdiv(heads, 2)):
            width = min(2, heads - 2 * p) * HEAD
            first = 2 * p * HEAD
            attended = matmul(
                query[rows, first : first + width], used[f, p, :width, :width]
            )
            for h in range(width // HEAD):
                one = attended[:, h * HEAD : (h + 1) * HEAD]
                scale = lax.rsqrt(jnp.mean(one * one, axis=1, keepdims=True) + EPS)
                at = first + h * HEAD
                head_out[rows, at : at + HEAD] = (one * scale).astype(BF16)


def used_shape(frames, heads):
    return pltpu.VMEM((frames, pl.cdiv(heads, 2), 2 * HEAD, 2 * HEAD), BF16)


def partial_call(core, video, chunk, w_out, frames):
    tokens, d = video.shape
    heads = chunk[3].shape[0]

    def kernel(core, video, query, parts, other_parts, carry, other_carry, w_out, out,
               used, head_out):
        attend(frames, core, query, parts, other_parts, carry, other_carry, used, head_out)
        per = tokens // frames
        for f in range(frames):
            rows = slice(f * per, (f + 1) * per)
            out[rows, :] = video[rows, :].astype(F32) + matmul(
                head_out[rows, :], w_out[: heads * HEAD, :]
            )

    return pl.pallas_call(
        kernel,
        out_shape=shape((tokens, d), F32),
        in_specs=[IN_SMEM] + [IN_VMEM] * 7,
        out_specs=IN_VMEM,
        scratch_shapes=[used_shape(frames, heads), pltpu.VMEM((tokens, heads * HEAD), BF16)],
        name="partial",
        compiler_params=params(20),
    )(core, video, *chunk, w_out)


def latent_kernel(
    frames, columns, tiles, core, partial, query, parts, other_parts, carry, other_carry,
    w_out, w_latent, out, used, head_out, latent,
):
    tokens, d = partial.shape
    per = tokens // frames
    width = head_out.shape[1]
    attend(frames, core, query, parts, other_parts, carry, other_carry, used, head_out)
    for f in range(frames):
        rows = slice(f * per, (f + 1) * per)
        summed = partial[rows, :] + matmul(head_out[rows, :], w_out[d - width :, :])
        scale = lax.rsqrt(jnp.mean(summed * summed, axis=1, keepdims=True) + EPS)
        latent[rows, :] = matmul((summed * scale).astype(BF16), w_latent[...])

    own = columns // tiles
    grid_rows = per // columns
    main = grid_rows * frames * own
    for t in range(tiles):
        for r in range(grid_rows):
            block = [
                latent[pl.ds(f * per + r * columns + t * own, own), :] for f in range(frames)
            ]
            at = r * frames * own
            out[t, at : at + frames * own, :] = jnp.concatenate(block, axis=0).astype(BF16)
        sides = []
        for column in (t * own - 1, (t + 1) * own):
            for f in range(frames):
                if 0 <= column < columns:
                    at = f * per + column
                    sides.append(latent[pl.ds(at, grid_rows, stride=columns), :])
                else:
                    sides.append(jnp.zeros((grid_rows, out.shape[2]), F32))
        out[t, main:, :] = jnp.concatenate(sides, axis=0).astype(BF16)


def latent_call(core, partial, chunk, w_out, w_latent, frames, columns, tiles):
    tokens, _ = partial.shape
    channels = w_latent.shape[1]
    heads = chunk[3].shape[0]
    rows = tokens // columns * (columns // tiles + 2)
    return pl.pallas_call(
        functools.partial(latent_kernel, frames, columns, tiles),
        out_shape=shape((tiles, rows, channels), BF16),
        in_specs=[IN_SMEM] + [IN_VMEM] * 8,
        out_specs=IN_VMEM,
        scratch_shapes=[
            used_shape(frames, heads),
            pltpu.VMEM((tokens, heads * HEAD), BF16),
            pltpu.VMEM((tokens, channels), F32),
        ],
        name="latent",
        compiler_params=params(20),
    )(core, partial, *chunk, w_out, w_latent)


def decode_kernel(
    frames, tiles, grid_rows, own, core, blocks, edge, weight, bias,
    out, left, middle, right, taps, wide,
):
    group = frames * own
    main = grid_rows * group
    column = lax.broadcasted_iota(jnp.int32, (group, 1), 0) % own
    channels = weight.shape[2]

    def place(row, t, body, sides):
        at = slice(t * group, (t + 1) * group)
        first = jnp.concatenate(
            [jnp.broadcast_to(sides[f : f + 1], (own, channels)) for f in range(frames)], axis=0
        )
        last = jnp.concatenate(
            [jnp.broadcast_to(sides[frames + f : frames + f + 1], (own, channels))
             for f in range(frames)], axis=0
        )
        down = pltpu.roll(body, 1, 0)
        up = pltpu.roll(body, group - 1, 0)
        left[row, at, :] = jnp.where(column == 0, first, down).astype(BF16)
        middle[row, at, :] = body.astype(BF16)
        right[row, at, :] = jnp.where(column == own - 1, last, up).astype(BF16)

    for t in range(tiles):
        everything = blocks[t].astype(F32)
        for r in range(grid_rows):
            body = everything[r * group : (r + 1) * group]
            sides = [
                everything[main + s * grid_rows + r : main + s * grid_rows + r + 1]
                for s in range(2 * frames)
            ]
            place(r + 1, t, body, jnp.concatenate(sides, axis=0))
        beside = edge[t].astype(F32)
        for row, present in ((0, core[0] == 1), (grid_rows + 1, core[0] == 0)):
            there = jnp.where(present, beside, 0.0)
            place(row, t, there[:group], there[group:])

    w = weight[...].astype(F32)
    row_sets = (((0,), (1, 2)), ((0, 1), (2,)))
    for a in range(2):
        for b in range(2):
            for i, rows in enumerate(row_sets[a]):
                for j, cols in enumerate(row_sets[b]):
                    tap = sum(w[r, c] for r in rows for c in cols)
                    at = (2 * i + j) * channels
                    taps[2 * a + b, at : at + channels, :] = tap.astype(BF16)

    views = ((left, middle), (middle, right))
    total = tiles * group
    for a in range(2):
        for b in range(2):
            lhs = jnp.concatenate(
                [v[a + i : a + i + grid_rows].reshape(grid_rows * total, channels)
                 for i in range(2) for v in views[b]], axis=1
            )
            mapped = matmul(lhs, taps[2 * a + b]) + bias[...]
            value = 0.5 * mapped * (1.0 + jnp.tanh(0.5 * mapped))
            for n in range(wide.shape[0]):
                wide[n, pl.ds(b, grid_rows * total, stride=2), :] = value[:, n * 128 : (n + 1) * 128]
        for n in range(wide.shape[0]):
            shaped = wide[n].reshape(grid_rows, tiles * frames, 2 * own, 128)
            for r in range(grid_rows):
                out[:, 2 * r + a, :, n * 128 : (n + 1) * 128] = shaped[r].astype(BF16)


def prefix_rounds(total, tiles, here):
    carry = jnp.zeros_like(total)
    step, number = 1, 0
    while step < tiles:
        sent = total.astype(BF16)
        if 2 * step < tiles:
            pairs = [(i, i ^ step) for i in range(tiles)]
            got = lax.ppermute(sent, "tm", pairs).astype(F32)
            carry = carry + jnp.where((here & step) != 0, got, 0.0)
            total = total + got
        else:
            pairs = [(i, i + step) for i in range(step)]
            carry = carry + lax.ppermute(sent, "tm", pairs).astype(F32)
        step *= 2
        number += 1
    return carry.astype(BF16)


SWAP = [(0, 1), (1, 0)]


def body(video, w_query, w_key, w_value, w_out, w_latent, conv_weight, conv_bias):
    frames, grid_rows, columns, d = video.shape
    tiles = lax.axis_size("tm")
    own = columns // tiles
    flat = video.reshape(-1, d)
    core = lax.axis_index("space").astype(jnp.int32).reshape(1)
    here = lax.axis_index("tm")
    heads = d // HEAD
    split = heads // 3 * 2
    chunks = (("a", 0, split), ("b", split, heads - split))

    loaded = flat
    sent = {}
    for name, first, count in chunks:
        made = states_call(
            core, loaded, w_key, w_value, frames, first, count, name == "a"
        )
        parts, mine, theirs = made[:3]
        if name == "a":
            loaded = made[3]
        total = mine + lax.ppermute(theirs, "space", SWAP).astype(F32)
        other_parts = lax.ppermute(parts, "space", SWAP)
        sent[name] = (parts, other_parts, total)

    ready = {}
    for name, first, count in chunks:
        parts, other_parts, total = sent[name]
        query = query_call(loaded, w_query, first * HEAD, count * HEAD)
        carry = prefix_rounds(total, tiles, here)
        other_carry = lax.ppermute(carry, "space", SWAP)
        ready[name] = (query, parts, other_parts, carry, other_carry)

    partial = partial_call(core, loaded, ready["a"], w_out, frames)
    blocks = latent_call(
        core, partial, ready["b"], w_out, w_latent, frames, columns, tiles
    )
    blocks = lax.all_to_all(blocks, "tm", 0, 0, tiled=True)
    return decode(core, blocks, conv_weight, conv_bias, frames, grid_rows, own, tiles)


def decode(core, blocks, conv_weight, conv_bias, frames, grid_rows, own, tiles):
    channels = conv_weight.shape[2]
    width = conv_weight.shape[3]
    group = frames * own
    main = grid_rows * group
    sides = blocks[:, main:].reshape(tiles, 2 * frames, grid_rows, channels)

    def edge(r):
        return jnp.concatenate([blocks[:, r * group : (r + 1) * group], sides[:, :, r]], axis=1)

    mine = jnp.where(core[0] == 0, edge(grid_rows - 1), edge(0))
    beside = lax.ppermute(mine, "space", SWAP)
    total = tiles * group
    return pl.pallas_call(
        functools.partial(decode_kernel, frames, tiles, grid_rows, own),
        out_shape=shape((tiles * frames, 2 * grid_rows, 2 * own, width), BF16),
        in_specs=[IN_SMEM] + [IN_VMEM] * 4,
        out_specs=IN_VMEM,
        scratch_shapes=[pltpu.VMEM((grid_rows + 2, total, channels), BF16)] * 3
        + [
            pltpu.VMEM((4, 4 * channels, width), BF16),
            pltpu.VMEM((width // 128, 2 * grid_rows * total, 128), F32),
        ],
        name="decode",
        compiler_params=params(36),
    )(core, blocks, beside, conv_weight, conv_bias.reshape(1, width))


def solution(mesh):
    assert mesh.shape["space"] == 2
    tiles = mesh.shape["tm"]
    assert tiles & (tiles - 1) == 0
    placed = (P(("groups", "tm"), "space", None, None), P(), P(), P(), P(), P(), P(), P())
    return jax.shard_map(
        body,
        mesh=mesh,
        in_specs=placed,
        out_specs=P("groups", "space", "tm", None),
        check_vma=False,
    )
```

```python
import functools

import jax
import jax.numpy as jnp
from jax import lax
from jax.experimental import pallas as pl
from jax.experimental.pallas import tpu as pltpu
from jax.sharding import PartitionSpec as P


HEAD = 128
EPS = 1e-06
BF16 = jnp.bfloat16
F32 = jnp.float32


IN_HBM = pl.BlockSpec(memory_space=pltpu.HBM)
IN_VMEM = pl.BlockSpec(memory_space=pltpu.VMEM)
IN_SMEM = pl.BlockSpec(memory_space=pltpu.SMEM)


def shape(dims, dtype):
    return jax.ShapeDtypeStruct(dims, dtype)


def params(megabytes):
    return pltpu.CompilerParams(vmem_limit_bytes=megabytes << 20)


def in_hbm(x):
    return pltpu.with_memory_space_constraint(x, pltpu.HBM)


def in_vmem(x):
    return pltpu.with_memory_space_constraint(x, pltpu.VMEM)


def matmul(a, b):
    return jnp.dot(a, b, preferred_element_type=F32)


def features(x):
    return jnp.where(x > 0.0, x + 1.0, jnp.exp(jnp.minimum(x, 0.0)))


def states_kernel(frames, first, heads, later, fetched, place, video_in, wk_hbm, wv_hbm, *refs):
    refs = list(refs)
    wq_hbm = refs.pop(0) if fetched else None
    parts_out = refs.pop(0)
    if fetched:
        wq_out, key, value, wq_sem = refs
        video, wk, wv = video_in, wk_hbm, wv_hbm
    else:
        video, wk_out, wv_out, wk, wv, key, value, wk_sem, wv_sem, video_sem, late_sem = refs
    per = video.shape[0] // frames
    blocks = 2 * frames
    rows_of = video.shape[0] // blocks

    def weight_copies(h):
        source = pl.ds(pl.multiple_of((first + h) * HEAD, HEAD), HEAD)
        cols = pl.ds(pl.multiple_of(h * HEAD, HEAD), HEAD)
        return (
            pltpu.make_async_copy(wk_hbm.at[:, source], wk.at[:, cols], wk_sem.at[h]),
            pltpu.make_async_copy(wv_hbm.at[:, source], wv.at[:, cols], wv_sem.at[h]),
        )

    def video_copy(i):
        rows = pl.ds(i * rows_of, rows_of)
        return pltpu.make_async_copy(video_in.at[rows], video.at[rows], video_sem.at[i])

    def project(h, rows, both):
        kv = matmul(video[rows, :], both)
        key[h, rows, :] = features(kv[:, :HEAD]).astype(BF16)
        value[h, rows, :] = kv[:, HEAD:].astype(BF16)

    def weights(h):
        cols = pl.ds(pl.multiple_of(h * HEAD, HEAD), HEAD)
        return jnp.concatenate([wk[:, cols], wv[:, cols]], axis=1)

    def one_head(h, carry):
        if not fetched:
            for c in weight_copies(h):
                c.wait()
        both = weights(h)
        for f in range(frames):
            project(h, slice(f * per, (f + 1) * per), both)
        return carry

    if fetched:
        late = [pltpu.make_async_copy(wq_hbm, wq_out, wq_sem)]
        late[0].start()
        lax.fori_loop(0, heads, one_head, 0)
    else:
        for c in weight_copies(0):
            c.start()
        for i in range(blocks):
            video_copy(i).start()
        for c in weight_copies(0):
            c.wait()
        both = weights(0)
        for i in range(blocks):
            video_copy(i).wait()
            if i == 0:
                for h in range(1, heads):
                    for c in weight_copies(h):
                        c.start()
            project(0, slice(i * rows_of, (i + 1) * rows_of), both)
        source = pl.ds((first + heads) * HEAD, later * HEAD)
        late = [
            pltpu.make_async_copy(wk_hbm.at[:, source], wk_out, late_sem.at[0]),
            pltpu.make_async_copy(wv_hbm.at[:, source], wv_out, late_sem.at[1]),
        ]
        for c in late:
            c.start()
        lax.fori_loop(1, heads, one_head, 0)

    for h in range(heads):
        for f in range(frames):
            rows = slice(f * per, (f + 1) * per)
            state = lax.dot_general(
                key[h, rows, :], value[h, rows, :], (((0,), (0,)), ((), ())),
                preferred_element_type=F32,
            )
            parts_out[f, h] = state.astype(BF16)
    for c in late:
        c.wait()


def first_states(place, video, wk, wv, frames, heads, later):
    tokens, d = video.shape
    width = heads * HEAD
    return pl.pallas_call(
        functools.partial(states_kernel, frames, 0, heads, later, False),
        out_shape=[
            shape((frames, heads, HEAD, HEAD), BF16),
            shape((tokens, d), BF16),
            shape((d, later * HEAD), BF16),
            shape((d, later * HEAD), BF16),
        ],
        in_specs=[IN_SMEM] + [IN_HBM] * 3,
        out_specs=[IN_VMEM] * 4,
        scratch_shapes=[
            pltpu.VMEM((d, width), BF16),
            pltpu.VMEM((d, width), BF16),
            pltpu.VMEM((heads, tokens, HEAD), BF16),
            pltpu.VMEM((heads, tokens, HEAD), BF16),
            pltpu.SemaphoreType.DMA((heads,)),
            pltpu.SemaphoreType.DMA((heads,)),
            pltpu.SemaphoreType.DMA((2 * frames,)),
            pltpu.SemaphoreType.DMA((2,)),
        ],
        name="states",
        compiler_params=params(20),
    )(place, in_hbm(video), in_hbm(wk), in_hbm(wv))


def second_states(place, video, wk, wv, wq, frames):
    tokens, _ = video.shape
    heads = wk.shape[1] // HEAD
    return pl.pallas_call(
        functools.partial(states_kernel, frames, 0, heads, 0, True),
        out_shape=[
            shape((frames, heads, HEAD, HEAD), BF16),
            shape(wq.shape, BF16),
        ],
        in_specs=[IN_SMEM] + [IN_VMEM] * 3 + [IN_HBM],
        out_specs=[IN_VMEM] * 2,
        scratch_shapes=[
            pltpu.VMEM((heads, tokens, HEAD), BF16),
            pltpu.VMEM((heads, tokens, HEAD), BF16),
            pltpu.SemaphoreType.DMA,
        ],
        name="states",
        compiler_params=params(20),
    )(place, video, wk, wv, in_hbm(wq))


def total_call(place, parts, other_parts):
    frames, heads = parts.shape[:2]
    half = HEAD // 2

    def kernel(place, parts, other_parts, out, sent):
        low = place[0] == 0
        for h in range(heads):
            total = None
            for f in range(frames):
                one = parts[f, h].astype(F32) + other_parts[f, h].astype(F32)
                total = one if total is None else total + one
            total = jnp.where(low, total[:half], total[half:])
            out[h] = total
            sent[h] = total.astype(BF16)

    dims = (heads, half, HEAD)
    return pl.pallas_call(
        kernel,
        out_shape=[shape(dims, F32), shape(dims, BF16)],
        in_specs=[IN_SMEM] + [IN_VMEM] * 2,
        out_specs=[IN_VMEM] * 2,
        name="total",
        compiler_params=params(4),
    )(place, in_vmem(parts), in_vmem(other_parts))


def query_call(video, w, first, width):
    def kernel(video, w, out):
        out[...] = features(matmul(video[...], w[:, first : first + width])).astype(BF16)

    return pl.pallas_call(
        kernel,
        out_shape=shape((video.shape[0], width), BF16),
        in_specs=[IN_VMEM] * 2,
        out_specs=IN_VMEM,
        name="query",
        compiler_params=params(16),
    )(video, w)


def attend(frames, place, query, parts, other_parts, carry, other_carry, used, head_out):
    heads = carry.shape[0]
    per = query.shape[0] // frames
    low = place[0] == 0
    used[...] = jnp.zeros_like(used)
    for h in range(heads):
        mine, theirs = carry[h].astype(F32), other_carry[h].astype(F32)
        running = jnp.concatenate(
            [jnp.where(low, mine, theirs), jnp.where(low, theirs, mine)], axis=0
        )
        at = (h % 2) * HEAD
        for f in range(frames):
            running = running + parts[f, h].astype(F32) + other_parts[f, h].astype(F32)
            used[f, h // 2, at : at + HEAD, at : at + HEAD] = running.astype(BF16)
    for f in range(frames):
        rows = slice(f * per, (f + 1) * per)
        for p in range(pl.cdiv(heads, 2)):
            width = min(2, heads - 2 * p) * HEAD
            first = 2 * p * HEAD
            attended = matmul(
                query[rows, first : first + width], used[f, p, :width, :width]
            )
            for h in range(width // HEAD):
                one = attended[:, h * HEAD : (h + 1) * HEAD]
                scale = lax.rsqrt(jnp.mean(one * one, axis=1, keepdims=True) + EPS)
                at = first + h * HEAD
                head_out[rows, at : at + HEAD] = (one * scale).astype(BF16)


def used_shape(frames, heads):
    return pltpu.VMEM((frames, pl.cdiv(heads, 2), 2 * HEAD, 2 * HEAD), BF16)


def partial_call(place, video, chunk, w_out, frames):
    tokens, d = video.shape
    heads = chunk[3].shape[0]

    def kernel(place, video, query, parts, other_parts, carry, other_carry, w_out, out,
               used, head_out):
        attend(frames, place, query, parts, other_parts, carry, other_carry, used, head_out)
        per = tokens // frames
        for f in range(frames):
            rows = slice(f * per, (f + 1) * per)
            out[rows, :] = video[rows, :].astype(F32) + matmul(
                head_out[rows, :], w_out[: heads * HEAD, :]
            )

    return pl.pallas_call(
        kernel,
        out_shape=shape((tokens, d), F32),
        in_specs=[IN_SMEM] + [IN_VMEM] * 7,
        out_specs=IN_VMEM,
        scratch_shapes=[used_shape(frames, heads), pltpu.VMEM((tokens, heads * HEAD), BF16)],
        name="partial",
        compiler_params=params(20),
    )(place, video, *chunk, w_out)


def latent_kernel(
    frames, columns, tiles, place, partial, query, parts, other_parts, carry, other_carry,
    w_out, w_latent, out, used, head_out, latent,
):
    tokens, d = partial.shape
    per = tokens // frames
    width = head_out.shape[1]
    attend(frames, place, query, parts, other_parts, carry, other_carry, used, head_out)
    for f in range(frames):
        rows = slice(f * per, (f + 1) * per)
        summed = partial[rows, :] + matmul(head_out[rows, :], w_out[d - width :, :])
        scale = lax.rsqrt(jnp.mean(summed * summed, axis=1, keepdims=True) + EPS)
        latent[rows, :] = matmul((summed * scale).astype(BF16), w_latent[...])

    own = columns // tiles
    grid_rows = per // columns
    main = grid_rows * frames * own
    for t in range(tiles):
        for r in range(grid_rows):
            block = [
                latent[pl.ds(f * per + r * columns + t * own, own), :] for f in range(frames)
            ]
            at = r * frames * own
            out[t, at : at + frames * own, :] = jnp.concatenate(block, axis=0).astype(BF16)
        sides = []
        for column in (t * own - 1, (t + 1) * own):
            for f in range(frames):
                if 0 <= column < columns:
                    at = f * per + column
                    sides.append(latent[pl.ds(at, grid_rows, stride=columns), :])
                else:
                    sides.append(jnp.zeros((grid_rows, out.shape[2]), F32))
        out[t, main:, :] = jnp.concatenate(sides, axis=0).astype(BF16)


def latent_call(place, partial, chunk, w_out, w_latent, frames, columns, tiles):
    tokens, _ = partial.shape
    channels = w_latent.shape[1]
    heads = chunk[3].shape[0]
    rows = tokens // columns * (columns // tiles + 2)
    return pl.pallas_call(
        functools.partial(latent_kernel, frames, columns, tiles),
        out_shape=shape((tiles, rows, channels), BF16),
        in_specs=[IN_SMEM] + [IN_VMEM] * 8,
        out_specs=IN_VMEM,
        scratch_shapes=[
            used_shape(frames, heads),
            pltpu.VMEM((tokens, heads * HEAD), BF16),
            pltpu.VMEM((tokens, channels), F32),
        ],
        name="latent",
        compiler_params=params(20),
    )(place, partial, *chunk, w_out, w_latent)


def decode_kernel(
    frames, tiles, grid_rows, own, place, blocks, edge, weight, bias,
    out, left, middle, right, taps, wide,
):
    group = frames * own
    main = grid_rows * group
    column = lax.broadcasted_iota(jnp.int32, (group, 1), 0) % own
    channels = weight.shape[2]

    def lay(row, t, body, sides):
        at = slice(t * group, (t + 1) * group)
        first = jnp.concatenate(
            [jnp.broadcast_to(sides[f : f + 1], (own, channels)) for f in range(frames)], axis=0
        )
        last = jnp.concatenate(
            [jnp.broadcast_to(sides[frames + f : frames + f + 1], (own, channels))
             for f in range(frames)], axis=0
        )
        down = pltpu.roll(body, 1, 0)
        up = pltpu.roll(body, group - 1, 0)
        left[row, at, :] = jnp.where(column == 0, first, down).astype(BF16)
        middle[row, at, :] = body.astype(BF16)
        right[row, at, :] = jnp.where(column == own - 1, last, up).astype(BF16)

    for t in range(tiles):
        everything = blocks[t].astype(F32)
        for r in range(grid_rows):
            body = everything[r * group : (r + 1) * group]
            sides = [
                everything[main + s * grid_rows + r : main + s * grid_rows + r + 1]
                for s in range(2 * frames)
            ]
            lay(r + 1, t, body, jnp.concatenate(sides, axis=0))
        beside = edge[t].astype(F32)
        for row, present in ((0, place[0] == 1), (grid_rows + 1, place[0] == 0)):
            there = jnp.where(present, beside, 0.0)
            lay(row, t, there[:group], there[group:])

    w = weight[...].astype(F32)
    row_sets = (((0,), (1, 2)), ((0, 1), (2,)))
    for a in range(2):
        for b in range(2):
            for i, rows in enumerate(row_sets[a]):
                for j, cols in enumerate(row_sets[b]):
                    tap = sum(w[r, c] for r in rows for c in cols)
                    at = (2 * i + j) * channels
                    taps[2 * a + b, at : at + channels, :] = tap.astype(BF16)

    views = ((left, middle), (middle, right))
    total = tiles * group
    for a in range(2):
        for b in range(2):
            lhs = jnp.concatenate(
                [v[a + i : a + i + grid_rows].reshape(grid_rows * total, channels)
                 for i in range(2) for v in views[b]], axis=1
            )
            mapped = matmul(lhs, taps[2 * a + b]) + bias[...]
            value = 0.5 * mapped * (1.0 + jnp.tanh(0.5 * mapped))
            for n in range(wide.shape[0]):
                wide[n, pl.ds(b, grid_rows * total, stride=2), :] = value[:, n * 128 : (n + 1) * 128]
        for n in range(wide.shape[0]):
            shaped = wide[n].reshape(grid_rows, tiles * frames, 2 * own, 128)
            for r in range(grid_rows):
                out[:, 2 * r + a, :, n * 128 : (n + 1) * 128] = shaped[r].astype(BF16)


def round_call(place, step, last, got, total, carry):
    def kernel(place, got, total, *refs):
        upper = (place[1] // step) % 2 == 1
        received = got[...].astype(F32)
        before = jnp.where(upper, received, 0.0)
        if carry is not None:
            before = refs[0][...] + before
            refs = refs[1:]
        if last:
            refs[0][...] = before.astype(BF16)
        else:
            carry_out, total_out, sent_out = refs
            carry_out[...] = before
            both = total[...] + received
            total_out[...] = both
            sent_out[...] = both.astype(BF16)

    near = [got, total] + ([] if carry is None else [carry])
    kinds = [BF16] if last else [F32, F32, BF16]
    return pl.pallas_call(
        kernel,
        out_shape=[shape(total.shape, kind) for kind in kinds],
        in_specs=[IN_SMEM] + [IN_VMEM] * len(near),
        out_specs=[IN_VMEM] * len(kinds),
        name="round",
        compiler_params=params(4),
    )(place, *near)


def prefix_rounds(place, total, sent, tiles):
    carry = None
    step, number = 1, 0
    while step < tiles:
        last = 2 * step >= tiles
        if last:
            pairs = [(i, i + step) for i in range(step)]
        else:
            pairs = [(i, i ^ step) for i in range(tiles)]
        got = lax.ppermute(sent, "tm", pairs)
        out = round_call(place, step, last, got, total, carry)
        if last:
            return out[0]
        carry, total, sent = out
        step *= 2
        number += 1
    return jnp.zeros_like(sent)


SWAP = [(0, 1), (1, 0)]


def body(video, w_query, w_key, w_value, w_out, w_latent, conv_weight, conv_bias):
    frames, grid_rows, columns, d = video.shape
    tiles = lax.axis_size("tm")
    own = columns // tiles
    flat = video.reshape(-1, d)
    place = jnp.stack([lax.axis_index("space"), lax.axis_index("tm")]).astype(jnp.int32)
    heads = d // HEAD
    split = heads // 3 * 2
    rest = heads - split
    parts_a, near, wk_b, wv_b = first_states(place, flat, w_key, w_value, frames, split, rest)
    other_a = lax.ppermute(parts_a, "space", SWAP)
    parts_b, near_query = second_states(place, near, wk_b, wv_b, w_query, frames)
    other_b = lax.ppermute(parts_b, "space", SWAP)

    ready = {}
    for name, first, parts, other in (("a", 0, parts_a, other_a), ("b", split, parts_b, other_b)):
        count = parts.shape[1]
        total, sent = total_call(place, parts, other)
        query = query_call(near, near_query, first * HEAD, count * HEAD)
        carry = prefix_rounds(place, total, sent, tiles)
        other_carry = lax.ppermute(carry, "space", SWAP)
        ready[name] = (query, parts, other, carry, other_carry)

    partial = partial_call(place, near, ready["a"], w_out, frames)
    blocks = latent_call(place, partial, ready["b"], w_out, w_latent, frames, columns, tiles)
    blocks = lax.all_to_all(blocks, "tm", 0, 0, tiled=True)
    return decode(place, blocks, conv_weight, conv_bias, frames, grid_rows, own, tiles)


def decode(place, blocks, conv_weight, conv_bias, frames, grid_rows, own, tiles):
    channels = conv_weight.shape[2]
    width = conv_weight.shape[3]
    group = frames * own
    main = grid_rows * group
    sides = blocks[:, main:].reshape(tiles, 2 * frames, grid_rows, channels)

    def edge(r):
        return jnp.concatenate([blocks[:, r * group : (r + 1) * group], sides[:, :, r]], axis=1)

    mine = jnp.where(place[0] == 0, edge(grid_rows - 1), edge(0))
    beside = lax.ppermute(mine, "space", SWAP)
    total = tiles * group
    return pl.pallas_call(
        functools.partial(decode_kernel, frames, tiles, grid_rows, own),
        out_shape=shape((tiles * frames, 2 * grid_rows, 2 * own, width), BF16),
        in_specs=[IN_SMEM] + [IN_VMEM] * 4,
        out_specs=IN_VMEM,
        scratch_shapes=[pltpu.VMEM((grid_rows + 2, total, channels), BF16)] * 3
        + [
            pltpu.VMEM((4, 4 * channels, width), BF16),
            pltpu.VMEM((width // 128, 2 * grid_rows * total, 128), F32),
        ],
        name="decode",
        compiler_params=params(36),
    )(place, blocks, beside, conv_weight, conv_bias.reshape(1, width))


def solution(mesh):
    assert mesh.shape["space"] == 2
    tiles = mesh.shape["tm"]
    assert tiles & (tiles - 1) == 0
    placed = (P(("groups", "tm"), "space", None, None), P(), P(), P(), P(), P(), P(), P())
    return jax.shard_map(
        body,
        mesh=mesh,
        in_specs=placed,
        out_specs=P("groups", "space", "tm", None),
        check_vma=False,
    )
```

```python
import functools

import jax
import jax.numpy as jnp
from jax import lax
from jax.experimental import pallas as pl
from jax.experimental.pallas import tpu as pltpu
from jax.sharding import PartitionSpec as P


HEAD = 128
EPS = 1e-06
BF16 = jnp.bfloat16
F32 = jnp.float32


IN_HBM = pl.BlockSpec(memory_space=pltpu.HBM)
IN_VMEM = pl.BlockSpec(memory_space=pltpu.VMEM)


def shape(dims, dtype):
    return jax.ShapeDtypeStruct(dims, dtype)


def params(megabytes):
    return pltpu.CompilerParams(vmem_limit_bytes=megabytes << 20)


def in_hbm(x):
    return pltpu.with_memory_space_constraint(x, pltpu.HBM)


def matmul(a, b):
    return jnp.dot(a, b, preferred_element_type=F32)


def features(x):
    return jnp.where(x > 0.0, x + 1.0, jnp.exp(jnp.minimum(x, 0.0)))


def states_kernel(frames, first, heads, later, fetched, video_in, wk_hbm, wv_hbm, *refs):
    refs = list(refs)
    wq_hbm = refs.pop(0) if fetched else None
    parts_out = refs.pop(0)
    if fetched:
        wq_out, key, value, wq_sem = refs
        video, wk, wv = video_in, wk_hbm, wv_hbm
    else:
        video, wk_out, wv_out, wk, wv, key, value, wk_sem, wv_sem, video_sem, late_sem = refs
    per = video.shape[0] // frames
    blocks = 2 * frames
    rows_of = video.shape[0] // blocks

    def weight_copies(h):
        source = pl.ds(pl.multiple_of((first + h) * HEAD, HEAD), HEAD)
        cols = pl.ds(pl.multiple_of(h * HEAD, HEAD), HEAD)
        return (
            pltpu.make_async_copy(wk_hbm.at[:, source], wk.at[:, cols], wk_sem.at[h]),
            pltpu.make_async_copy(wv_hbm.at[:, source], wv.at[:, cols], wv_sem.at[h]),
        )

    def video_copy(i):
        rows = pl.ds(i * rows_of, rows_of)
        return pltpu.make_async_copy(video_in.at[rows], video.at[rows], video_sem.at[i])

    def project(h, rows, both):
        kv = matmul(video[rows, :], both)
        key[h, rows, :] = features(kv[:, :HEAD]).astype(BF16)
        value[h, rows, :] = kv[:, HEAD:].astype(BF16)

    def weights(h):
        cols = pl.ds(pl.multiple_of(h * HEAD, HEAD), HEAD)
        return jnp.concatenate([wk[:, cols], wv[:, cols]], axis=1)

    def one_head(h, carry):
        if not fetched:
            for c in weight_copies(h):
                c.wait()
        both = weights(h)
        for f in range(frames):
            project(h, slice(f * per, (f + 1) * per), both)
        return carry

    if fetched:
        late = [pltpu.make_async_copy(wq_hbm, wq_out, wq_sem)]
        late[0].start()
        lax.fori_loop(0, heads, one_head, 0)
    else:
        for c in weight_copies(0):
            c.start()
        for i in range(blocks):
            video_copy(i).start()
        for c in weight_copies(0):
            c.wait()
        both = weights(0)
        for i in range(blocks):
            video_copy(i).wait()
            if i == 0:
                for h in range(1, heads):
                    for c in weight_copies(h):
                        c.start()
            project(0, slice(i * rows_of, (i + 1) * rows_of), both)
        source = pl.ds((first + heads) * HEAD, later * HEAD)
        late = [
            pltpu.make_async_copy(wk_hbm.at[:, source], wk_out, late_sem.at[0]),
            pltpu.make_async_copy(wv_hbm.at[:, source], wv_out, late_sem.at[1]),
        ]
        for c in late:
            c.start()
        lax.fori_loop(1, heads, one_head, 0)

    for h in range(heads):
        for f in range(frames):
            rows = slice(f * per, (f + 1) * per)
            state = lax.dot_general(
                key[h, rows, :], value[h, rows, :], (((0,), (0,)), ((), ())),
                preferred_element_type=F32,
            )
            parts_out[f, h] = state.astype(BF16)
    for c in late:
        c.wait()


def first_states(video, wk, wv, frames, heads, later):
    tokens, d = video.shape
    width = heads * HEAD
    return pl.pallas_call(
        functools.partial(states_kernel, frames, 0, heads, later, False),
        out_shape=[
            shape((frames, heads, HEAD, HEAD), BF16),
            shape((tokens, d), BF16),
            shape((d, later * HEAD), BF16),
            shape((d, later * HEAD), BF16),
        ],
        in_specs=[IN_HBM] * 3,
        out_specs=[IN_VMEM] * 4,
        scratch_shapes=[
            pltpu.VMEM((d, width), BF16),
            pltpu.VMEM((d, width), BF16),
            pltpu.VMEM((heads, tokens, HEAD), BF16),
            pltpu.VMEM((heads, tokens, HEAD), BF16),
            pltpu.SemaphoreType.DMA((heads,)),
            pltpu.SemaphoreType.DMA((heads,)),
            pltpu.SemaphoreType.DMA((2 * frames,)),
            pltpu.SemaphoreType.DMA((2,)),
        ],
        name="states",
        compiler_params=params(20),
    )(in_hbm(video), in_hbm(wk), in_hbm(wv))


def second_states(video, wk, wv, wq, frames):
    tokens, _ = video.shape
    heads = wk.shape[1] // HEAD
    return pl.pallas_call(
        functools.partial(states_kernel, frames, 0, heads, 0, True),
        out_shape=[
            shape((frames, heads, HEAD, HEAD), BF16),
            shape(wq.shape, BF16),
        ],
        in_specs=[IN_VMEM] * 3 + [IN_HBM],
        out_specs=[IN_VMEM] * 2,
        scratch_shapes=[
            pltpu.VMEM((heads, tokens, HEAD), BF16),
            pltpu.VMEM((heads, tokens, HEAD), BF16),
            pltpu.SemaphoreType.DMA,
        ],
        name="states",
        compiler_params=params(20),
    )(video, wk, wv, in_hbm(wq))


def total_call(parts, other_parts):
    frames, heads = parts.shape[:2]
    half = HEAD // 2

    def kernel(parts, other_parts, out, sent):
        low = lax.axis_index("space") == 0
        for h in range(heads):
            total = None
            for f in range(frames):
                one = parts[f, h].astype(F32) + other_parts[f, h].astype(F32)
                total = one if total is None else total + one
            total = jnp.where(low, total[:half], total[half:])
            out[h] = total
            sent[h] = total.astype(BF16)

    dims = (heads, half, HEAD)
    return pl.pallas_call(
        kernel,
        out_shape=[shape(dims, F32), shape(dims, BF16)],
        in_specs=[IN_VMEM] * 2,
        out_specs=[IN_VMEM] * 2,
        name="total",
        compiler_params=params(4),
    )(parts, other_parts)


def query_call(video, w, first, width):
    def kernel(video, w, out):
        out[...] = features(matmul(video[...], w[:, first : first + width])).astype(BF16)

    return pl.pallas_call(
        kernel,
        out_shape=shape((video.shape[0], width), BF16),
        in_specs=[IN_VMEM] * 2,
        out_specs=IN_VMEM,
        name="query",
        compiler_params=params(16),
    )(video, w)


def attend(frames, query, parts, other_parts, carry, other_carry, used, head_out):
    heads = carry.shape[0]
    per = query.shape[0] // frames
    low = lax.axis_index("space") == 0
    used[...] = jnp.zeros_like(used)
    for h in range(heads):
        mine, theirs = carry[h].astype(F32), other_carry[h].astype(F32)
        running = jnp.concatenate(
            [jnp.where(low, mine, theirs), jnp.where(low, theirs, mine)], axis=0
        )
        at = (h % 2) * HEAD
        for f in range(frames):
            running = running + parts[f, h].astype(F32) + other_parts[f, h].astype(F32)
            used[f, h // 2, at : at + HEAD, at : at + HEAD] = running.astype(BF16)
    for f in range(frames):
        rows = slice(f * per, (f + 1) * per)
        for p in range(pl.cdiv(heads, 2)):
            width = min(2, heads - 2 * p) * HEAD
            first = 2 * p * HEAD
            attended = matmul(
                query[rows, first : first + width], used[f, p, :width, :width]
            )
            for h in range(width // HEAD):
                one = attended[:, h * HEAD : (h + 1) * HEAD]
                scale = lax.rsqrt(jnp.mean(one * one, axis=1, keepdims=True) + EPS)
                at = first + h * HEAD
                head_out[rows, at : at + HEAD] = (one * scale).astype(BF16)


def used_shape(frames, heads):
    return pltpu.VMEM((frames, pl.cdiv(heads, 2), 2 * HEAD, 2 * HEAD), BF16)


def partial_call(video, chunk, w_out, frames):
    tokens, d = video.shape
    heads = chunk[3].shape[0]

    def kernel(video, query, parts, other_parts, carry, other_carry, w_out, out,
               used, head_out):
        attend(frames, query, parts, other_parts, carry, other_carry, used, head_out)
        per = tokens // frames
        for f in range(frames):
            rows = slice(f * per, (f + 1) * per)
            out[rows, :] = video[rows, :].astype(F32) + matmul(
                head_out[rows, :], w_out[: heads * HEAD, :]
            )

    return pl.pallas_call(
        kernel,
        out_shape=shape((tokens, d), F32),
        in_specs=[IN_VMEM] * 7,
        out_specs=IN_VMEM,
        scratch_shapes=[used_shape(frames, heads), pltpu.VMEM((tokens, heads * HEAD), BF16)],
        name="partial",
        compiler_params=params(20),
    )(video, *chunk, w_out)


def latent_kernel(
    frames, columns, tiles, partial, query, parts, other_parts, carry, other_carry,
    w_out, w_latent, out, used, head_out, latent,
):
    tokens, d = partial.shape
    per = tokens // frames
    width = head_out.shape[1]
    attend(frames, query, parts, other_parts, carry, other_carry, used, head_out)
    for f in range(frames):
        rows = slice(f * per, (f + 1) * per)
        summed = partial[rows, :] + matmul(head_out[rows, :], w_out[d - width :, :])
        scale = lax.rsqrt(jnp.mean(summed * summed, axis=1, keepdims=True) + EPS)
        latent[rows, :] = matmul((summed * scale).astype(BF16), w_latent[...])

    own = columns // tiles
    grid_rows = per // columns
    main = grid_rows * frames * own
    for t in range(tiles):
        for r in range(grid_rows):
            block = [
                latent[pl.ds(f * per + r * columns + t * own, own), :] for f in range(frames)
            ]
            at = r * frames * own
            out[t, at : at + frames * own, :] = jnp.concatenate(block, axis=0).astype(BF16)
        sides = []
        for column in (t * own - 1, (t + 1) * own):
            for f in range(frames):
                if 0 <= column < columns:
                    at = f * per + column
                    sides.append(latent[pl.ds(at, grid_rows, stride=columns), :])
                else:
                    sides.append(jnp.zeros((grid_rows, out.shape[2]), F32))
        out[t, main:, :] = jnp.concatenate(sides, axis=0).astype(BF16)


def latent_call(partial, chunk, w_out, w_latent, frames, columns, tiles):
    tokens, _ = partial.shape
    channels = w_latent.shape[1]
    heads = chunk[3].shape[0]
    rows = tokens // columns * (columns // tiles + 2)
    return pl.pallas_call(
        functools.partial(latent_kernel, frames, columns, tiles),
        out_shape=shape((tiles, rows, channels), BF16),
        in_specs=[IN_VMEM] * 8,
        out_specs=IN_VMEM,
        scratch_shapes=[
            used_shape(frames, heads),
            pltpu.VMEM((tokens, heads * HEAD), BF16),
            pltpu.VMEM((tokens, channels), F32),
        ],
        name="latent",
        compiler_params=params(20),
    )(partial, *chunk, w_out, w_latent)


def decode_kernel(
    frames, tiles, grid_rows, own, blocks, edge, weight, bias,
    out, left, middle, right, taps, wide,
):
    group = frames * own
    main = grid_rows * group
    tile = lax.axis_index("space")
    column = lax.broadcasted_iota(jnp.int32, (group, 1), 0) % own
    channels = weight.shape[2]

    def lay(row, t, body, sides):
        at = slice(t * group, (t + 1) * group)
        first = jnp.concatenate(
            [jnp.broadcast_to(sides[f : f + 1], (own, channels)) for f in range(frames)], axis=0
        )
        last = jnp.concatenate(
            [jnp.broadcast_to(sides[frames + f : frames + f + 1], (own, channels))
             for f in range(frames)], axis=0
        )
        down = pltpu.roll(body, 1, 0)
        up = pltpu.roll(body, group - 1, 0)
        left[row, at, :] = jnp.where(column == 0, first, down).astype(BF16)
        middle[row, at, :] = body.astype(BF16)
        right[row, at, :] = jnp.where(column == own - 1, last, up).astype(BF16)

    for t in range(tiles):
        everything = blocks[t].astype(F32)
        for r in range(grid_rows):
            body = everything[r * group : (r + 1) * group]
            sides = [
                everything[main + s * grid_rows + r : main + s * grid_rows + r + 1]
                for s in range(2 * frames)
            ]
            lay(r + 1, t, body, jnp.concatenate(sides, axis=0))
        beside = edge[t].astype(F32)
        for row, present in ((0, tile == 1), (grid_rows + 1, tile == 0)):
            there = jnp.where(present, beside, 0.0)
            lay(row, t, there[:group], there[group:])

    w = weight[...].astype(F32)
    row_sets = (((0,), (1, 2)), ((0, 1), (2,)))
    for a in range(2):
        for b in range(2):
            for i, rows in enumerate(row_sets[a]):
                for j, cols in enumerate(row_sets[b]):
                    tap = sum(w[r, c] for r in rows for c in cols)
                    at = (2 * i + j) * channels
                    taps[2 * a + b, at : at + channels, :] = tap.astype(BF16)

    views = ((left, middle), (middle, right))
    total = tiles * group
    for a in range(2):
        for b in range(2):
            lhs = jnp.concatenate(
                [v[a + i : a + i + grid_rows].reshape(grid_rows * total, channels)
                 for i in range(2) for v in views[b]], axis=1
            )
            mapped = matmul(lhs, taps[2 * a + b]) + bias[...]
            value = 0.5 * mapped * (1.0 + jnp.tanh(0.5 * mapped))
            for n in range(wide.shape[0]):
                wide[n, pl.ds(b, grid_rows * total, stride=2), :] = value[:, n * 128 : (n + 1) * 128]
        for n in range(wide.shape[0]):
            shaped = wide[n].reshape(grid_rows, tiles * frames, 2 * own, 128)
            for r in range(grid_rows):
                out[:, 2 * r + a, :, n * 128 : (n + 1) * 128] = shaped[r].astype(BF16)


def round_call(step, last, got, total, carry):
    def kernel(got, total, *refs):
        upper = (lax.axis_index("tm") // step) % 2 == 1
        received = got[...].astype(F32)
        before = jnp.where(upper, received, 0.0)
        if carry is not None:
            before = refs[0][...] + before
            refs = refs[1:]
        if last:
            refs[0][...] = before.astype(BF16)
        else:
            carry_out, total_out, sent_out = refs
            carry_out[...] = before
            both = total[...] + received
            total_out[...] = both
            sent_out[...] = both.astype(BF16)

    near = [got, total] + ([] if carry is None else [carry])
    kinds = [BF16] if last else [F32, F32, BF16]
    return pl.pallas_call(
        kernel,
        out_shape=[shape(total.shape, kind) for kind in kinds],
        in_specs=[IN_VMEM] * len(near),
        out_specs=[IN_VMEM] * len(kinds),
        name="round",
        compiler_params=params(4),
    )(*near)


def prefix_rounds(total, sent, tiles):
    carry = None
    step, number = 1, 0
    while step < tiles:
        last = 2 * step >= tiles
        if last:
            pairs = [(i, i + step) for i in range(step)]
        else:
            pairs = [(i, i ^ step) for i in range(tiles)]
        got = lax.ppermute(sent, "tm", pairs)
        out = round_call(step, last, got, total, carry)
        if last:
            return out[0]
        carry, total, sent = out
        step *= 2
        number += 1
    return jnp.zeros_like(sent)


SWAP = [(0, 1), (1, 0)]


def body(video, w_query, w_key, w_value, w_out, w_latent, conv_weight, conv_bias):
    frames, grid_rows, columns, d = video.shape
    tiles = lax.axis_size("tm")
    own = columns // tiles
    flat = video.reshape(-1, d)
    heads = d // HEAD
    split = heads // 3 * 2
    rest = heads - split
    parts_a, near, wk_b, wv_b = first_states(flat, w_key, w_value, frames, split, rest)
    other_a = lax.ppermute(parts_a, "space", SWAP)
    parts_b, near_query = second_states(near, wk_b, wv_b, w_query, frames)
    other_b = lax.ppermute(parts_b, "space", SWAP)

    ready = {}
    for name, first, parts, other in (("a", 0, parts_a, other_a), ("b", split, parts_b, other_b)):
        count = parts.shape[1]
        total, sent = total_call(parts, other)
        query = query_call(near, near_query, first * HEAD, count * HEAD)
        carry = prefix_rounds(total, sent, tiles)
        other_carry = lax.ppermute(carry, "space", SWAP)
        ready[name] = (query, parts, other, carry, other_carry)

    partial = partial_call(near, ready["a"], w_out, frames)
    blocks = latent_call(
        partial, ready["b"], w_out, w_latent, frames, columns, tiles
    )
    blocks = lax.all_to_all(blocks, "tm", 0, 0, tiled=True)
    return decode(blocks, conv_weight, conv_bias, frames, grid_rows, own, tiles)


def decode(blocks, conv_weight, conv_bias, frames, grid_rows, own, tiles):
    channels = conv_weight.shape[2]
    width = conv_weight.shape[3]
    group = frames * own
    main = grid_rows * group
    sides = blocks[:, main:].reshape(tiles, 2 * frames, grid_rows, channels)

    def edge(r):
        return jnp.concatenate([blocks[:, r * group : (r + 1) * group], sides[:, :, r]], axis=1)

    mine = jnp.where(lax.axis_index("space") == 0, edge(grid_rows - 1), edge(0))
    beside = lax.ppermute(mine, "space", SWAP)
    total = tiles * group
    return pl.pallas_call(
        functools.partial(decode_kernel, frames, tiles, grid_rows, own),
        out_shape=shape((tiles * frames, 2 * grid_rows, 2 * own, width), BF16),
        in_specs=[IN_VMEM] * 4,
        out_specs=IN_VMEM,
        scratch_shapes=[pltpu.VMEM((grid_rows + 2, total, channels), BF16)] * 3
        + [
            pltpu.VMEM((4, 4 * channels, width), BF16),
            pltpu.VMEM((width // 128, 2 * grid_rows * total, 128), F32),
        ],
        name="decode",
        compiler_params=params(36),
    )(blocks, beside, conv_weight, conv_bias.reshape(1, width))


def solution(mesh):
    assert mesh.shape["space"] == 2
    tiles = mesh.shape["tm"]
    assert tiles & (tiles - 1) == 0
    placed = (P(("groups", "tm"), "space", None, None), P(), P(), P(), P(), P(), P(), P())
    return jax.shard_map(
        body,
        mesh=mesh,
        in_specs=placed,
        out_specs=P("groups", "space", "tm", None),
        check_vma=False,
    )
```

```python
import functools

import jax
import jax.numpy as jnp
from jax import lax
from jax.experimental import pallas as pl
from jax.experimental.pallas import tpu as pltpu
from jax.sharding import PartitionSpec as P


HEAD = 128
EPS = 1e-06
BF16 = jnp.bfloat16
F32 = jnp.float32


IN_HBM = pl.BlockSpec(memory_space=pltpu.HBM)
IN_VMEM = pl.BlockSpec(memory_space=pltpu.VMEM)


def shape(dims, dtype):
    return jax.ShapeDtypeStruct(dims, dtype)


def params(megabytes):
    return pltpu.CompilerParams(vmem_limit_bytes=megabytes << 20)


def in_hbm(x):
    return pltpu.with_memory_space_constraint(x, pltpu.HBM)


def matmul(a, b):
    return jnp.dot(a, b, preferred_element_type=F32)


def features(x):
    return jnp.where(x > 0.0, x + 1.0, jnp.exp(jnp.minimum(x, 0.0)))


def states_kernel(frames, heads, fetched, video_in, wk_hbm, wv_hbm, *refs):
    if fetched:
        parts_out, key, value = refs
        video, wk, wv = video_in, wk_hbm, wv_hbm
        late = []
    else:
        (wq_hbm, parts_out, video, wk_out, wv_out, wq_out, wk, wv, key, value,
         wk_sem, wv_sem, video_sem, late_sem) = refs
        rest = wk_out.shape[1]
        source = pl.ds(heads * HEAD, rest)
        late = [
            pltpu.make_async_copy(wq_hbm, wq_out, late_sem.at[0]),
            pltpu.make_async_copy(wk_hbm.at[:, source], wk_out, late_sem.at[1]),
            pltpu.make_async_copy(wv_hbm.at[:, source], wv_out, late_sem.at[2]),
        ]
    per = video.shape[0] // frames

    def weight_copies(h):
        cols = pl.ds(pl.multiple_of(h * HEAD, HEAD), HEAD)
        return (
            pltpu.make_async_copy(wk_hbm.at[:, cols], wk.at[:, cols], wk_sem.at[h]),
            pltpu.make_async_copy(wv_hbm.at[:, cols], wv.at[:, cols], wv_sem.at[h]),
        )

    def video_copy(f):
        rows = pl.ds(f * per, per)
        return pltpu.make_async_copy(video_in.at[rows], video.at[rows], video_sem.at[f])

    if not fetched:
        soon = min(2, heads)
        for h in range(soon):
            for c in weight_copies(h):
                c.start()
        for f in range(frames):
            video_copy(f).start()
        for f in range(frames):
            video_copy(f).wait()
        for h in range(soon, heads):
            for c in weight_copies(h):
                c.start()
        for c in late:
            c.start()

    def one_head(h, carry):
        if not fetched:
            for c in weight_copies(h):
                c.wait()
        cols = pl.ds(pl.multiple_of(h * HEAD, HEAD), HEAD)
        both = jnp.concatenate([wk[:, cols], wv[:, cols]], axis=1)
        for f in range(frames):
            rows = slice(f * per, (f + 1) * per)
            kv = matmul(video[rows, :], both)
            key[h, rows, :] = features(kv[:, :HEAD]).astype(BF16)
            value[h, rows, :] = kv[:, HEAD:].astype(BF16)
        return carry

    lax.fori_loop(0, heads, one_head, 0)

    for h in range(heads):
        for f in range(frames):
            rows = slice(f * per, (f + 1) * per)
            state = lax.dot_general(
                key[h, rows, :], value[h, rows, :], (((0,), (0,)), ((), ())),
                preferred_element_type=F32,
            )
            parts_out[f, h] = state.astype(BF16)
    for c in late:
        c.wait()


def first_states(video, wk, wv, wq, frames, heads):
    tokens, d = video.shape
    width = heads * HEAD
    return pl.pallas_call(
        functools.partial(states_kernel, frames, heads, False),
        out_shape=[
            shape((frames, heads, HEAD, HEAD), BF16),
            shape((tokens, d), BF16),
            shape((d, d - width), BF16),
            shape((d, d - width), BF16),
            shape((d, d), BF16),
        ],
        in_specs=[IN_HBM] * 4,
        out_specs=[IN_VMEM] * 5,
        scratch_shapes=[
            pltpu.VMEM((d, width), BF16),
            pltpu.VMEM((d, width), BF16),
            pltpu.VMEM((heads, tokens, HEAD), BF16),
            pltpu.VMEM((heads, tokens, HEAD), BF16),
            pltpu.SemaphoreType.DMA((heads,)),
            pltpu.SemaphoreType.DMA((heads,)),
            pltpu.SemaphoreType.DMA((frames,)),
            pltpu.SemaphoreType.DMA((3,)),
        ],
        name="states",
        compiler_params=params(20),
    )(in_hbm(video), in_hbm(wk), in_hbm(wv), in_hbm(wq))


def second_states(video, wk, wv, frames):
    tokens, _ = video.shape
    heads = wk.shape[1] // HEAD
    return pl.pallas_call(
        functools.partial(states_kernel, frames, heads, True),
        out_shape=shape((frames, heads, HEAD, HEAD), BF16),
        in_specs=[IN_VMEM] * 3,
        out_specs=IN_VMEM,
        scratch_shapes=[
            pltpu.VMEM((heads, tokens, HEAD), BF16),
            pltpu.VMEM((heads, tokens, HEAD), BF16),
        ],
        name="states",
        compiler_params=params(20),
    )(video, wk, wv)


def total_call(parts, other_parts):
    frames, heads = parts.shape[:2]
    half = HEAD // 2

    def kernel(parts, other_parts, out, sent):
        low = lax.axis_index("space") == 0
        for h in range(heads):
            total = None
            for f in range(frames):
                one = parts[f, h].astype(F32) + other_parts[f, h].astype(F32)
                total = one if total is None else total + one
            total = jnp.where(low, total[:half], total[half:])
            out[h] = total
            sent[h] = total.astype(BF16)

    dims = (heads, half, HEAD)
    return pl.pallas_call(
        kernel,
        out_shape=[shape(dims, F32), shape(dims, BF16)],
        in_specs=[IN_VMEM] * 2,
        out_specs=[IN_VMEM] * 2,
        name="total",
        compiler_params=params(4),
    )(parts, other_parts)


def query_call(video, w, first, width):
    def kernel(video, w, out):
        out[...] = features(matmul(video[...], w[:, first : first + width])).astype(BF16)

    return pl.pallas_call(
        kernel,
        out_shape=shape((video.shape[0], width), BF16),
        in_specs=[IN_VMEM] * 2,
        out_specs=IN_VMEM,
        name="query",
        compiler_params=params(16),
    )(video, w)


def attend(frames, query, parts, other_parts, carry, other_carry, used, head_out):
    heads = carry.shape[0]
    per = query.shape[0] // frames
    low = lax.axis_index("space") == 0
    used[...] = jnp.zeros_like(used)
    for h in range(heads):
        mine, theirs = carry[h].astype(F32), other_carry[h].astype(F32)
        running = jnp.concatenate(
            [jnp.where(low, mine, theirs), jnp.where(low, theirs, mine)], axis=0
        )
        at = (h % 2) * HEAD
        for f in range(frames):
            running = running + parts[f, h].astype(F32) + other_parts[f, h].astype(F32)
            used[f, h // 2, at : at + HEAD, at : at + HEAD] = running.astype(BF16)
    for f in range(frames):
        rows = slice(f * per, (f + 1) * per)
        for p in range(pl.cdiv(heads, 2)):
            width = min(2, heads - 2 * p) * HEAD
            first = 2 * p * HEAD
            attended = matmul(
                query[rows, first : first + width], used[f, p, :width, :width]
            )
            for h in range(width // HEAD):
                one = attended[:, h * HEAD : (h + 1) * HEAD]
                scale = lax.rsqrt(jnp.mean(one * one, axis=1, keepdims=True) + EPS)
                at = first + h * HEAD
                head_out[rows, at : at + HEAD] = (one * scale).astype(BF16)


def used_shape(frames, heads):
    return pltpu.VMEM((frames, pl.cdiv(heads, 2), 2 * HEAD, 2 * HEAD), BF16)


def partial_call(video, chunk, w_out, frames):
    tokens, d = video.shape
    heads = chunk[3].shape[0]

    def kernel(video, query, parts, other_parts, carry, other_carry, w_out, out,
               used, head_out):
        attend(frames, query, parts, other_parts, carry, other_carry, used, head_out)
        per = tokens // frames
        for f in range(frames):
            rows = slice(f * per, (f + 1) * per)
            out[rows, :] = video[rows, :].astype(F32) + matmul(
                head_out[rows, :], w_out[: heads * HEAD, :]
            )

    return pl.pallas_call(
        kernel,
        out_shape=shape((tokens, d), F32),
        in_specs=[IN_VMEM] * 7,
        out_specs=IN_VMEM,
        scratch_shapes=[used_shape(frames, heads), pltpu.VMEM((tokens, heads * HEAD), BF16)],
        name="partial",
        compiler_params=params(20),
    )(video, *chunk, w_out)


def latent_kernel(
    frames, columns, tiles, partial, query, parts, other_parts, carry, other_carry,
    w_out, w_latent, out, used, head_out, latent,
):
    tokens, d = partial.shape
    per = tokens // frames
    width = head_out.shape[1]
    attend(frames, query, parts, other_parts, carry, other_carry, used, head_out)
    for f in range(frames):
        rows = slice(f * per, (f + 1) * per)
        summed = partial[rows, :] + matmul(head_out[rows, :], w_out[d - width :, :])
        scale = lax.rsqrt(jnp.mean(summed * summed, axis=1, keepdims=True) + EPS)
        latent[rows, :] = matmul((summed * scale).astype(BF16), w_latent[...])

    own = columns // tiles
    grid_rows = per // columns
    main = grid_rows * frames * own
    for t in range(tiles):
        for r in range(grid_rows):
            block = [
                latent[pl.ds(f * per + r * columns + t * own, own), :] for f in range(frames)
            ]
            at = r * frames * own
            out[t, at : at + frames * own, :] = jnp.concatenate(block, axis=0).astype(BF16)
        sides = []
        for column in (t * own - 1, (t + 1) * own):
            for f in range(frames):
                if 0 <= column < columns:
                    at = f * per + column
                    sides.append(latent[pl.ds(at, grid_rows, stride=columns), :])
                else:
                    sides.append(jnp.zeros((grid_rows, out.shape[2]), F32))
        out[t, main:, :] = jnp.concatenate(sides, axis=0).astype(BF16)


def latent_call(partial, chunk, w_out, w_latent, frames, columns, tiles):
    tokens, _ = partial.shape
    channels = w_latent.shape[1]
    heads = chunk[3].shape[0]
    rows = tokens // columns * (columns // tiles + 2)
    return pl.pallas_call(
        functools.partial(latent_kernel, frames, columns, tiles),
        out_shape=shape((tiles, rows, channels), BF16),
        in_specs=[IN_VMEM] * 8,
        out_specs=IN_VMEM,
        scratch_shapes=[
            used_shape(frames, heads),
            pltpu.VMEM((tokens, heads * HEAD), BF16),
            pltpu.VMEM((tokens, channels), F32),
        ],
        name="latent",
        compiler_params=params(20),
    )(partial, *chunk, w_out, w_latent)


def decode_kernel(
    frames, tiles, grid_rows, own, blocks, edge, weight, bias,
    out, left, middle, right, taps, wide,
):
    group = frames * own
    main = grid_rows * group
    tile = lax.axis_index("space")
    column = lax.broadcasted_iota(jnp.int32, (group, 1), 0) % own
    channels = weight.shape[2]

    def lay(row, t, body, sides):
        at = slice(t * group, (t + 1) * group)
        first = jnp.concatenate(
            [jnp.broadcast_to(sides[f : f + 1], (own, channels)) for f in range(frames)], axis=0
        )
        last = jnp.concatenate(
            [jnp.broadcast_to(sides[frames + f : frames + f + 1], (own, channels))
             for f in range(frames)], axis=0
        )
        down = pltpu.roll(body, 1, 0)
        up = pltpu.roll(body, group - 1, 0)
        left[row, at, :] = jnp.where(column == 0, first, down).astype(BF16)
        middle[row, at, :] = body.astype(BF16)
        right[row, at, :] = jnp.where(column == own - 1, last, up).astype(BF16)

    for t in range(tiles):
        everything = blocks[t].astype(F32)
        for r in range(grid_rows):
            body = everything[r * group : (r + 1) * group]
            sides = [
                everything[main + s * grid_rows + r : main + s * grid_rows + r + 1]
                for s in range(2 * frames)
            ]
            lay(r + 1, t, body, jnp.concatenate(sides, axis=0))
        beside = edge[t].astype(F32)
        for row, present in ((0, tile == 1), (grid_rows + 1, tile == 0)):
            there = jnp.where(present, beside, 0.0)
            lay(row, t, there[:group], there[group:])

    w = weight[...].astype(F32)
    row_sets = (((0,), (1, 2)), ((0, 1), (2,)))
    for a in range(2):
        for b in range(2):
            for i, rows in enumerate(row_sets[a]):
                for j, cols in enumerate(row_sets[b]):
                    tap = sum(w[r, c] for r in rows for c in cols)
                    at = (2 * i + j) * channels
                    taps[2 * a + b, at : at + channels, :] = tap.astype(BF16)

    views = ((left, middle), (middle, right))
    total = tiles * group
    for a in range(2):
        for b in range(2):
            lhs = jnp.concatenate(
                [v[a + i : a + i + grid_rows].reshape(grid_rows * total, channels)
                 for i in range(2) for v in views[b]], axis=1
            )
            mapped = matmul(lhs, taps[2 * a + b]) + bias[...]
            value = 0.5 * mapped * (1.0 + jnp.tanh(0.5 * mapped))
            for n in range(wide.shape[0]):
                wide[n, pl.ds(b, grid_rows * total, stride=2), :] = value[:, n * 128 : (n + 1) * 128]
        for n in range(wide.shape[0]):
            shaped = wide[n].reshape(grid_rows, tiles * frames, 2 * own, 128)
            for r in range(grid_rows):
                out[:, 2 * r + a, :, n * 128 : (n + 1) * 128] = shaped[r].astype(BF16)


def round_call(step, last, got, total, carry):
    def kernel(got, total, *refs):
        upper = (lax.axis_index("tm") // step) % 2 == 1
        received = got[...].astype(F32)
        before = jnp.where(upper, received, 0.0)
        if carry is not None:
            before = refs[0][...] + before
            refs = refs[1:]
        if last:
            refs[0][...] = before.astype(BF16)
        else:
            carry_out, total_out, sent_out = refs
            carry_out[...] = before
            both = total[...] + received
            total_out[...] = both
            sent_out[...] = both.astype(BF16)

    near = [got, total] + ([] if carry is None else [carry])
    kinds = [BF16] if last else [F32, F32, BF16]
    return pl.pallas_call(
        kernel,
        out_shape=[shape(total.shape, kind) for kind in kinds],
        in_specs=[IN_VMEM] * len(near),
        out_specs=[IN_VMEM] * len(kinds),
        name="round",
        compiler_params=params(4),
    )(*near)


def prefix_rounds(total, sent, tiles):
    carry = None
    step, number = 1, 0
    while step < tiles:
        last = 2 * step >= tiles
        if last:
            pairs = [(i, i + step) for i in range(step)]
        else:
            pairs = [(i, i ^ step) for i in range(tiles)]
        got = lax.ppermute(sent, "tm", pairs)
        out = round_call(step, last, got, total, carry)
        if last:
            return out[0]
        carry, total, sent = out
        step *= 2
        number += 1
    return jnp.zeros_like(sent)


SWAP = [(0, 1), (1, 0)]


def body(video, w_query, w_key, w_value, w_out, w_latent, conv_weight, conv_bias):
    frames, grid_rows, columns, d = video.shape
    tiles = lax.axis_size("tm")
    own = columns // tiles
    flat = video.reshape(-1, d)
    heads = d // HEAD
    split = heads - heads // 2
    parts_a, near, wk_b, wv_b, near_query = first_states(
        flat, w_key, w_value, w_query, frames, split
    )
    other_a = lax.ppermute(parts_a, "space", SWAP)
    parts_b = second_states(near, wk_b, wv_b, frames)
    other_b = lax.ppermute(parts_b, "space", SWAP)

    ready = {}
    for name, first, parts, other in (
        ("a", 0, parts_a, other_a), ("b", split, parts_b, other_b),
    ):
        count = parts.shape[1]
        total, sent = total_call(parts, other)
        query = query_call(near, near_query, first * HEAD, count * HEAD)
        carry = prefix_rounds(total, sent, tiles)
        other_carry = lax.ppermute(carry, "space", SWAP)
        ready[name] = (query, parts, other, carry, other_carry)

    partial = partial_call(near, ready["a"], w_out, frames)
    blocks = latent_call(partial, ready["b"], w_out, w_latent, frames, columns, tiles)
    blocks = lax.all_to_all(blocks, "tm", 0, 0, tiled=True)
    return decode(blocks, conv_weight, conv_bias, frames, grid_rows, own, tiles)


def decode(blocks, conv_weight, conv_bias, frames, grid_rows, own, tiles):
    channels = conv_weight.shape[2]
    width = conv_weight.shape[3]
    group = frames * own
    main = grid_rows * group
    sides = blocks[:, main:].reshape(tiles, 2 * frames, grid_rows, channels)

    def edge(r):
        return jnp.concatenate([blocks[:, r * group : (r + 1) * group], sides[:, :, r]], axis=1)

    mine = jnp.where(lax.axis_index("space") == 0, edge(grid_rows - 1), edge(0))
    beside = lax.ppermute(mine, "space", SWAP)
    total = tiles * group
    return pl.pallas_call(
        functools.partial(decode_kernel, frames, tiles, grid_rows, own),
        out_shape=shape((tiles * frames, 2 * grid_rows, 2 * own, width), BF16),
        in_specs=[IN_VMEM] * 4,
        out_specs=IN_VMEM,
        scratch_shapes=[pltpu.VMEM((grid_rows + 2, total, channels), BF16)] * 3
        + [
            pltpu.VMEM((4, 4 * channels, width), BF16),
            pltpu.VMEM((width // 128, 2 * grid_rows * total, 128), F32),
        ],
        name="decode",
        compiler_params=params(36),
    )(blocks, beside, conv_weight, conv_bias.reshape(1, width))


def solution(mesh):
    assert mesh.shape["space"] == 2
    tiles = mesh.shape["tm"]
    assert tiles & (tiles - 1) == 0
    placed = (P(("groups", "tm"), "space", None, None), P(), P(), P(), P(), P(), P(), P())
    return jax.shard_map(
        body,
        mesh=mesh,
        in_specs=placed,
        out_specs=P("groups", "space", "tm", None),
        check_vma=False,
    )
```

```python
import functools

import jax
import jax.numpy as jnp
from jax import lax
from jax.experimental import pallas as pl
from jax.experimental.pallas import tpu as pltpu
from jax.sharding import PartitionSpec as P


HEAD = 128
EPS = 1e-06
BF16 = jnp.bfloat16
F32 = jnp.float32


IN_HBM = pl.BlockSpec(memory_space=pltpu.HBM)
IN_VMEM = pl.BlockSpec(memory_space=pltpu.VMEM)


def shape(dims, dtype):
    return jax.ShapeDtypeStruct(dims, dtype)


def params(megabytes):
    return pltpu.CompilerParams(vmem_limit_bytes=megabytes << 20)


def in_hbm(x):
    return pltpu.with_memory_space_constraint(x, pltpu.HBM)


def matmul(a, b):
    return jnp.dot(a, b, preferred_element_type=F32)


def features(x):
    return jnp.where(x > 0.0, x + 1.0, jnp.exp(jnp.minimum(x, 0.0)))


def states_kernel(frames, heads, fetched, video_in, wk_hbm, wv_hbm, *refs):
    if fetched:
        parts_out, key, value = refs
        video, wk, wv = video_in, wk_hbm, wv_hbm
        late = []
    else:
        (wq_hbm, parts_out, video, wk_out, wv_out, wq_out, wk, wv, key, value,
         wk_sem, wv_sem, video_sem, late_sem) = refs
        rest = wk_out.shape[1]
        source = pl.ds(heads * HEAD, rest)
        late = [
            pltpu.make_async_copy(wq_hbm, wq_out, late_sem.at[0]),
            pltpu.make_async_copy(wk_hbm.at[:, source], wk_out, late_sem.at[1]),
            pltpu.make_async_copy(wv_hbm.at[:, source], wv_out, late_sem.at[2]),
        ]
    per = video.shape[0] // frames

    def weight_copies(h):
        cols = pl.ds(pl.multiple_of(h * HEAD, HEAD), HEAD)
        return (
            pltpu.make_async_copy(wk_hbm.at[:, cols], wk.at[:, cols], wk_sem.at[h]),
            pltpu.make_async_copy(wv_hbm.at[:, cols], wv.at[:, cols], wv_sem.at[h]),
        )

    def video_copy(f):
        rows = pl.ds(f * per, per)
        return pltpu.make_async_copy(video_in.at[rows], video.at[rows], video_sem.at[f])

    if not fetched:
        soon = min(2, heads)
        for h in range(soon):
            for c in weight_copies(h):
                c.start()
        for f in range(frames):
            video_copy(f).start()
        for f in range(frames):
            video_copy(f).wait()
        for h in range(soon, heads):
            for c in weight_copies(h):
                c.start()
        for c in late:
            c.start()

    def one_head(h, carry):
        if not fetched:
            for c in weight_copies(h):
                c.wait()
        cols = pl.ds(pl.multiple_of(h * HEAD, HEAD), HEAD)
        both = jnp.concatenate([wk[:, cols], wv[:, cols]], axis=1)
        for f in range(frames):
            rows = slice(f * per, (f + 1) * per)
            kv = matmul(video[rows, :], both)
            key[h, rows, :] = features(kv[:, :HEAD]).astype(BF16)
            value[h, rows, :] = kv[:, HEAD:].astype(BF16)
        return carry

    lax.fori_loop(0, heads, one_head, 0)

    for h in range(heads):
        for f in range(frames):
            rows = slice(f * per, (f + 1) * per)
            state = lax.dot_general(
                key[h, rows, :], value[h, rows, :], (((0,), (0,)), ((), ())),
                preferred_element_type=F32,
            )
            parts_out[f, h] = state.astype(BF16)
    for c in late:
        c.wait()


def first_states(video, wk, wv, wq, frames, heads):
    tokens, d = video.shape
    width = heads * HEAD
    return pl.pallas_call(
        functools.partial(states_kernel, frames, heads, False),
        out_shape=[
            shape((frames, heads, HEAD, HEAD), BF16),
            shape((tokens, d), BF16),
            shape((d, d - width), BF16),
            shape((d, d - width), BF16),
            shape((d, d), BF16),
        ],
        in_specs=[IN_HBM] * 4,
        out_specs=[IN_VMEM] * 5,
        scratch_shapes=[
            pltpu.VMEM((d, width), BF16),
            pltpu.VMEM((d, width), BF16),
            pltpu.VMEM((heads, tokens, HEAD), BF16),
            pltpu.VMEM((heads, tokens, HEAD), BF16),
            pltpu.SemaphoreType.DMA((heads,)),
            pltpu.SemaphoreType.DMA((heads,)),
            pltpu.SemaphoreType.DMA((frames,)),
            pltpu.SemaphoreType.DMA((3,)),
        ],
        name="states",
        compiler_params=params(20),
    )(in_hbm(video), in_hbm(wk), in_hbm(wv), in_hbm(wq))


def second_states(video, wk, wv, frames):
    tokens, _ = video.shape
    heads = wk.shape[1] // HEAD
    return pl.pallas_call(
        functools.partial(states_kernel, frames, heads, True),
        out_shape=shape((frames, heads, HEAD, HEAD), BF16),
        in_specs=[IN_VMEM] * 3,
        out_specs=IN_VMEM,
        scratch_shapes=[
            pltpu.VMEM((heads, tokens, HEAD), BF16),
            pltpu.VMEM((heads, tokens, HEAD), BF16),
        ],
        name="states",
        compiler_params=params(20),
    )(video, wk, wv)


def total_call(parts, other_parts):
    frames, heads = parts.shape[:2]
    half = HEAD // 2

    def kernel(parts, other_parts, out, sent):
        low = lax.axis_index("space") == 0
        for h in range(heads):
            total = None
            for f in range(frames):
                one = parts[f, h].astype(F32) + other_parts[f, h].astype(F32)
                total = one if total is None else total + one
            total = jnp.where(low, total[:half], total[half:])
            out[h] = total
            sent[h] = total.astype(BF16)

    dims = (heads, half, HEAD)
    return pl.pallas_call(
        kernel,
        out_shape=[shape(dims, F32), shape(dims, BF16)],
        in_specs=[IN_VMEM] * 2,
        out_specs=[IN_VMEM] * 2,
        name="total",
        compiler_params=params(4),
    )(parts, other_parts)


def query_call(video, w, first, width):
    def kernel(video, w, out):
        out[...] = features(matmul(video[...], w[:, first : first + width])).astype(BF16)

    return pl.pallas_call(
        kernel,
        out_shape=shape((video.shape[0], width), BF16),
        in_specs=[IN_VMEM] * 2,
        out_specs=IN_VMEM,
        name="query",
        compiler_params=params(16),
    )(video, w)


def attend(frames, query, parts, other_parts, carry, other_carry, used, head_out):
    heads = carry.shape[0]
    per = query.shape[0] // frames
    low = lax.axis_index("space") == 0
    used[...] = jnp.zeros_like(used)
    for h in range(heads):
        mine, theirs = carry[h].astype(F32), other_carry[h].astype(F32)
        running = jnp.concatenate(
            [jnp.where(low, mine, theirs), jnp.where(low, theirs, mine)], axis=0
        )
        at = (h % 2) * HEAD
        for f in range(frames):
            running = running + parts[f, h].astype(F32) + other_parts[f, h].astype(F32)
            used[f, h // 2, at : at + HEAD, at : at + HEAD] = running.astype(BF16)
    for f in range(frames):
        rows = slice(f * per, (f + 1) * per)
        for p in range(pl.cdiv(heads, 2)):
            width = min(2, heads - 2 * p) * HEAD
            first = 2 * p * HEAD
            attended = matmul(
                query[rows, first : first + width], used[f, p, :width, :width]
            )
            for h in range(width // HEAD):
                one = attended[:, h * HEAD : (h + 1) * HEAD]
                scale = lax.rsqrt(jnp.mean(one * one, axis=1, keepdims=True) + EPS)
                at = first + h * HEAD
                head_out[rows, at : at + HEAD] = (one * scale).astype(BF16)


def used_shape(frames, heads):
    return pltpu.VMEM((frames, pl.cdiv(heads, 2), 2 * HEAD, 2 * HEAD), BF16)


def partial_call(video, chunk, w_out, frames):
    tokens, d = video.shape
    heads = chunk[3].shape[0]

    def kernel(video, query, parts, other_parts, carry, other_carry, w_out, out,
               used, head_out):
        attend(frames, query, parts, other_parts, carry, other_carry, used, head_out)
        per = tokens // frames
        for f in range(frames):
            rows = slice(f * per, (f + 1) * per)
            out[rows, :] = video[rows, :].astype(F32) + matmul(
                head_out[rows, :], w_out[: heads * HEAD, :]
            )

    return pl.pallas_call(
        kernel,
        out_shape=shape((tokens, d), F32),
        in_specs=[IN_VMEM] * 7,
        out_specs=IN_VMEM,
        scratch_shapes=[used_shape(frames, heads), pltpu.VMEM((tokens, heads * HEAD), BF16)],
        name="partial",
        compiler_params=params(20),
    )(video, *chunk, w_out)


def latent_kernel(
    frames, columns, tiles, partial, query, parts, other_parts, carry, other_carry,
    w_out, w_latent, out, used, head_out, latent,
):
    tokens, d = partial.shape
    per = tokens // frames
    width = head_out.shape[1]
    attend(frames, query, parts, other_parts, carry, other_carry, used, head_out)
    for f in range(frames):
        rows = slice(f * per, (f + 1) * per)
        summed = partial[rows, :] + matmul(head_out[rows, :], w_out[d - width :, :])
        scale = lax.rsqrt(jnp.mean(summed * summed, axis=1, keepdims=True) + EPS)
        latent[rows, :] = matmul(summed.astype(BF16), w_latent[...]) * scale

    own = columns // tiles
    grid_rows = per // columns
    main = grid_rows * frames * own
    for t in range(tiles):
        for r in range(grid_rows):
            block = [
                latent[pl.ds(f * per + r * columns + t * own, own), :] for f in range(frames)
            ]
            at = r * frames * own
            out[t, at : at + frames * own, :] = jnp.concatenate(block, axis=0).astype(BF16)
        sides = []
        for column in (t * own - 1, (t + 1) * own):
            for f in range(frames):
                if 0 <= column < columns:
                    at = f * per + column
                    sides.append(latent[pl.ds(at, grid_rows, stride=columns), :])
                else:
                    sides.append(jnp.zeros((grid_rows, out.shape[2]), F32))
        out[t, main:, :] = jnp.concatenate(sides, axis=0).astype(BF16)


def latent_call(partial, chunk, w_out, w_latent, frames, columns, tiles):
    tokens, _ = partial.shape
    channels = w_latent.shape[1]
    heads = chunk[3].shape[0]
    rows = tokens // columns * (columns // tiles + 2)
    return pl.pallas_call(
        functools.partial(latent_kernel, frames, columns, tiles),
        out_shape=shape((tiles, rows, channels), BF16),
        in_specs=[IN_VMEM] * 8,
        out_specs=IN_VMEM,
        scratch_shapes=[
            used_shape(frames, heads),
            pltpu.VMEM((tokens, heads * HEAD), BF16),
            pltpu.VMEM((tokens, channels), F32),
        ],
        name="latent",
        compiler_params=params(20),
    )(partial, *chunk, w_out, w_latent)


def decode_kernel(
    frames, tiles, grid_rows, own, chunk, blocks, edge, weight, bias,
    out, left, middle, right, taps, wide, staged, sem,
):
    group = frames * own
    main = grid_rows * group
    tile = lax.axis_index("space")
    column = lax.broadcasted_iota(jnp.int32, (group, 1), 0) % own
    channels = weight.shape[2]

    def lay(row, t, body, sides):
        at = slice(t * group, (t + 1) * group)
        first = jnp.concatenate(
            [jnp.broadcast_to(sides[f : f + 1], (own, channels)) for f in range(frames)], axis=0
        )
        last = jnp.concatenate(
            [jnp.broadcast_to(sides[frames + f : frames + f + 1], (own, channels))
             for f in range(frames)], axis=0
        )
        down = pltpu.roll(body, 1, 0)
        up = pltpu.roll(body, group - 1, 0)
        left[row, at, :] = jnp.where(column == 0, first, down).astype(BF16)
        middle[row, at, :] = body.astype(BF16)
        right[row, at, :] = jnp.where(column == own - 1, last, up).astype(BF16)

    for t in range(tiles):
        everything = blocks[t].astype(F32)
        for r in range(grid_rows):
            body = everything[r * group : (r + 1) * group]
            sides = [
                everything[main + s * grid_rows + r : main + s * grid_rows + r + 1]
                for s in range(2 * frames)
            ]
            lay(r + 1, t, body, jnp.concatenate(sides, axis=0))
        beside = edge[t].astype(F32)
        for row, present in ((0, tile == 1), (grid_rows + 1, tile == 0)):
            there = jnp.where(present, beside, 0.0)
            lay(row, t, there[:group], there[group:])

    w = weight[...].astype(F32)
    row_sets = (((0,), (1, 2)), ((0, 1), (2,)))
    for a in range(2):
        for b in range(2):
            for i, rows in enumerate(row_sets[a]):
                for j, cols in enumerate(row_sets[b]):
                    tap = sum(w[r, c] for r in rows for c in cols)
                    at = (2 * i + j) * channels
                    taps[2 * a + b, at : at + channels, :] = (0.5 * tap).astype(BF16)

    views = ((left, middle), (middle, right))
    total = tiles * group
    half_bias = 0.5 * bias[...]
    lanes = wide.shape[-1]
    copies = []
    for i in range(grid_rows // chunk):
        for a in range(2):
            for b in range(2):
                lhs = jnp.concatenate(
                    [v[i * chunk + a + k : i * chunk + a + k + chunk].reshape(
                        chunk * total, channels) for k in range(2) for v in views[b]], axis=1
                )
                h = matmul(lhs, taps[2 * a + b]) + half_bias
                value = h + h * jnp.tanh(h)
                for n in range(wide.shape[1]):
                    wide[a, n, pl.ds(b, chunk * total, stride=2), :] = (
                        value[:, n * lanes : (n + 1) * lanes]
                    )
            for n in range(wide.shape[1]):
                shaped = wide[a, n].reshape(chunk, tiles * frames, 2 * own, lanes)
                for r in range(chunk):
                    staged[:, 2 * (i * chunk + r) + a, :, n * lanes : (n + 1) * lanes] = (
                        shaped[r].astype(BF16)
                    )
        rows = pl.ds(2 * i * chunk, 2 * chunk)
        copies.append(pltpu.make_async_copy(staged.at[:, rows], out.at[:, rows], sem.at[i]))
        copies[-1].start()
    for c in copies:
        c.wait()


def round_call(step, last, got, total, carry):
    def kernel(got, total, *refs):
        upper = (lax.axis_index("tm") // step) % 2 == 1
        received = got[...].astype(F32)
        before = jnp.where(upper, received, 0.0)
        if carry is not None:
            before = refs[0][...] + before
            refs = refs[1:]
        if last:
            refs[0][...] = before.astype(BF16)
        else:
            carry_out, total_out, sent_out = refs
            carry_out[...] = before
            both = total[...] + received
            total_out[...] = both
            sent_out[...] = both.astype(BF16)

    near = [got, total] + ([] if carry is None else [carry])
    kinds = [BF16] if last else [F32, F32, BF16]
    return pl.pallas_call(
        kernel,
        out_shape=[shape(total.shape, kind) for kind in kinds],
        in_specs=[IN_VMEM] * len(near),
        out_specs=[IN_VMEM] * len(kinds),
        name="round",
        compiler_params=params(4),
    )(*near)


def prefix_rounds(total, sent, tiles):
    carry = None
    step, number = 1, 0
    while step < tiles:
        last = 2 * step >= tiles
        if last:
            pairs = [(i, i + step) for i in range(step)]
        else:
            pairs = [(i, i ^ step) for i in range(tiles)]
        got = lax.ppermute(sent, "tm", pairs)
        out = round_call(step, last, got, total, carry)
        if last:
            return out[0]
        carry, total, sent = out
        step *= 2
        number += 1
    return jnp.zeros_like(sent)


SWAP = [(0, 1), (1, 0)]


def body(video, w_query, w_key, w_value, w_out, w_latent, conv_weight, conv_bias):
    frames, grid_rows, columns, d = video.shape
    tiles = lax.axis_size("tm")
    own = columns // tiles
    flat = video.reshape(-1, d)
    heads = d // HEAD
    split = heads - heads // 2
    parts_a, near, wk_b, wv_b, near_query = first_states(
        flat, w_key, w_value, w_query, frames, split
    )
    other_a = lax.ppermute(parts_a, "space", SWAP)
    parts_b = second_states(near, wk_b, wv_b, frames)
    other_b = lax.ppermute(parts_b, "space", SWAP)

    ready = {}
    for name, first, parts, other in (("a", 0, parts_a, other_a), ("b", split, parts_b, other_b)):
        count = parts.shape[1]
        total, sent = total_call(parts, other)
        query = query_call(near, near_query, first * HEAD, count * HEAD)
        carry = prefix_rounds(total, sent, tiles)
        other_carry = lax.ppermute(carry, "space", SWAP)
        ready[name] = (query, parts, other, carry, other_carry)

    partial = partial_call(near, ready["a"], w_out, frames)
    blocks = latent_call(
        partial, ready["b"], w_out, w_latent, frames, columns, tiles
    )
    blocks = lax.all_to_all(blocks, "tm", 0, 0, tiled=True)
    return decode(blocks, conv_weight, conv_bias, frames, grid_rows, own, tiles)


def decode(blocks, conv_weight, conv_bias, frames, grid_rows, own, tiles):
    channels = conv_weight.shape[2]
    width = conv_weight.shape[3]
    group = frames * own
    main = grid_rows * group
    sides = blocks[:, main:].reshape(tiles, 2 * frames, grid_rows, channels)

    def edge(r):
        return jnp.concatenate([blocks[:, r * group : (r + 1) * group], sides[:, :, r]], axis=1)

    mine = jnp.where(lax.axis_index("space") == 0, edge(grid_rows - 1), edge(0))
    beside = lax.ppermute(mine, "space", SWAP)
    total = tiles * group
    chunk = 1 if grid_rows % 1 == 0 else grid_rows
    dims = (tiles * frames, 2 * grid_rows, 2 * own, width)
    return pl.pallas_call(
        functools.partial(decode_kernel, frames, tiles, grid_rows, own, chunk),
        out_shape=shape(dims, BF16),
        in_specs=[IN_VMEM] * 4,
        out_specs=IN_HBM,
        scratch_shapes=[pltpu.VMEM((grid_rows + 2, total, channels), BF16)] * 3
        + [
            pltpu.VMEM((4, 4 * channels, width), BF16),
            pltpu.VMEM((2, width // HEAD, 2 * chunk * total, HEAD), F32),
            pltpu.VMEM(dims, BF16),
            pltpu.SemaphoreType.DMA((grid_rows // chunk,)),
        ],
        name="decode",
        compiler_params=params(36),
    )(blocks, beside, conv_weight, conv_bias.reshape(1, width))


def solution(mesh):
    assert mesh.shape["space"] == 2
    tiles = mesh.shape["tm"]
    assert tiles & (tiles - 1) == 0
    placed = (P(("groups", "tm"), "space", None, None), P(), P(), P(), P(), P(), P(), P())
    return jax.shard_map(
        body,
        mesh=mesh,
        in_specs=placed,
        out_specs=P("groups", "space", "tm", None),
        check_vma=False,
    )
```

```python
import functools

import jax
import jax.numpy as jnp
from jax import lax
from jax.experimental import pallas as pl
from jax.experimental.pallas import tpu as pltpu
from jax.sharding import PartitionSpec as P


HEAD = 128
EPS = 1e-06
BF16 = jnp.bfloat16
F32 = jnp.float32


IN_HBM = pl.BlockSpec(memory_space=pltpu.HBM)
IN_VMEM = pl.BlockSpec(memory_space=pltpu.VMEM)


def shape(dims, dtype):
    return jax.ShapeDtypeStruct(dims, dtype)


def params(megabytes):
    return pltpu.CompilerParams(vmem_limit_bytes=megabytes << 20)


def in_hbm(x):
    return pltpu.with_memory_space_constraint(x, pltpu.HBM)


def matmul(a, b):
    return jnp.dot(a, b, preferred_element_type=F32)


def features(x):
    return jnp.where(x > 0.0, x + 1.0, jnp.exp(jnp.minimum(x, 0.0)))


def states_kernel(frames, heads, fetched, video_in, wk_hbm, wv_hbm, *refs):
    if fetched:
        parts_out, key, value = refs
        video, wk, wv = video_in, wk_hbm, wv_hbm
        late = []
    else:
        (wq_hbm, parts_out, video, wk_out, wv_out, wq_out, wk, wv, key, value,
         wk_sem, wv_sem, video_sem, late_sem) = refs
        rest = wk_out.shape[1]
        source = pl.ds(heads * HEAD, rest)
        late = [
            pltpu.make_async_copy(wq_hbm, wq_out, late_sem.at[0]),
            pltpu.make_async_copy(wk_hbm.at[:, source], wk_out, late_sem.at[1]),
            pltpu.make_async_copy(wv_hbm.at[:, source], wv_out, late_sem.at[2]),
        ]
    per = video.shape[0] // frames

    def weight_copies(h):
        cols = pl.ds(pl.multiple_of(h * HEAD, HEAD), HEAD)
        return (
            pltpu.make_async_copy(wk_hbm.at[:, cols], wk.at[:, cols], wk_sem.at[h]),
            pltpu.make_async_copy(wv_hbm.at[:, cols], wv.at[:, cols], wv_sem.at[h]),
        )

    def video_copy(f):
        rows = pl.ds(f * per, per)
        return pltpu.make_async_copy(video_in.at[rows], video.at[rows], video_sem.at[f])

    if not fetched:
        soon = min(2, heads)
        for h in range(soon):
            for c in weight_copies(h):
                c.start()
        for f in range(frames):
            video_copy(f).start()
        for f in range(frames):
            video_copy(f).wait()
        for h in range(soon, heads):
            for c in weight_copies(h):
                c.start()
        for c in late:
            c.start()

    def one_head(h, carry):
        if not fetched:
            for c in weight_copies(h):
                c.wait()
        cols = pl.ds(pl.multiple_of(h * HEAD, HEAD), HEAD)
        both = jnp.concatenate([wk[:, cols], wv[:, cols]], axis=1)
        for f in range(frames):
            rows = slice(f * per, (f + 1) * per)
            kv = matmul(video[rows, :], both)
            key[h, rows, :] = features(kv[:, :HEAD]).astype(BF16)
            value[h, rows, :] = kv[:, HEAD:].astype(BF16)
        return carry

    lax.fori_loop(0, heads, one_head, 0)

    for h in range(heads):
        for f in range(frames):
            rows = slice(f * per, (f + 1) * per)
            state = lax.dot_general(
                key[h, rows, :], value[h, rows, :], (((0,), (0,)), ((), ())),
                preferred_element_type=F32,
            )
            parts_out[f, h] = state.astype(BF16)
    for c in late:
        c.wait()


def first_states(video, wk, wv, wq, frames, heads):
    tokens, d = video.shape
    width = heads * HEAD
    return pl.pallas_call(
        functools.partial(states_kernel, frames, heads, False),
        out_shape=[
            shape((frames, heads, HEAD, HEAD), BF16),
            shape((tokens, d), BF16),
            shape((d, d - width), BF16),
            shape((d, d - width), BF16),
            shape((d, d), BF16),
        ],
        in_specs=[IN_HBM] * 4,
        out_specs=[IN_VMEM] * 5,
        scratch_shapes=[
            pltpu.VMEM((d, width), BF16),
            pltpu.VMEM((d, width), BF16),
            pltpu.VMEM((heads, tokens, HEAD), BF16),
            pltpu.VMEM((heads, tokens, HEAD), BF16),
            pltpu.SemaphoreType.DMA((heads,)),
            pltpu.SemaphoreType.DMA((heads,)),
            pltpu.SemaphoreType.DMA((frames,)),
            pltpu.SemaphoreType.DMA((3,)),
        ],
        name="states",
        compiler_params=params(20),
    )(in_hbm(video), in_hbm(wk), in_hbm(wv), in_hbm(wq))


def second_states(video, wk, wv, frames):
    tokens, _ = video.shape
    heads = wk.shape[1] // HEAD
    return pl.pallas_call(
        functools.partial(states_kernel, frames, heads, True),
        out_shape=shape((frames, heads, HEAD, HEAD), BF16),
        in_specs=[IN_VMEM] * 3,
        out_specs=IN_VMEM,
        scratch_shapes=[
            pltpu.VMEM((heads, tokens, HEAD), BF16),
            pltpu.VMEM((heads, tokens, HEAD), BF16),
        ],
        name="states",
        compiler_params=params(20),
    )(video, wk, wv)


def total_call(parts, other_parts):
    frames, heads = parts.shape[:2]
    half = HEAD // 2

    def kernel(parts, other_parts, out, sent):
        low = lax.axis_index("space") == 0
        for h in range(heads):
            total = None
            for f in range(frames):
                one = parts[f, h].astype(F32) + other_parts[f, h].astype(F32)
                total = one if total is None else total + one
            total = jnp.where(low, total[:half], total[half:])
            out[h] = total
            sent[h] = total.astype(BF16)

    dims = (heads, half, HEAD)
    return pl.pallas_call(
        kernel,
        out_shape=[shape(dims, F32), shape(dims, BF16)],
        in_specs=[IN_VMEM] * 2,
        out_specs=[IN_VMEM] * 2,
        name="total",
        compiler_params=params(4),
    )(parts, other_parts)


def query_call(video, w, first, width):
    def kernel(video, w, out):
        out[...] = features(matmul(video[...], w[:, first : first + width])).astype(BF16)

    return pl.pallas_call(
        kernel,
        out_shape=shape((video.shape[0], width), BF16),
        in_specs=[IN_VMEM] * 2,
        out_specs=IN_VMEM,
        name="query",
        compiler_params=params(16),
    )(video, w)


def attend(frames, query, parts, other_parts, carry, other_carry, used, head_out):
    heads = carry.shape[0]
    per = query.shape[0] // frames
    low = lax.axis_index("space") == 0
    used[...] = jnp.zeros_like(used)
    for h in range(heads):
        mine, theirs = carry[h].astype(F32), other_carry[h].astype(F32)
        running = jnp.concatenate(
            [jnp.where(low, mine, theirs), jnp.where(low, theirs, mine)], axis=0
        )
        at = (h % 2) * HEAD
        for f in range(frames):
            running = running + parts[f, h].astype(F32) + other_parts[f, h].astype(F32)
            used[f, h // 2, at : at + HEAD, at : at + HEAD] = running.astype(BF16)
    for f in range(frames):
        rows = slice(f * per, (f + 1) * per)
        for p in range(pl.cdiv(heads, 2)):
            width = min(2, heads - 2 * p) * HEAD
            first = 2 * p * HEAD
            attended = matmul(
                query[rows, first : first + width], used[f, p, :width, :width]
            )
            for h in range(width // HEAD):
                one = attended[:, h * HEAD : (h + 1) * HEAD]
                scale = lax.rsqrt(jnp.mean(one * one, axis=1, keepdims=True) + EPS)
                at = first + h * HEAD
                head_out[rows, at : at + HEAD] = (one * scale).astype(BF16)


def used_shape(frames, heads):
    return pltpu.VMEM((frames, pl.cdiv(heads, 2), 2 * HEAD, 2 * HEAD), BF16)


def partial_call(video, chunk, w_out, frames):
    tokens, d = video.shape
    heads = chunk[3].shape[0]

    def kernel(video, query, parts, other_parts, carry, other_carry, w_out, out,
               used, head_out):
        attend(frames, query, parts, other_parts, carry, other_carry, used, head_out)
        per = tokens // frames
        for f in range(frames):
            rows = slice(f * per, (f + 1) * per)
            out[rows, :] = video[rows, :].astype(F32) + matmul(
                head_out[rows, :], w_out[: heads * HEAD, :]
            )

    return pl.pallas_call(
        kernel,
        out_shape=shape((tokens, d), F32),
        in_specs=[IN_VMEM] * 7,
        out_specs=IN_VMEM,
        scratch_shapes=[used_shape(frames, heads), pltpu.VMEM((tokens, heads * HEAD), BF16)],
        name="partial",
        compiler_params=params(20),
    )(video, *chunk, w_out)


def latent_kernel(
    frames, columns, tiles, partial, query, parts, other_parts, carry, other_carry,
    w_out, w_latent, out, used, head_out, latent,
):
    tokens, d = partial.shape
    per = tokens // frames
    width = head_out.shape[1]
    attend(frames, query, parts, other_parts, carry, other_carry, used, head_out)
    for f in range(frames):
        rows = slice(f * per, (f + 1) * per)
        summed = partial[rows, :] + matmul(head_out[rows, :], w_out[d - width :, :])
        scale = lax.rsqrt(jnp.mean(summed * summed, axis=1, keepdims=True) + EPS)
        latent[rows, :] = matmul(summed.astype(BF16), w_latent[...]) * scale

    own = columns // tiles
    grid_rows = per // columns
    main = grid_rows * frames * own
    for t in range(tiles):
        for r in range(grid_rows):
            block = [
                latent[pl.ds(f * per + r * columns + t * own, own), :] for f in range(frames)
            ]
            at = r * frames * own
            out[t, at : at + frames * own, :] = jnp.concatenate(block, axis=0).astype(BF16)
        sides = []
        for column in (t * own - 1, (t + 1) * own):
            for f in range(frames):
                if 0 <= column < columns:
                    at = f * per + column
                    sides.append(latent[pl.ds(at, grid_rows, stride=columns), :])
                else:
                    sides.append(jnp.zeros((grid_rows, out.shape[2]), F32))
        out[t, main:, :] = jnp.concatenate(sides, axis=0).astype(BF16)


def latent_call(partial, chunk, w_out, w_latent, frames, columns, tiles):
    tokens, _ = partial.shape
    channels = w_latent.shape[1]
    heads = chunk[3].shape[0]
    rows = tokens // columns * (columns // tiles + 2)
    return pl.pallas_call(
        functools.partial(latent_kernel, frames, columns, tiles),
        out_shape=shape((tiles, rows, channels), BF16),
        in_specs=[IN_VMEM] * 8,
        out_specs=IN_VMEM,
        scratch_shapes=[
            used_shape(frames, heads),
            pltpu.VMEM((tokens, heads * HEAD), BF16),
            pltpu.VMEM((tokens, channels), F32),
        ],
        name="latent",
        compiler_params=params(20),
    )(partial, *chunk, w_out, w_latent)


def decode_kernel(
    frames, tiles, grid_rows, own, chunk, blocks, edge, weight, bias,
    out, left, middle, right, taps, wide, staged, sem,
):
    group = frames * own
    main = grid_rows * group
    tile = lax.axis_index("space")
    column = lax.broadcasted_iota(jnp.int32, (group, 1), 0) % own
    channels = weight.shape[2]

    def lay(row, t, body, sides):
        at = slice(t * group, (t + 1) * group)
        first = jnp.concatenate(
            [jnp.broadcast_to(sides[f : f + 1], (own, channels)) for f in range(frames)], axis=0
        )
        last = jnp.concatenate(
            [jnp.broadcast_to(sides[frames + f : frames + f + 1], (own, channels))
             for f in range(frames)], axis=0
        )
        down = pltpu.roll(body, 1, 0)
        up = pltpu.roll(body, group - 1, 0)
        left[row, at, :] = jnp.where(column == 0, first, down).astype(BF16)
        middle[row, at, :] = body.astype(BF16)
        right[row, at, :] = jnp.where(column == own - 1, last, up).astype(BF16)

    for t in range(tiles):
        everything = blocks[t].astype(F32)
        for r in range(grid_rows):
            body = everything[r * group : (r + 1) * group]
            sides = [
                everything[main + s * grid_rows + r : main + s * grid_rows + r + 1]
                for s in range(2 * frames)
            ]
            lay(r + 1, t, body, jnp.concatenate(sides, axis=0))
        beside = edge[t].astype(F32)
        for row, present in ((0, tile == 1), (grid_rows + 1, tile == 0)):
            there = jnp.where(present, beside, 0.0)
            lay(row, t, there[:group], there[group:])

    w = weight[...].astype(F32)
    row_sets = (((0,), (1, 2)), ((0, 1), (2,)))
    for a in range(2):
        for b in range(2):
            for i, rows in enumerate(row_sets[a]):
                for j, cols in enumerate(row_sets[b]):
                    tap = sum(w[r, c] for r in rows for c in cols)
                    at = (2 * i + j) * channels
                    taps[2 * a + b, at : at + channels, :] = (0.5 * tap).astype(BF16)

    views = ((left, middle), (middle, right))
    total = tiles * group
    half_bias = 0.5 * bias[...]
    lanes = wide.shape[-1]
    copies = []
    for i in range(grid_rows // chunk):
        for a in range(2):
            for b in range(2):
                lhs = jnp.concatenate(
                    [v[i * chunk + a + k : i * chunk + a + k + chunk].reshape(
                        chunk * total, channels) for k in range(2) for v in views[b]], axis=1
                )
                h = matmul(lhs, taps[2 * a + b]) + half_bias
                value = h + h * jnp.tanh(h)
                for n in range(wide.shape[1]):
                    wide[a, n, pl.ds(b, chunk * total, stride=2), :] = (
                        value[:, n * lanes : (n + 1) * lanes]
                    )
            for n in range(wide.shape[1]):
                shaped = wide[a, n].reshape(chunk, tiles * frames, 2 * own, lanes)
                for r in range(chunk):
                    staged[:, 2 * (i * chunk + r) + a, :, n * lanes : (n + 1) * lanes] = (
                        shaped[r].astype(BF16)
                    )
        rows = pl.ds(2 * i * chunk, 2 * chunk)
        copies.append(pltpu.make_async_copy(staged.at[:, rows], out.at[:, rows], sem.at[i]))
        copies[-1].start()
    for c in copies:
        c.wait()


def round_call(step, last, got, total, carry):
    def kernel(got, total, *refs):
        upper = (lax.axis_index("tm") // step) % 2 == 1
        received = got[...].astype(F32)
        before = jnp.where(upper, received, 0.0)
        if carry is not None:
            before = refs[0][...] + before
            refs = refs[1:]
        if last:
            refs[0][...] = before.astype(BF16)
        else:
            carry_out, total_out, sent_out = refs
            carry_out[...] = before
            both = total[...] + received
            total_out[...] = both
            sent_out[...] = both.astype(BF16)

    near = [got, total] + ([] if carry is None else [carry])
    kinds = [BF16] if last else [F32, F32, BF16]
    return pl.pallas_call(
        kernel,
        out_shape=[shape(total.shape, kind) for kind in kinds],
        in_specs=[IN_VMEM] * len(near),
        out_specs=[IN_VMEM] * len(kinds),
        name="round",
        compiler_params=params(4),
    )(*near)


def prefix_rounds(total, sent, tiles):
    carry = None
    step, number = 1, 0
    while step < tiles:
        last = 2 * step >= tiles
        got = lax.ppermute(sent, "tm", [(i, i ^ step) for i in range(tiles)])
        out = round_call(step, last, got, total, carry)
        if last:
            return out[0]
        carry, total, sent = out
        step *= 2
        number += 1
    return jnp.zeros_like(sent)


SWAP = [(0, 1), (1, 0)]


def body(video, w_query, w_key, w_value, w_out, w_latent, conv_weight, conv_bias):
    frames, grid_rows, columns, d = video.shape
    tiles = lax.axis_size("tm")
    own = columns // tiles
    flat = video.reshape(-1, d)
    heads = d // HEAD
    split = heads - heads // 2
    parts_a, near, wk_b, wv_b, near_query = first_states(
        flat, w_key, w_value, w_query, frames, split
    )
    other_a = lax.ppermute(parts_a, "space", SWAP)
    parts_b = second_states(near, wk_b, wv_b, frames)
    other_b = lax.ppermute(parts_b, "space", SWAP)

    ready = {}
    for name, first, parts, other in (("a", 0, parts_a, other_a), ("b", split, parts_b, other_b)):
        count = parts.shape[1]
        total, sent = total_call(parts, other)
        query = query_call(near, near_query, first * HEAD, count * HEAD)
        carry = prefix_rounds(total, sent, tiles)
        other_carry = lax.ppermute(carry, "space", SWAP)
        ready[name] = (query, parts, other, carry, other_carry)

    partial = partial_call(near, ready["a"], w_out, frames)
    blocks = latent_call(
        partial, ready["b"], w_out, w_latent, frames, columns, tiles
    )
    blocks = lax.all_to_all(blocks, "tm", 0, 0, tiled=True)
    return decode(blocks, conv_weight, conv_bias, frames, grid_rows, own, tiles)


def decode(blocks, conv_weight, conv_bias, frames, grid_rows, own, tiles):
    channels = conv_weight.shape[2]
    width = conv_weight.shape[3]
    group = frames * own
    main = grid_rows * group
    sides = blocks[:, main:].reshape(tiles, 2 * frames, grid_rows, channels)

    def edge(r):
        return jnp.concatenate([blocks[:, r * group : (r + 1) * group], sides[:, :, r]], axis=1)

    mine = jnp.where(lax.axis_index("space") == 0, edge(grid_rows - 1), edge(0))
    beside = lax.ppermute(mine, "space", SWAP)
    total = tiles * group
    chunk = 1 if grid_rows % 1 == 0 else grid_rows
    dims = (tiles * frames, 2 * grid_rows, 2 * own, width)
    return pl.pallas_call(
        functools.partial(decode_kernel, frames, tiles, grid_rows, own, chunk),
        out_shape=shape(dims, BF16),
        in_specs=[IN_VMEM] * 4,
        out_specs=IN_HBM,
        scratch_shapes=[pltpu.VMEM((grid_rows + 2, total, channels), BF16)] * 3
        + [
            pltpu.VMEM((4, 4 * channels, width), BF16),
            pltpu.VMEM((2, width // HEAD, 2 * chunk * total, HEAD), F32),
            pltpu.VMEM(dims, BF16),
            pltpu.SemaphoreType.DMA((grid_rows // chunk,)),
        ],
        name="decode",
        compiler_params=params(36),
    )(blocks, beside, conv_weight, conv_bias.reshape(1, width))


def solution(mesh):
    assert mesh.shape["space"] == 2
    tiles = mesh.shape["tm"]
    assert tiles & (tiles - 1) == 0
    placed = (P(("groups", "tm"), "space", None, None), P(), P(), P(), P(), P(), P(), P())
    return jax.shard_map(
        body,
        mesh=mesh,
        in_specs=placed,
        out_specs=P("groups", "space", "tm", None),
        check_vma=False,
    )
```

```python
import functools

import jax
import jax.numpy as jnp
from jax import lax
from jax.experimental import pallas as pl
from jax.experimental.pallas import tpu as pltpu
from jax.sharding import PartitionSpec as P


HEAD = 128
EPS = 1e-06
BF16 = jnp.bfloat16
F32 = jnp.float32


IN_HBM = pl.BlockSpec(memory_space=pltpu.HBM)
IN_VMEM = pl.BlockSpec(memory_space=pltpu.VMEM)


def shape(dims, dtype):
    return jax.ShapeDtypeStruct(dims, dtype)


def params(megabytes):
    return pltpu.CompilerParams(vmem_limit_bytes=megabytes << 20)


def in_hbm(x):
    return pltpu.with_memory_space_constraint(x, pltpu.HBM)


def matmul(a, b):
    return jnp.dot(a, b, preferred_element_type=F32)


def features(x):
    return jnp.where(x > 0.0, x + 1.0, jnp.exp(jnp.minimum(x, 0.0)))


def states_kernel(frames, heads, fetched, video_in, wk_hbm, wv_hbm, *refs):
    if fetched:
        parts_out, key, value = refs
        video, wk, wv = video_in, wk_hbm, wv_hbm
        late = []
    else:
        (wq_hbm, parts_out, video, wk_out, wv_out, wq_out, wk, wv, key, value,
         wk_sem, wv_sem, video_sem, late_sem) = refs
        rest = wk_out.shape[1]
        source = pl.ds(heads * HEAD, rest)
        late = [
            pltpu.make_async_copy(wq_hbm, wq_out, late_sem.at[0]),
            pltpu.make_async_copy(wk_hbm.at[:, source], wk_out, late_sem.at[1]),
            pltpu.make_async_copy(wv_hbm.at[:, source], wv_out, late_sem.at[2]),
        ]
    per = video.shape[0] // frames

    def weight_copies(h):
        cols = pl.ds(pl.multiple_of(h * HEAD, HEAD), HEAD)
        return (
            pltpu.make_async_copy(wk_hbm.at[:, cols], wk.at[:, cols], wk_sem.at[h]),
            pltpu.make_async_copy(wv_hbm.at[:, cols], wv.at[:, cols], wv_sem.at[h]),
        )

    def video_copy(f):
        rows = pl.ds(f * per, per)
        return pltpu.make_async_copy(video_in.at[rows], video.at[rows], video_sem.at[f])

    if not fetched:
        soon = min(2, heads)
        for h in range(soon):
            for c in weight_copies(h):
                c.start()
        for f in range(frames):
            video_copy(f).start()
        for f in range(frames):
            video_copy(f).wait()
        for h in range(soon, heads):
            for c in weight_copies(h):
                c.start()
        for c in late:
            c.start()

    def one_head(h, carry):
        if not fetched:
            for c in weight_copies(h):
                c.wait()
        cols = pl.ds(pl.multiple_of(h * HEAD, HEAD), HEAD)
        both = jnp.concatenate([wk[:, cols], wv[:, cols]], axis=1)
        for f in range(frames):
            rows = slice(f * per, (f + 1) * per)
            kv = matmul(video[rows, :], both)
            key[h, rows, :] = features(kv[:, :HEAD]).astype(BF16)
            value[h, rows, :] = kv[:, HEAD:].astype(BF16)
        return carry

    lax.fori_loop(0, heads, one_head, 0)

    for h in range(heads):
        for f in range(frames):
            rows = slice(f * per, (f + 1) * per)
            state = lax.dot_general(
                key[h, rows, :], value[h, rows, :], (((0,), (0,)), ((), ())),
                preferred_element_type=F32,
            )
            parts_out[f, h] = state.astype(BF16)
    for c in late:
        c.wait()


def first_states(video, wk, wv, wq, frames, heads):
    tokens, d = video.shape
    width = heads * HEAD
    return pl.pallas_call(
        functools.partial(states_kernel, frames, heads, False),
        out_shape=[
            shape((frames, heads, HEAD, HEAD), BF16),
            shape((tokens, d), BF16),
            shape((d, d - width), BF16),
            shape((d, d - width), BF16),
            shape((d, d), BF16),
        ],
        in_specs=[IN_HBM] * 4,
        out_specs=[IN_VMEM] * 5,
        scratch_shapes=[
            pltpu.VMEM((d, width), BF16),
            pltpu.VMEM((d, width), BF16),
            pltpu.VMEM((heads, tokens, HEAD), BF16),
            pltpu.VMEM((heads, tokens, HEAD), BF16),
            pltpu.SemaphoreType.DMA((heads,)),
            pltpu.SemaphoreType.DMA((heads,)),
            pltpu.SemaphoreType.DMA((frames,)),
            pltpu.SemaphoreType.DMA((3,)),
        ],
        name="states",
        compiler_params=params(20),
    )(in_hbm(video), in_hbm(wk), in_hbm(wv), in_hbm(wq))


def second_states(video, wk, wv, frames):
    tokens, _ = video.shape
    heads = wk.shape[1] // HEAD
    return pl.pallas_call(
        functools.partial(states_kernel, frames, heads, True),
        out_shape=shape((frames, heads, HEAD, HEAD), BF16),
        in_specs=[IN_VMEM] * 3,
        out_specs=IN_VMEM,
        scratch_shapes=[
            pltpu.VMEM((heads, tokens, HEAD), BF16),
            pltpu.VMEM((heads, tokens, HEAD), BF16),
        ],
        name="states",
        compiler_params=params(20),
    )(video, wk, wv)


def total_call(parts, other_parts):
    frames, heads = parts.shape[:2]
    half = HEAD // 2

    def kernel(parts, other_parts, out, sent):
        low = lax.axis_index("space") == 0
        for h in range(heads):
            total = None
            for f in range(frames):
                one = parts[f, h].astype(F32) + other_parts[f, h].astype(F32)
                total = one if total is None else total + one
            total = jnp.where(low, total[:half], total[half:])
            out[h] = total
            sent[h] = total.astype(BF16)

    dims = (heads, half, HEAD)
    return pl.pallas_call(
        kernel,
        out_shape=[shape(dims, F32), shape(dims, BF16)],
        in_specs=[IN_VMEM] * 2,
        out_specs=[IN_VMEM] * 2,
        name="total",
        compiler_params=params(4),
    )(parts, other_parts)


def query_call(video, w, first, width):
    def kernel(video, w, out):
        out[...] = features(matmul(video[...], w[:, first : first + width])).astype(BF16)

    return pl.pallas_call(
        kernel,
        out_shape=shape((video.shape[0], width), BF16),
        in_specs=[IN_VMEM] * 2,
        out_specs=IN_VMEM,
        name="query",
        compiler_params=params(16),
    )(video, w)


def attend(frames, queries, parts, other_parts, carry, other_carry, used, head_out):
    heads = carry.shape[0]
    per = head_out.shape[0] // frames
    low = lax.axis_index("space") == 0
    used[...] = jnp.zeros_like(used)
    for h in range(heads):
        mine, theirs = carry[h].astype(F32), other_carry[h].astype(F32)
        running = jnp.concatenate(
            [jnp.where(low, mine, theirs), jnp.where(low, theirs, mine)], axis=0
        )
        at = (h % 2) * HEAD
        for f in range(frames):
            running = running + parts[f, h].astype(F32) + other_parts[f, h].astype(F32)
            used[f, h // 2, at : at + HEAD, at : at + HEAD] = running.astype(BF16)
    for f in range(frames):
        rows = slice(f * per, (f + 1) * per)
        for p in range(pl.cdiv(heads, 2)):
            width = min(2, heads - 2 * p) * HEAD
            first = 2 * p * HEAD
            query, at = queries[0], first
            for piece in queries[1:]:
                if at < query.shape[1]:
                    break
                query, at = piece, at - query.shape[1]
            attended = matmul(query[rows, at : at + width], used[f, p, :width, :width])
            for h in range(width // HEAD):
                one = attended[:, h * HEAD : (h + 1) * HEAD]
                scale = lax.rsqrt(jnp.mean(one * one, axis=1, keepdims=True) + EPS)
                at = first + h * HEAD
                head_out[rows, at : at + HEAD] = (one * scale).astype(BF16)


def used_shape(frames, heads):
    return pltpu.VMEM((frames, pl.cdiv(heads, 2), 2 * HEAD, 2 * HEAD), BF16)


def partial_call(video, chunk, w_out, frames):
    tokens, d = video.shape
    heads = chunk[3].shape[0]

    queries, chunk = chunk[0], chunk[1:]
    n = len(queries)

    def kernel(video, *refs):
        parts, other_parts, carry, other_carry, w_out, out, used, head_out = refs[n:]
        attend(frames, refs[:n], parts, other_parts, carry, other_carry, used, head_out)
        per = tokens // frames
        for f in range(frames):
            rows = slice(f * per, (f + 1) * per)
            out[rows, :] = video[rows, :].astype(F32) + matmul(
                head_out[rows, :], w_out[: heads * HEAD, :]
            )

    return pl.pallas_call(
        kernel,
        out_shape=shape((tokens, d), F32),
        in_specs=[IN_VMEM] * (n + 6),
        out_specs=IN_VMEM,
        scratch_shapes=[used_shape(frames, heads), pltpu.VMEM((tokens, heads * HEAD), BF16)],
        name="partial",
        compiler_params=params(20),
    )(video, *queries, *chunk, w_out)


def latent_kernel(
    frames, columns, tiles, partial, query, parts, other_parts, carry, other_carry,
    w_out, w_latent, out, used, head_out, latent,
):
    tokens, d = partial.shape
    per = tokens // frames
    width = head_out.shape[1]
    attend(frames, [query], parts, other_parts, carry, other_carry, used, head_out)
    for f in range(frames):
        rows = slice(f * per, (f + 1) * per)
        summed = partial[rows, :] + matmul(head_out[rows, :], w_out[d - width :, :])
        scale = lax.rsqrt(jnp.mean(summed * summed, axis=1, keepdims=True) + EPS)
        latent[rows, :] = matmul(summed.astype(BF16), w_latent[...]) * scale

    own = columns // tiles
    grid_rows = per // columns
    main = grid_rows * frames * own
    for t in range(tiles):
        for r in range(grid_rows):
            block = [
                latent[pl.ds(f * per + r * columns + t * own, own), :] for f in range(frames)
            ]
            at = r * frames * own
            out[t, at : at + frames * own, :] = jnp.concatenate(block, axis=0).astype(BF16)
        sides = []
        for column in (t * own - 1, (t + 1) * own):
            for f in range(frames):
                if 0 <= column < columns:
                    at = f * per + column
                    sides.append(latent[pl.ds(at, grid_rows, stride=columns), :])
                else:
                    sides.append(jnp.zeros((grid_rows, out.shape[2]), F32))
        out[t, main:, :] = jnp.concatenate(sides, axis=0).astype(BF16)


def latent_call(partial, chunk, w_out, w_latent, frames, columns, tiles):
    tokens, _ = partial.shape
    channels = w_latent.shape[1]
    heads = chunk[3].shape[0]
    rows = tokens // columns * (columns // tiles + 2)
    return pl.pallas_call(
        functools.partial(latent_kernel, frames, columns, tiles),
        out_shape=shape((tiles, rows, channels), BF16),
        in_specs=[IN_VMEM] * 8,
        out_specs=IN_VMEM,
        scratch_shapes=[
            used_shape(frames, heads),
            pltpu.VMEM((tokens, heads * HEAD), BF16),
            pltpu.VMEM((tokens, channels), F32),
        ],
        name="latent",
        compiler_params=params(20),
    )(partial, *chunk[0], *chunk[1:], w_out, w_latent)


def decode_kernel(
    frames, tiles, grid_rows, own, chunk, blocks, edge, weight, bias,
    out, left, middle, right, taps, wide, staged, sem,
):
    group = frames * own
    main = grid_rows * group
    tile = lax.axis_index("space")
    column = lax.broadcasted_iota(jnp.int32, (group, 1), 0) % own
    channels = weight.shape[2]

    def lay(row, t, body, sides):
        at = slice(t * group, (t + 1) * group)
        first = jnp.concatenate(
            [jnp.broadcast_to(sides[f : f + 1], (own, channels)) for f in range(frames)], axis=0
        )
        last = jnp.concatenate(
            [jnp.broadcast_to(sides[frames + f : frames + f + 1], (own, channels))
             for f in range(frames)], axis=0
        )
        down = pltpu.roll(body, 1, 0)
        up = pltpu.roll(body, group - 1, 0)
        left[row, at, :] = jnp.where(column == 0, first, down).astype(BF16)
        middle[row, at, :] = body.astype(BF16)
        right[row, at, :] = jnp.where(column == own - 1, last, up).astype(BF16)

    for t in range(tiles):
        everything = blocks[t].astype(F32)
        for r in range(grid_rows):
            body = everything[r * group : (r + 1) * group]
            sides = [
                everything[main + s * grid_rows + r : main + s * grid_rows + r + 1]
                for s in range(2 * frames)
            ]
            lay(r + 1, t, body, jnp.concatenate(sides, axis=0))
        beside = edge[t].astype(F32)
        for row, present in ((0, tile == 1), (grid_rows + 1, tile == 0)):
            there = jnp.where(present, beside, 0.0)
            lay(row, t, there[:group], there[group:])

    w = weight[...].astype(F32)
    row_sets = (((0,), (1, 2)), ((0, 1), (2,)))
    for a in range(2):
        for b in range(2):
            for i, rows in enumerate(row_sets[a]):
                for j, cols in enumerate(row_sets[b]):
                    tap = sum(w[r, c] for r in rows for c in cols)
                    at = (2 * i + j) * channels
                    taps[2 * a + b, at : at + channels, :] = (0.5 * tap).astype(BF16)

    views = ((left, middle), (middle, right))
    total = tiles * group
    half_bias = 0.5 * bias[...]
    lanes = wide.shape[-1]
    copies = []
    for i in range(grid_rows // chunk):
        for a in range(2):
            for b in range(2):
                lhs = jnp.concatenate(
                    [v[i * chunk + a + k : i * chunk + a + k + chunk].reshape(
                        chunk * total, channels) for k in range(2) for v in views[b]], axis=1
                )
                h = matmul(lhs, taps[2 * a + b]) + half_bias
                value = h + h * jnp.tanh(h)
                for n in range(wide.shape[1]):
                    wide[a, n, pl.ds(b, chunk * total, stride=2), :] = (
                        value[:, n * lanes : (n + 1) * lanes]
                    )
            for n in range(wide.shape[1]):
                shaped = wide[a, n].reshape(chunk, tiles * frames, 2 * own, lanes)
                for r in range(chunk):
                    staged[:, 2 * (i * chunk + r) + a, :, n * lanes : (n + 1) * lanes] = (
                        shaped[r].astype(BF16)
                    )
        rows = pl.ds(2 * i * chunk, 2 * chunk)
        copies.append(pltpu.make_async_copy(staged.at[:, rows], out.at[:, rows], sem.at[i]))
        copies[-1].start()
    for c in copies:
        c.wait()


def round_call(step, last, got, total, carry):
    def kernel(got, total, *refs):
        upper = (lax.axis_index("tm") // step) % 2 == 1
        received = got[...].astype(F32)
        before = jnp.where(upper, received, 0.0)
        if carry is not None:
            before = refs[0][...] + before
            refs = refs[1:]
        if last:
            refs[0][...] = before.astype(BF16)
        else:
            carry_out, total_out, sent_out = refs
            carry_out[...] = before
            both = total[...] + received
            total_out[...] = both
            sent_out[...] = both.astype(BF16)

    near = [got, total] + ([] if carry is None else [carry])
    kinds = [BF16] if last else [F32, F32, BF16]
    return pl.pallas_call(
        kernel,
        out_shape=[shape(total.shape, kind) for kind in kinds],
        in_specs=[IN_VMEM] * len(near),
        out_specs=[IN_VMEM] * len(kinds),
        name="round",
        compiler_params=params(4),
    )(*near)


def prefix_rounds(total, sent, tiles):
    carry = None
    step, number = 1, 0
    while step < tiles:
        last = 2 * step >= tiles
        got = lax.ppermute(sent, "tm", [(i, i ^ step) for i in range(tiles)])
        out = round_call(step, last, got, total, carry)
        if last:
            return out[0]
        carry, total, sent = out
        step *= 2
        number += 1
    return jnp.zeros_like(sent)


SWAP = [(0, 1), (1, 0)]


def body(video, w_query, w_key, w_value, w_out, w_latent, conv_weight, conv_bias):
    frames, grid_rows, columns, d = video.shape
    tiles = lax.axis_size("tm")
    own = columns // tiles
    flat = video.reshape(-1, d)
    heads = d // HEAD
    split = heads - heads // 2
    parts_a, near, wk_b, wv_b, near_query = first_states(
        flat, w_key, w_value, w_query, frames, split
    )
    other_a = lax.ppermute(parts_a, "space", SWAP)
    parts_b = second_states(near, wk_b, wv_b, frames)
    other_b = lax.ppermute(parts_b, "space", SWAP)

    ready = {}
    for name, first, parts, other in (("a", 0, parts_a, other_a), ("b", split, parts_b, other_b)):
        count = parts.shape[1]
        total, sent = total_call(parts, other)
        cuts = [first, first + 2, first + count] if name == "a" else [first, first + count]
        queries = []
        for low, high in zip(cuts, cuts[1:]):
            queries.append(
                query_call(near, near_query, low * HEAD, (high - low) * HEAD)
            )
        carry = prefix_rounds(total, sent, tiles)
        other_carry = lax.ppermute(carry, "space", SWAP)
        ready[name] = (queries, parts, other, carry, other_carry)

    partial = partial_call(near, ready["a"], w_out, frames)
    blocks = latent_call(
        partial, ready["b"], w_out, w_latent, frames, columns, tiles
    )
    blocks = lax.all_to_all(blocks, "tm", 0, 0, tiled=True)
    return decode(blocks, conv_weight, conv_bias, frames, grid_rows, own, tiles)


def decode(blocks, conv_weight, conv_bias, frames, grid_rows, own, tiles):
    channels = conv_weight.shape[2]
    width = conv_weight.shape[3]
    group = frames * own
    main = grid_rows * group
    sides = blocks[:, main:].reshape(tiles, 2 * frames, grid_rows, channels)

    def edge(r):
        return jnp.concatenate([blocks[:, r * group : (r + 1) * group], sides[:, :, r]], axis=1)

    mine = jnp.where(lax.axis_index("space") == 0, edge(grid_rows - 1), edge(0))
    beside = lax.ppermute(mine, "space", SWAP)
    total = tiles * group
    chunk = 1 if grid_rows % 1 == 0 else grid_rows
    dims = (tiles * frames, 2 * grid_rows, 2 * own, width)
    return pl.pallas_call(
        functools.partial(decode_kernel, frames, tiles, grid_rows, own, chunk),
        out_shape=shape(dims, BF16),
        in_specs=[IN_VMEM] * 4,
        out_specs=IN_HBM,
        scratch_shapes=[pltpu.VMEM((grid_rows + 2, total, channels), BF16)] * 3
        + [
            pltpu.VMEM((4, 4 * channels, width), BF16),
            pltpu.VMEM((2, width // HEAD, 2 * chunk * total, HEAD), F32),
            pltpu.VMEM(dims, BF16),
            pltpu.SemaphoreType.DMA((grid_rows // chunk,)),
        ],
        name="decode",
        compiler_params=params(36),
    )(blocks, beside, conv_weight, conv_bias.reshape(1, width))


def solution(mesh):
    assert mesh.shape["space"] == 2
    tiles = mesh.shape["tm"]
    assert tiles & (tiles - 1) == 0
    placed = (P(("groups", "tm"), "space", None, None), P(), P(), P(), P(), P(), P(), P())
    return jax.shard_map(
        body,
        mesh=mesh,
        in_specs=placed,
        out_specs=P("groups", "space", "tm", None),
        check_vma=False,
    )
```

```python
import functools

import jax
import jax.numpy as jnp
from jax import lax
from jax.experimental import pallas as pl
from jax.experimental.pallas import tpu as pltpu
from jax.sharding import PartitionSpec as P


HEAD = 128
EPS = 1e-06
BF16 = jnp.bfloat16
F32 = jnp.float32


IN_HBM = pl.BlockSpec(memory_space=pltpu.HBM)
IN_VMEM = pl.BlockSpec(memory_space=pltpu.VMEM)


def shape(dims, dtype):
    return jax.ShapeDtypeStruct(dims, dtype)


def params(megabytes):
    return pltpu.CompilerParams(vmem_limit_bytes=megabytes << 20)


def in_hbm(x):
    return pltpu.with_memory_space_constraint(x, pltpu.HBM)


def matmul(a, b):
    return jnp.dot(a, b, preferred_element_type=F32)


def features(x):
    return jnp.where(x > 0.0, x + 1.0, jnp.exp(jnp.minimum(x, 0.0)))


def states_kernel(frames, heads, fetched, video_in, wk_hbm, wv_hbm, *refs):
    if fetched:
        parts_out, key, value = refs
        video, wk, wv = video_in, wk_hbm, wv_hbm
        late = []
    else:
        (wq_hbm, parts_out, video, wk_out, wv_out, wq_out, wk, wv, key, value,
         wk_sem, wv_sem, video_sem, late_sem) = refs
        rest = wk_out.shape[1]
        source = pl.ds(heads * HEAD, rest)
        late = [
            pltpu.make_async_copy(wq_hbm, wq_out, late_sem.at[0]),
            pltpu.make_async_copy(wk_hbm.at[:, source], wk_out, late_sem.at[1]),
            pltpu.make_async_copy(wv_hbm.at[:, source], wv_out, late_sem.at[2]),
        ]
    per = video.shape[0] // frames

    def weight_copies(h):
        cols = pl.ds(pl.multiple_of(h * HEAD, HEAD), HEAD)
        return (
            pltpu.make_async_copy(wk_hbm.at[:, cols], wk.at[:, cols], wk_sem.at[h]),
            pltpu.make_async_copy(wv_hbm.at[:, cols], wv.at[:, cols], wv_sem.at[h]),
        )

    def video_copy(f):
        rows = pl.ds(f * per, per)
        return pltpu.make_async_copy(video_in.at[rows], video.at[rows], video_sem.at[f])

    if not fetched:
        soon = min(2, heads)
        for h in range(soon):
            for c in weight_copies(h):
                c.start()
        for f in range(frames):
            video_copy(f).start()
        for f in range(frames):
            video_copy(f).wait()
        for h in range(soon, heads):
            for c in weight_copies(h):
                c.start()
        for c in late:
            c.start()

    def one_head(h, carry):
        if not fetched:
            for c in weight_copies(h):
                c.wait()
        cols = pl.ds(pl.multiple_of(h * HEAD, HEAD), HEAD)
        both = jnp.concatenate([wk[:, cols], wv[:, cols]], axis=1)
        for f in range(frames):
            rows = slice(f * per, (f + 1) * per)
            kv = matmul(video[rows, :], both)
            key[h, rows, :] = features(kv[:, :HEAD]).astype(BF16)
            value[h, rows, :] = kv[:, HEAD:].astype(BF16)
        return carry

    lax.fori_loop(0, heads, one_head, 0)

    for h in range(heads):
        for f in range(frames):
            rows = slice(f * per, (f + 1) * per)
            state = lax.dot_general(
                key[h, rows, :], value[h, rows, :], (((0,), (0,)), ((), ())),
                preferred_element_type=F32,
            )
            parts_out[f, h] = state.astype(BF16)
    for c in late:
        c.wait()


def first_states(video, wk, wv, wq, frames, heads):
    tokens, d = video.shape
    width = heads * HEAD
    return pl.pallas_call(
        functools.partial(states_kernel, frames, heads, False),
        out_shape=[
            shape((frames, heads, HEAD, HEAD), BF16),
            shape((tokens, d), BF16),
            shape((d, d - width), BF16),
            shape((d, d - width), BF16),
            shape((d, d), BF16),
        ],
        in_specs=[IN_HBM] * 4,
        out_specs=[IN_VMEM] * 5,
        scratch_shapes=[
            pltpu.VMEM((d, width), BF16),
            pltpu.VMEM((d, width), BF16),
            pltpu.VMEM((heads, tokens, HEAD), BF16),
            pltpu.VMEM((heads, tokens, HEAD), BF16),
            pltpu.SemaphoreType.DMA((heads,)),
            pltpu.SemaphoreType.DMA((heads,)),
            pltpu.SemaphoreType.DMA((frames,)),
            pltpu.SemaphoreType.DMA((3,)),
        ],
        name="states",
        compiler_params=params(20),
    )(in_hbm(video), in_hbm(wk), in_hbm(wv), in_hbm(wq))


def second_states(video, wk, wv, frames):
    tokens, _ = video.shape
    heads = wk.shape[1] // HEAD
    return pl.pallas_call(
        functools.partial(states_kernel, frames, heads, True),
        out_shape=shape((frames, heads, HEAD, HEAD), BF16),
        in_specs=[IN_VMEM] * 3,
        out_specs=IN_VMEM,
        scratch_shapes=[
            pltpu.VMEM((heads, tokens, HEAD), BF16),
            pltpu.VMEM((heads, tokens, HEAD), BF16),
        ],
        name="states",
        compiler_params=params(20),
    )(video, wk, wv)


def total_call(parts, other_parts):
    frames, heads = parts.shape[:2]
    half = HEAD // 2

    def kernel(parts, other_parts, out, sent):
        low = lax.axis_index("space") == 0
        for h in range(heads):
            total = None
            for f in range(frames):
                one = parts[f, h].astype(F32) + other_parts[f, h].astype(F32)
                total = one if total is None else total + one
            total = jnp.where(low, total[:half], total[half:])
            out[h] = total
            sent[h] = total.astype(BF16)

    dims = (heads, half, HEAD)
    return pl.pallas_call(
        kernel,
        out_shape=[shape(dims, F32), shape(dims, BF16)],
        in_specs=[IN_VMEM] * 2,
        out_specs=[IN_VMEM] * 2,
        name="total",
        compiler_params=params(4),
    )(parts, other_parts)


def query_call(video, w, first, width):
    def kernel(video, w, out):
        out[...] = features(matmul(video[...], w[:, first : first + width])).astype(BF16)

    return pl.pallas_call(
        kernel,
        out_shape=shape((video.shape[0], width), BF16),
        in_specs=[IN_VMEM] * 2,
        out_specs=IN_VMEM,
        name="query",
        compiler_params=params(16),
    )(video, w)


def attend(frames, queries, parts, other_parts, carry, other_carry, used, head_out):
    heads = carry.shape[0]
    per = head_out.shape[0] // frames
    low = lax.axis_index("space") == 0
    used[...] = jnp.zeros_like(used)
    for h in range(heads):
        mine, theirs = carry[h].astype(F32), other_carry[h].astype(F32)
        running = jnp.concatenate(
            [jnp.where(low, mine, theirs), jnp.where(low, theirs, mine)], axis=0
        )
        at = (h % 2) * HEAD
        for f in range(frames):
            running = running + parts[f, h].astype(F32) + other_parts[f, h].astype(F32)
            used[f, h // 2, at : at + HEAD, at : at + HEAD] = running.astype(BF16)
    for f in range(frames):
        rows = slice(f * per, (f + 1) * per)
        for p in range(pl.cdiv(heads, 2)):
            width = min(2, heads - 2 * p) * HEAD
            first = 2 * p * HEAD
            query, at = queries[0], first
            for piece in queries[1:]:
                if at < query.shape[1]:
                    break
                query, at = piece, at - query.shape[1]
            attended = matmul(query[rows, at : at + width], used[f, p, :width, :width])
            for h in range(width // HEAD):
                one = attended[:, h * HEAD : (h + 1) * HEAD]
                scale = lax.rsqrt(jnp.mean(one * one, axis=1, keepdims=True) + EPS)
                at = first + h * HEAD
                head_out[rows, at : at + HEAD] = (one * scale).astype(BF16)


def used_shape(frames, heads):
    return pltpu.VMEM((frames, pl.cdiv(heads, 2), 2 * HEAD, 2 * HEAD), BF16)


def partial_call(video, chunk, w_out, frames):
    tokens, d = video.shape
    heads = chunk[3].shape[0]

    queries, chunk = chunk[0], chunk[1:]
    n = len(queries)

    def kernel(video, *refs):
        parts, other_parts, carry, other_carry, w_out, out, used, head_out = refs[n:]
        attend(frames, refs[:n], parts, other_parts, carry, other_carry, used, head_out)
        per = tokens // frames
        for f in range(frames):
            rows = slice(f * per, (f + 1) * per)
            out[rows, :] = video[rows, :].astype(F32) + matmul(
                head_out[rows, :], w_out[: heads * HEAD, :]
            )

    return pl.pallas_call(
        kernel,
        out_shape=shape((tokens, d), F32),
        in_specs=[IN_VMEM] * (n + 6),
        out_specs=IN_VMEM,
        scratch_shapes=[used_shape(frames, heads), pltpu.VMEM((tokens, heads * HEAD), BF16)],
        name="partial",
        compiler_params=params(20),
    )(video, *queries, *chunk, w_out)


def latent_kernel(
    frames, columns, tiles, partial, query, parts, other_parts, carry, other_carry,
    w_out, w_latent, out, used, head_out, latent,
):
    tokens, d = partial.shape
    per = tokens // frames
    width = head_out.shape[1]
    attend(frames, [query], parts, other_parts, carry, other_carry, used, head_out)
    for f in range(frames):
        rows = slice(f * per, (f + 1) * per)
        summed = partial[rows, :] + matmul(head_out[rows, :], w_out[d - width :, :])
        scale = lax.rsqrt(jnp.mean(summed * summed, axis=1, keepdims=True) + EPS)
        latent[rows, :] = matmul(summed.astype(BF16), w_latent[...]) * scale

    own = columns // tiles
    grid_rows = per // columns
    main = grid_rows * frames * own
    for t in range(tiles):
        for r in range(grid_rows):
            block = [
                latent[pl.ds(f * per + r * columns + t * own, own), :] for f in range(frames)
            ]
            at = r * frames * own
            out[t, at : at + frames * own, :] = jnp.concatenate(block, axis=0).astype(BF16)
        sides = []
        for column in (t * own - 1, (t + 1) * own):
            for f in range(frames):
                if 0 <= column < columns:
                    at = f * per + column
                    sides.append(latent[pl.ds(at, grid_rows, stride=columns), :])
                else:
                    sides.append(jnp.zeros((grid_rows, out.shape[2]), F32))
        out[t, main:, :] = jnp.concatenate(sides, axis=0).astype(BF16)


def latent_call(partial, chunk, w_out, w_latent, frames, columns, tiles):
    tokens, _ = partial.shape
    channels = w_latent.shape[1]
    heads = chunk[3].shape[0]
    rows = tokens // columns * (columns // tiles + 2)
    return pl.pallas_call(
        functools.partial(latent_kernel, frames, columns, tiles),
        out_shape=shape((tiles, rows, channels), BF16),
        in_specs=[IN_VMEM] * 8,
        out_specs=IN_VMEM,
        scratch_shapes=[
            used_shape(frames, heads),
            pltpu.VMEM((tokens, heads * HEAD), BF16),
            pltpu.VMEM((tokens, channels), F32),
        ],
        name="latent",
        compiler_params=params(20),
    )(partial, *chunk[0], *chunk[1:], w_out, w_latent)


def decode_kernel(
    frames, tiles, grid_rows, own, chunk, blocks, edge, weight, bias,
    out, left, middle, right, taps, wide, staged, sem,
):
    group = frames * own
    main = grid_rows * group
    tile = lax.axis_index("space")
    column = lax.broadcasted_iota(jnp.int32, (group, 1), 0) % own
    channels = weight.shape[2]

    def lay(row, t, body, sides):
        at = slice(t * group, (t + 1) * group)
        first = jnp.concatenate(
            [jnp.broadcast_to(sides[f : f + 1], (own, channels)) for f in range(frames)], axis=0
        )
        last = jnp.concatenate(
            [jnp.broadcast_to(sides[frames + f : frames + f + 1], (own, channels))
             for f in range(frames)], axis=0
        )
        down = pltpu.roll(body, 1, 0)
        up = pltpu.roll(body, group - 1, 0)
        left[row, at, :] = jnp.where(column == 0, first, down).astype(BF16)
        middle[row, at, :] = body.astype(BF16)
        right[row, at, :] = jnp.where(column == own - 1, last, up).astype(BF16)

    for t in range(tiles):
        everything = blocks[t].astype(F32)
        for r in range(grid_rows):
            body = everything[r * group : (r + 1) * group]
            sides = [
                everything[main + s * grid_rows + r : main + s * grid_rows + r + 1]
                for s in range(2 * frames)
            ]
            lay(r + 1, t, body, jnp.concatenate(sides, axis=0))
        beside = edge[t].astype(F32)
        for row, present in ((0, tile == 1), (grid_rows + 1, tile == 0)):
            there = jnp.where(present, beside, 0.0)
            lay(row, t, there[:group], there[group:])

    w = weight[...].astype(F32)
    row_sets = (((0,), (1, 2)), ((0, 1), (2,)))
    for a in range(2):
        for b in range(2):
            for i, rows in enumerate(row_sets[a]):
                for j, cols in enumerate(row_sets[b]):
                    tap = sum(w[r, c] for r in rows for c in cols)
                    at = (2 * i + j) * channels
                    taps[2 * a + b, at : at + channels, :] = (0.5 * tap).astype(BF16)

    views = ((left, middle), (middle, right))
    total = tiles * group
    half_bias = 0.5 * bias[...]
    lanes = wide.shape[-1]
    copies = []
    for i in range(grid_rows // chunk):
        for a in range(2):
            for b in range(2):
                lhs = jnp.concatenate(
                    [v[i * chunk + a + k : i * chunk + a + k + chunk].reshape(
                        chunk * total, channels) for k in range(2) for v in views[b]], axis=1
                )
                h = matmul(lhs, taps[2 * a + b]) + half_bias
                value = h + h * jnp.tanh(h)
                for n in range(wide.shape[1]):
                    wide[a, n, pl.ds(b, chunk * total, stride=2), :] = (
                        value[:, n * lanes : (n + 1) * lanes]
                    )
            for n in range(wide.shape[1]):
                shaped = wide[a, n].reshape(chunk, tiles * frames, 2 * own, lanes)
                for r in range(chunk):
                    staged[:, 2 * (i * chunk + r) + a, :, n * lanes : (n + 1) * lanes] = (
                        shaped[r].astype(BF16)
                    )
        rows = pl.ds(2 * i * chunk, 2 * chunk)
        copies.append(pltpu.make_async_copy(staged.at[:, rows], out.at[:, rows], sem.at[i]))
        copies[-1].start()
    for c in copies:
        c.wait()


def round_call(step, last, got, total, carry):
    def kernel(got, total, *refs):
        upper = (lax.axis_index("tm") // step) % 2 == 1
        received = got[...].astype(F32)
        before = jnp.where(upper, received, 0.0)
        if carry is not None:
            before = refs[0][...] + before
            refs = refs[1:]
        if last:
            refs[0][...] = before.astype(BF16)
        else:
            carry_out, total_out, sent_out = refs
            carry_out[...] = before
            both = total[...] + received
            total_out[...] = both
            sent_out[...] = both.astype(BF16)

    near = [got, total] + ([] if carry is None else [carry])
    kinds = [BF16] if last else [F32, F32, BF16]
    return pl.pallas_call(
        kernel,
        out_shape=[shape(total.shape, kind) for kind in kinds],
        in_specs=[IN_VMEM] * len(near),
        out_specs=[IN_VMEM] * len(kinds),
        name="round",
        compiler_params=params(4),
    )(*near)


def prefix_rounds(total, sent, tiles):
    carry = None
    step, number = 1, 0
    while step < tiles:
        last = 2 * step >= tiles
        got = lax.ppermute(sent, "tm", [(i, i ^ step) for i in range(tiles)])
        out = round_call(step, last, got, total, carry)
        if last:
            return out[0]
        carry, total, sent = out
        step *= 2
        number += 1
    return jnp.zeros_like(sent)


SWAP = [(0, 1), (1, 0)]


def body(video, w_query, w_key, w_value, w_out, w_latent, conv_weight, conv_bias):
    frames, grid_rows, columns, d = video.shape
    tiles = lax.axis_size("tm")
    own = columns // tiles
    flat = video.reshape(-1, d)
    heads = d // HEAD
    split = heads - heads // 2
    parts_a, near, wk_b, wv_b, near_query = first_states(
        flat, w_key, w_value, w_query, frames, split
    )
    other_a = lax.ppermute(parts_a, "space", SWAP)
    parts_b = second_states(near, wk_b, wv_b, frames)
    other_b = lax.ppermute(parts_b, "space", SWAP)

    ready = {}
    for name, first, parts, other in (("a", 0, parts_a, other_a), ("b", split, parts_b, other_b)):
        count = parts.shape[1]
        total, sent = total_call(parts, other)
        cuts = [first, first + 2, first + count] if name == "a" else [first, first + count]
        queries = []
        for low, high in zip(cuts, cuts[1:]):
            queries.append(
                query_call(near, near_query, low * HEAD, (high - low) * HEAD)
            )
        carry = prefix_rounds(total, sent, tiles)
        other_carry = lax.ppermute(carry, "space", SWAP)
        ready[name] = (queries, parts, other, carry, other_carry)

    partial = partial_call(near, ready["a"], w_out, frames)
    blocks = latent_call(
        partial, ready["b"], w_out, w_latent, frames, columns, tiles
    )
    blocks = lax.all_to_all(blocks, "tm", 0, 0, tiled=True)
    return decode(blocks, conv_weight, conv_bias, frames, grid_rows, own, tiles)


def decode(blocks, conv_weight, conv_bias, frames, grid_rows, own, tiles):
    channels = conv_weight.shape[2]
    width = conv_weight.shape[3]
    group = frames * own
    main = grid_rows * group

    def edge_kernel(blocks, out):
        def take(r):
            for t in range(tiles):
                out[t, :group] = blocks[t, r * group : (r + 1) * group]
                sides = blocks[t, main:].astype(F32)
                out[t, group:] = jnp.concatenate(
                    [sides[k * grid_rows + r : k * grid_rows + r + 1] for k in range(2 * frames)],
                    axis=0,
                ).astype(BF16)

        upper = lax.axis_index("space") == 0

        @pl.when(upper)
        def _():
            take(grid_rows - 1)

        @pl.when(jnp.logical_not(upper))
        def _():
            take(0)

    mine = pl.pallas_call(
        edge_kernel,
        out_shape=shape((tiles, group + 2 * frames, channels), BF16),
        in_specs=[IN_VMEM],
        out_specs=IN_VMEM,
        name="edge",
        compiler_params=params(4),
    )(blocks)
    beside = lax.ppermute(mine, "space", SWAP)
    total = tiles * group
    chunk = 1 if grid_rows % 1 == 0 else grid_rows
    dims = (tiles * frames, 2 * grid_rows, 2 * own, width)
    return pl.pallas_call(
        functools.partial(decode_kernel, frames, tiles, grid_rows, own, chunk),
        out_shape=shape(dims, BF16),
        in_specs=[IN_VMEM] * 4,
        out_specs=IN_HBM,
        scratch_shapes=[pltpu.VMEM((grid_rows + 2, total, channels), BF16)] * 3
        + [
            pltpu.VMEM((4, 4 * channels, width), BF16),
            pltpu.VMEM((2, width // HEAD, 2 * chunk * total, HEAD), F32),
            pltpu.VMEM(dims, BF16),
            pltpu.SemaphoreType.DMA((grid_rows // chunk,)),
        ],
        name="decode",
        compiler_params=params(36),
    )(blocks, beside, conv_weight, conv_bias.reshape(1, width))


def solution(mesh):
    assert mesh.shape["space"] == 2
    tiles = mesh.shape["tm"]
    assert tiles & (tiles - 1) == 0
    placed = (P(("groups", "tm"), "space", None, None), P(), P(), P(), P(), P(), P(), P())
    return jax.shard_map(
        body,
        mesh=mesh,
        in_specs=placed,
        out_specs=P("groups", "space", "tm", None),
        check_vma=False,
    )
```

```python
import functools

import jax
import jax.numpy as jnp
from jax import lax
from jax.experimental import pallas as pl
from jax.experimental.pallas import tpu as pltpu
from jax.sharding import PartitionSpec as P


HEAD = 128
EPS = 1e-06
BF16 = jnp.bfloat16
F32 = jnp.float32


IN_HBM = pl.BlockSpec(memory_space=pltpu.HBM)
IN_VMEM = pl.BlockSpec(memory_space=pltpu.VMEM)


def shape(dims, dtype):
    return jax.ShapeDtypeStruct(dims, dtype)


def params(megabytes):
    return pltpu.CompilerParams(vmem_limit_bytes=megabytes << 20)


def in_hbm(x):
    return pltpu.with_memory_space_constraint(x, pltpu.HBM)


def matmul(a, b):
    return jnp.dot(a, b, preferred_element_type=F32)


def features(x):
    return jnp.where(x > 0.0, x + 1.0, jnp.exp(jnp.minimum(x, 0.0)))


def states_kernel(frames, heads, fetched, video_in, wk_hbm, wv_hbm, *refs):
    if fetched:
        parts_out, key, value = refs
        video, wk, wv = video_in, wk_hbm, wv_hbm
        late = []
    else:
        (wq_hbm, parts_out, video, wk_out, wv_out, wq_out, wk, wv, key, value,
         wk_sem, wv_sem, video_sem, late_sem) = refs
        rest = wk_out.shape[1]
        source = pl.ds(heads * HEAD, rest)
        late = [
            pltpu.make_async_copy(wq_hbm, wq_out, late_sem.at[0]),
            pltpu.make_async_copy(wk_hbm.at[:, source], wk_out, late_sem.at[1]),
            pltpu.make_async_copy(wv_hbm.at[:, source], wv_out, late_sem.at[2]),
        ]
    per = video.shape[0] // frames

    def weight_copies(h):
        cols = pl.ds(pl.multiple_of(h * HEAD, HEAD), HEAD)
        return (
            pltpu.make_async_copy(wk_hbm.at[:, cols], wk.at[:, cols], wk_sem.at[h]),
            pltpu.make_async_copy(wv_hbm.at[:, cols], wv.at[:, cols], wv_sem.at[h]),
        )

    def video_copy(f):
        rows = pl.ds(f * per, per)
        return pltpu.make_async_copy(video_in.at[rows], video.at[rows], video_sem.at[f])

    if not fetched:
        soon = min(2, heads)
        for f in range(frames):
            video_copy(f).start()
        for h in range(soon):
            for c in weight_copies(h):
                c.start()
        for f in range(frames):
            video_copy(f).wait()
        for h in range(soon, heads):
            for c in weight_copies(h):
                c.start()
        for c in late:
            c.start()

    def one_head(h, carry):
        if not fetched:
            for c in weight_copies(h):
                c.wait()
        cols = pl.ds(pl.multiple_of(h * HEAD, HEAD), HEAD)
        both = jnp.concatenate([wk[:, cols], wv[:, cols]], axis=1)
        for f in range(frames):
            rows = slice(f * per, (f + 1) * per)
            kv = matmul(video[rows, :], both)
            key[h, rows, :] = features(kv[:, :HEAD]).astype(BF16)
            value[h, rows, :] = kv[:, HEAD:].astype(BF16)
        return carry

    lax.fori_loop(0, heads, one_head, 0)

    for h in range(heads):
        for f in range(frames):
            rows = slice(f * per, (f + 1) * per)
            state = lax.dot_general(
                key[h, rows, :], value[h, rows, :], (((0,), (0,)), ((), ())),
                preferred_element_type=F32,
            )
            parts_out[f, h] = state.astype(BF16)
    for c in late:
        c.wait()


def first_states(video, wk, wv, wq, frames, heads):
    tokens, d = video.shape
    width = heads * HEAD
    return pl.pallas_call(
        functools.partial(states_kernel, frames, heads, False),
        out_shape=[
            shape((frames, heads, HEAD, HEAD), BF16),
            shape((tokens, d), BF16),
            shape((d, d - width), BF16),
            shape((d, d - width), BF16),
            shape((d, d), BF16),
        ],
        in_specs=[IN_HBM] * 4,
        out_specs=[IN_VMEM] * 5,
        scratch_shapes=[
            pltpu.VMEM((d, width), BF16),
            pltpu.VMEM((d, width), BF16),
            pltpu.VMEM((heads, tokens, HEAD), BF16),
            pltpu.VMEM((heads, tokens, HEAD), BF16),
            pltpu.SemaphoreType.DMA((heads,)),
            pltpu.SemaphoreType.DMA((heads,)),
            pltpu.SemaphoreType.DMA((frames,)),
            pltpu.SemaphoreType.DMA((3,)),
        ],
        name="states",
        compiler_params=params(20),
    )(in_hbm(video), in_hbm(wk), in_hbm(wv), in_hbm(wq))


def second_states(video, wk, wv, frames):
    tokens, _ = video.shape
    heads = wk.shape[1] // HEAD
    return pl.pallas_call(
        functools.partial(states_kernel, frames, heads, True),
        out_shape=shape((frames, heads, HEAD, HEAD), BF16),
        in_specs=[IN_VMEM] * 3,
        out_specs=IN_VMEM,
        scratch_shapes=[
            pltpu.VMEM((heads, tokens, HEAD), BF16),
            pltpu.VMEM((heads, tokens, HEAD), BF16),
        ],
        name="states",
        compiler_params=params(20),
    )(video, wk, wv)


def total_call(parts, other_parts):
    frames, heads = parts.shape[:2]
    half = HEAD // 2

    def kernel(parts, other_parts, out, sent):
        low = lax.axis_index("space") == 0
        for h in range(heads):
            total = None
            for f in range(frames):
                one = parts[f, h].astype(F32) + other_parts[f, h].astype(F32)
                total = one if total is None else total + one
            total = jnp.where(low, total[:half], total[half:])
            out[h] = total
            sent[h] = total.astype(BF16)

    dims = (heads, half, HEAD)
    return pl.pallas_call(
        kernel,
        out_shape=[shape(dims, F32), shape(dims, BF16)],
        in_specs=[IN_VMEM] * 2,
        out_specs=[IN_VMEM] * 2,
        name="total",
        compiler_params=params(4),
    )(parts, other_parts)


def query_call(video, w, first, width):
    def kernel(video, w, out):
        out[...] = features(matmul(video[...], w[:, first : first + width])).astype(BF16)

    return pl.pallas_call(
        kernel,
        out_shape=shape((video.shape[0], width), BF16),
        in_specs=[IN_VMEM] * 2,
        out_specs=IN_VMEM,
        name="query",
        compiler_params=params(16),
    )(video, w)


def attend(frames, queries, parts, other_parts, carry, other_carry, used, head_out):
    heads = carry.shape[0]
    per = head_out.shape[0] // frames
    low = lax.axis_index("space") == 0
    used[...] = jnp.zeros_like(used)
    for h in range(heads):
        mine, theirs = carry[h].astype(F32), other_carry[h].astype(F32)
        running = jnp.concatenate(
            [jnp.where(low, mine, theirs), jnp.where(low, theirs, mine)], axis=0
        )
        at = (h % 2) * HEAD
        for f in range(frames):
            running = running + parts[f, h].astype(F32) + other_parts[f, h].astype(F32)
            used[f, h // 2, at : at + HEAD, at : at + HEAD] = running.astype(BF16)
    for f in range(frames):
        rows = slice(f * per, (f + 1) * per)
        for p in range(pl.cdiv(heads, 2)):
            width = min(2, heads - 2 * p) * HEAD
            first = 2 * p * HEAD
            query, at = queries[0], first
            for piece in queries[1:]:
                if at < query.shape[1]:
                    break
                query, at = piece, at - query.shape[1]
            attended = matmul(query[rows, at : at + width], used[f, p, :width, :width])
            for h in range(width // HEAD):
                one = attended[:, h * HEAD : (h + 1) * HEAD]
                scale = lax.rsqrt(jnp.mean(one * one, axis=1, keepdims=True) + EPS)
                at = first + h * HEAD
                head_out[rows, at : at + HEAD] = (one * scale).astype(BF16)


def used_shape(frames, heads):
    return pltpu.VMEM((frames, pl.cdiv(heads, 2), 2 * HEAD, 2 * HEAD), BF16)


def partial_call(video, chunk, w_out, frames):
    tokens, d = video.shape
    heads = chunk[3].shape[0]

    queries, chunk = chunk[0], chunk[1:]
    n = len(queries)

    def kernel(video, *refs):
        parts, other_parts, carry, other_carry, w_out, out, used, head_out = refs[n:]
        attend(frames, refs[:n], parts, other_parts, carry, other_carry, used, head_out)
        per = tokens // frames
        for f in range(frames):
            rows = slice(f * per, (f + 1) * per)
            out[rows, :] = video[rows, :].astype(F32) + matmul(
                head_out[rows, :], w_out[: heads * HEAD, :]
            )

    return pl.pallas_call(
        kernel,
        out_shape=shape((tokens, d), F32),
        in_specs=[IN_VMEM] * (n + 6),
        out_specs=IN_VMEM,
        scratch_shapes=[used_shape(frames, heads), pltpu.VMEM((tokens, heads * HEAD), BF16)],
        name="partial",
        compiler_params=params(20),
    )(video, *queries, *chunk, w_out)


def latent_kernel(
    frames, columns, tiles, partial, query, parts, other_parts, carry, other_carry,
    w_out, w_latent, out, used, head_out, latent,
):
    tokens, d = partial.shape
    per = tokens // frames
    width = head_out.shape[1]
    attend(frames, [query], parts, other_parts, carry, other_carry, used, head_out)
    for f in range(frames):
        rows = slice(f * per, (f + 1) * per)
        summed = partial[rows, :] + matmul(head_out[rows, :], w_out[d - width :, :])
        scale = lax.rsqrt(jnp.mean(summed * summed, axis=1, keepdims=True) + EPS)
        latent[rows, :] = matmul(summed.astype(BF16), w_latent[...]) * scale

    own = columns // tiles
    grid_rows = per // columns
    main = grid_rows * frames * own
    for t in range(tiles):
        for r in range(grid_rows):
            block = [
                latent[pl.ds(f * per + r * columns + t * own, own), :] for f in range(frames)
            ]
            at = r * frames * own
            out[t, at : at + frames * own, :] = jnp.concatenate(block, axis=0).astype(BF16)
        sides = []
        for column in (t * own - 1, (t + 1) * own):
            for f in range(frames):
                if 0 <= column < columns:
                    at = f * per + column
                    sides.append(latent[pl.ds(at, grid_rows, stride=columns), :])
                else:
                    sides.append(jnp.zeros((grid_rows, out.shape[2]), F32))
        out[t, main:, :] = jnp.concatenate(sides, axis=0).astype(BF16)


def latent_call(partial, chunk, w_out, w_latent, frames, columns, tiles):
    tokens, _ = partial.shape
    channels = w_latent.shape[1]
    heads = chunk[3].shape[0]
    rows = tokens // columns * (columns // tiles + 2)
    return pl.pallas_call(
        functools.partial(latent_kernel, frames, columns, tiles),
        out_shape=shape((tiles, rows, channels), BF16),
        in_specs=[IN_VMEM] * 8,
        out_specs=IN_VMEM,
        scratch_shapes=[
            used_shape(frames, heads),
            pltpu.VMEM((tokens, heads * HEAD), BF16),
            pltpu.VMEM((tokens, channels), F32),
        ],
        name="latent",
        compiler_params=params(20),
    )(partial, *chunk[0], *chunk[1:], w_out, w_latent)


def lay_rows(frames, tiles, grid_rows, own, rows, blocks, edge, left, middle, right):
    group = frames * own
    main = grid_rows * group
    channels = left.shape[-1]
    column = lax.broadcasted_iota(jnp.int32, (group, 1), 0) % own

    def lay(index, t, body, sides):
        at = slice(t * group, (t + 1) * group)
        first, last = (
            jnp.concatenate(
                [jnp.broadcast_to(sides[k : k + 1], (own, channels))
                 for k in range(side * frames, (side + 1) * frames)], axis=0
            )
            for side in range(2)
        )
        down = pltpu.roll(body, 1, 0)
        up = pltpu.roll(body, group - 1, 0)
        left[index, at, :] = jnp.where(column == 0, first, down).astype(BF16)
        middle[index, at, :] = body.astype(BF16)
        right[index, at, :] = jnp.where(column == own - 1, last, up).astype(BF16)

    for t in range(tiles):
        everything = blocks[t].astype(F32)
        beside = None if edge is None else edge[t].astype(F32)
        for index, row in enumerate(rows):
            if 0 <= row < grid_rows:
                sides = [
                    everything[main + k * grid_rows + row : main + k * grid_rows + row + 1]
                    for k in range(2 * frames)
                ]
                lay(index, t, everything[row * group : (row + 1) * group],
                    jnp.concatenate(sides, axis=0))
            else:
                present = lax.axis_index("space") == (1 if row < 0 else 0)
                there = jnp.where(present, beside, 0.0)
                lay(index, t, there[:group], there[group:])


def lay_taps(weight, taps):
    w = weight[...].astype(F32)
    channels = weight.shape[2]
    row_sets = (((0,), (1, 2)), ((0, 1), (2,)))
    for a in range(2):
        for b in range(2):
            for i, rows in enumerate(row_sets[a]):
                for j, cols in enumerate(row_sets[b]):
                    tap = sum(w[r, c] for r in rows for c in cols)
                    at = (2 * i + j) * channels
                    taps[2 * a + b, at : at + channels, :] = (0.5 * tap).astype(BF16)


def decode_row(own, index, bias, left, middle, right, taps, wide, staged, first):
    views = ((left, middle), (middle, right))
    half_bias = 0.5 * bias[...]
    lanes = wide.shape[-1]
    total = left.shape[1]
    for a in range(2):
        for b in range(2):
            lhs = jnp.concatenate(
                [v[index + a + k] for k in range(2) for v in views[b]], axis=1
            )
            h = matmul(lhs, taps[2 * a + b]) + half_bias
            value = h + h * jnp.tanh(h)
            for n in range(wide.shape[1]):
                wide[a, n, pl.ds(b, total, stride=2), :] = value[:, n * lanes : (n + 1) * lanes]
        for n in range(wide.shape[1]):
            shaped = wide[a, n].reshape(total // own, 2 * own, lanes)
            staged[:, first + a, :, n * lanes : (n + 1) * lanes] = shaped.astype(BF16)


def decode_scratch(rows, total, channels, width):
    return [pltpu.VMEM((rows, total, channels), BF16)] * 3 + [
        pltpu.VMEM((2, width // HEAD, 2 * total, HEAD), F32)
    ]


def interior_call(blocks, weight, bias, frames, tiles, grid_rows, own):
    channels, width = weight.shape[2:]
    total = tiles * frames * own

    def kernel(blocks, weight, bias, out, taps, left, middle, right, wide):
        lay_taps(weight, taps)
        lay_rows(frames, tiles, grid_rows, own, range(grid_rows), blocks, None,
                 left, middle, right)
        for r in range(1, grid_rows - 1):
            decode_row(own, r - 1, bias, left, middle, right, taps, wide, out, 2 * (r - 1))

    return pl.pallas_call(
        kernel,
        out_shape=[
            shape((tiles * frames, 2 * (grid_rows - 2), 2 * own, width), BF16),
            shape((4, 4 * channels, width), BF16),
        ],
        in_specs=[IN_VMEM] * 3,
        out_specs=[IN_VMEM] * 2,
        scratch_shapes=decode_scratch(grid_rows, total, channels, width),
        name="interior",
        compiler_params=params(24),
    )(blocks, weight, bias)


def border_call(blocks, edge, interior, taps, bias, frames, tiles, grid_rows, own):
    channels = blocks.shape[2]
    width = taps.shape[2]
    total = tiles * frames * own
    last = 2 * (grid_rows - 1)

    def kernel(blocks, edge, interior, taps, bias, out, left, middle, right, wide, staged, sem):
        copies = [pltpu.make_async_copy(interior, out.at[:, pl.ds(2, last - 2)], sem.at[2])]
        copies[0].start()
        rows = [-1, 0, 1, grid_rows - 2, grid_rows - 1, grid_rows]
        lay_rows(frames, tiles, grid_rows, own, rows, blocks, edge, left, middle, right)
        for i, (index, row) in enumerate(((0, 0), (3, last))):
            decode_row(own, index, bias, left, middle, right, taps, wide, staged, 2 * i)
            copies.append(
                pltpu.make_async_copy(
                    staged.at[:, pl.ds(2 * i, 2)], out.at[:, pl.ds(row, 2)], sem.at[i]
                )
            )
            copies[-1].start()
        for c in copies:
            c.wait()

    return pl.pallas_call(
        kernel,
        out_shape=shape((tiles * frames, 2 * grid_rows, 2 * own, width), BF16),
        in_specs=[IN_VMEM] * 5,
        out_specs=IN_HBM,
        scratch_shapes=decode_scratch(6, total, channels, width)
        + [
            pltpu.VMEM((tiles * frames, 4, 2 * own, width), BF16),
            pltpu.SemaphoreType.DMA((3,)),
        ],
        name="border",
        compiler_params=params(24),
    )(blocks, edge, interior, taps, bias)


def round_call(step, last, got, total, carry):
    def kernel(got, total, *refs):
        upper = (lax.axis_index("tm") // step) % 2 == 1
        received = got[...].astype(F32)
        before = jnp.where(upper, received, 0.0)
        if carry is not None:
            before = refs[0][...] + before
            refs = refs[1:]
        if last:
            refs[0][...] = before.astype(BF16)
        else:
            carry_out, total_out, sent_out = refs
            carry_out[...] = before
            both = total[...] + received
            total_out[...] = both
            sent_out[...] = both.astype(BF16)

    near = [got, total] + ([] if carry is None else [carry])
    kinds = [BF16] if last else [F32, F32, BF16]
    return pl.pallas_call(
        kernel,
        out_shape=[shape(total.shape, kind) for kind in kinds],
        in_specs=[IN_VMEM] * len(near),
        out_specs=[IN_VMEM] * len(kinds),
        name="round",
        compiler_params=params(4),
    )(*near)


def prefix_rounds(total, sent, tiles):
    carry = None
    step, number = 1, 0
    while step < tiles:
        last = 2 * step >= tiles
        got = lax.ppermute(sent, "tm", [(i, i ^ step) for i in range(tiles)])
        out = round_call(step, last, got, total, carry)
        if last:
            return out[0]
        carry, total, sent = out
        step *= 2
        number += 1
    return jnp.zeros_like(sent)


SWAP = [(0, 1), (1, 0)]


def body(video, w_query, w_key, w_value, w_out, w_latent, conv_weight, conv_bias):
    frames, grid_rows, columns, d = video.shape
    tiles = lax.axis_size("tm")
    own = columns // tiles
    flat = video.reshape(-1, d)
    heads = d // HEAD
    split = heads - heads // 2
    parts_a, near, wk_b, wv_b, near_query = first_states(
        flat, w_key, w_value, w_query, frames, split
    )
    other_a = lax.ppermute(parts_a, "space", SWAP)
    parts_b = second_states(near, wk_b, wv_b, frames)
    other_b = lax.ppermute(parts_b, "space", SWAP)

    ready = {}
    for name, first, parts, other in (("a", 0, parts_a, other_a), ("b", split, parts_b, other_b)):
        count = parts.shape[1]
        total, sent = total_call(parts, other)
        cuts = [first, first + 2, first + count] if name == "a" else [first, first + count]
        queries = []
        for low, high in zip(cuts, cuts[1:]):
            queries.append(
                query_call(near, near_query, low * HEAD, (high - low) * HEAD)
            )
        carry = prefix_rounds(total, sent, tiles)
        other_carry = lax.ppermute(carry, "space", SWAP)
        ready[name] = (queries, parts, other, carry, other_carry)

    partial = partial_call(near, ready["a"], w_out, frames)
    blocks = latent_call(
        partial, ready["b"], w_out, w_latent, frames, columns, tiles
    )
    blocks = lax.all_to_all(blocks, "tm", 0, 0, tiled=True)
    return decode(blocks, conv_weight, conv_bias, frames, grid_rows, own, tiles)


def decode(blocks, conv_weight, conv_bias, frames, grid_rows, own, tiles):
    channels = conv_weight.shape[2]
    width = conv_weight.shape[3]
    group = frames * own
    main = grid_rows * group

    def edge_kernel(blocks, out):
        def take(r):
            for t in range(tiles):
                out[t, :group] = blocks[t, r * group : (r + 1) * group]
                sides = blocks[t, main:].astype(F32)
                out[t, group:] = jnp.concatenate(
                    [sides[k * grid_rows + r : k * grid_rows + r + 1] for k in range(2 * frames)],
                    axis=0,
                ).astype(BF16)

        upper = lax.axis_index("space") == 0

        @pl.when(upper)
        def _():
            take(grid_rows - 1)

        @pl.when(jnp.logical_not(upper))
        def _():
            take(0)

    mine = pl.pallas_call(
        edge_kernel,
        out_shape=shape((tiles, group + 2 * frames, channels), BF16),
        in_specs=[IN_VMEM],
        out_specs=IN_VMEM,
        name="edge",
        compiler_params=params(4),
    )(blocks)
    beside = lax.ppermute(mine, "space", SWAP)
    bias = conv_bias.reshape(1, width)
    interior, taps = interior_call(
        blocks, conv_weight, bias, frames, tiles, grid_rows, own
    )
    return border_call(blocks, beside, interior, taps, bias, frames, tiles, grid_rows, own)


def solution(mesh):
    assert mesh.shape["space"] == 2
    tiles = mesh.shape["tm"]
    assert tiles & (tiles - 1) == 0
    placed = (P(("groups", "tm"), "space", None, None), P(), P(), P(), P(), P(), P(), P())
    return jax.shard_map(
        body,
        mesh=mesh,
        in_specs=placed,
        out_specs=P("groups", "space", "tm", None),
        check_vma=False,
    )
```

```python
import functools

import jax
import jax.numpy as jnp
from jax import lax
from jax.experimental import pallas as pl
from jax.experimental.pallas import tpu as pltpu
from jax.sharding import PartitionSpec as P


HEAD = 128
EPS = 1e-06
BF16 = jnp.bfloat16
F32 = jnp.float32


IN_HBM = pl.BlockSpec(memory_space=pltpu.HBM)
IN_VMEM = pl.BlockSpec(memory_space=pltpu.VMEM)


def shape(dims, dtype):
    return jax.ShapeDtypeStruct(dims, dtype)


def params(megabytes):
    return pltpu.CompilerParams(vmem_limit_bytes=megabytes << 20)


def in_hbm(x):
    return pltpu.with_memory_space_constraint(x, pltpu.HBM)


def matmul(a, b):
    return jnp.dot(a, b, preferred_element_type=F32)


def features(x):
    return jnp.where(x > 0.0, x + 1.0, jnp.exp(jnp.minimum(x, 0.0)))


def states_kernel(frames, heads, fetched, video_in, wk_hbm, wv_hbm, *refs):
    if fetched:
        parts_out, mine_out, theirs_out, key, value = refs
        video, wk, wv = video_in, wk_hbm, wv_hbm
        late = []
    else:
        (wq_hbm, parts_out, video, wk_out, wv_out, wq_out, wk, wv, key, value,
         wk_sem, wv_sem, video_sem, late_sem) = refs
        rest = wk_out.shape[1]
        source = pl.ds(heads * HEAD, rest)
        late = [
            pltpu.make_async_copy(wq_hbm, wq_out, late_sem.at[0]),
            pltpu.make_async_copy(wk_hbm.at[:, source], wk_out, late_sem.at[1]),
            pltpu.make_async_copy(wv_hbm.at[:, source], wv_out, late_sem.at[2]),
        ]
    per = video.shape[0] // frames

    def weight_copies(h):
        cols = pl.ds(pl.multiple_of(h * HEAD, HEAD), HEAD)
        return (
            pltpu.make_async_copy(wk_hbm.at[:, cols], wk.at[:, cols], wk_sem.at[h]),
            pltpu.make_async_copy(wv_hbm.at[:, cols], wv.at[:, cols], wv_sem.at[h]),
        )

    def video_copy(f):
        rows = pl.ds(f * per, per)
        return pltpu.make_async_copy(video_in.at[rows], video.at[rows], video_sem.at[f])

    if not fetched:
        soon = min(2, heads)
        for f in range(frames):
            video_copy(f).start()
        for h in range(soon):
            for c in weight_copies(h):
                c.start()
        for f in range(frames):
            video_copy(f).wait()
        for h in range(soon, heads):
            for c in weight_copies(h):
                c.start()
        for c in late:
            c.start()

    def one_head(h, carry):
        if not fetched:
            for c in weight_copies(h):
                c.wait()
        cols = pl.ds(pl.multiple_of(h * HEAD, HEAD), HEAD)
        both = jnp.concatenate([wk[:, cols], wv[:, cols]], axis=1)
        for f in range(frames):
            rows = slice(f * per, (f + 1) * per)
            kv = matmul(video[rows, :], both)
            key[h, rows, :] = features(kv[:, :HEAD]).astype(BF16)
            value[h, rows, :] = kv[:, HEAD:].astype(BF16)
        return carry

    lax.fori_loop(0, heads, one_head, 0)

    totals = []
    for h in range(heads):
        total = None
        for f in range(frames):
            rows = slice(f * per, (f + 1) * per)
            state = lax.dot_general(
                key[h, rows, :], value[h, rows, :], (((0,), (0,)), ((), ())),
                preferred_element_type=F32,
            )
            parts_out[f, h] = state.astype(BF16)
            total = state if total is None else total + state
        totals.append(total)
    if fetched:
        lower = lax.axis_index("space") == 0
        half = heads // 2
        for h in range(half):
            mine_out[h] = jnp.where(lower, totals[h], totals[half + h])
            theirs_out[h] = jnp.where(lower, totals[half + h], totals[h]).astype(BF16)
    for c in late:
        c.wait()


def first_states(video, wk, wv, wq, frames, heads):
    tokens, d = video.shape
    width = heads * HEAD
    return pl.pallas_call(
        functools.partial(states_kernel, frames, heads, False),
        out_shape=[
            shape((frames, heads, HEAD, HEAD), BF16),
            shape((tokens, d), BF16),
            shape((d, d - width), BF16),
            shape((d, d - width), BF16),
            shape((d, d), BF16),
        ],
        in_specs=[IN_HBM] * 4,
        out_specs=[IN_VMEM] * 5,
        scratch_shapes=[
            pltpu.VMEM((d, width), BF16),
            pltpu.VMEM((d, width), BF16),
            pltpu.VMEM((heads, tokens, HEAD), BF16),
            pltpu.VMEM((heads, tokens, HEAD), BF16),
            pltpu.SemaphoreType.DMA((heads,)),
            pltpu.SemaphoreType.DMA((heads,)),
            pltpu.SemaphoreType.DMA((frames,)),
            pltpu.SemaphoreType.DMA((3,)),
        ],
        name="states",
        compiler_params=params(20),
    )(in_hbm(video), in_hbm(wk), in_hbm(wv), in_hbm(wq))


def second_states(video, wk, wv, frames):
    tokens, _ = video.shape
    heads = wk.shape[1] // HEAD
    return pl.pallas_call(
        functools.partial(states_kernel, frames, heads, True),
        out_shape=[
            shape((frames, heads, HEAD, HEAD), BF16),
            shape((heads // 2, HEAD, HEAD), F32),
            shape((heads // 2, HEAD, HEAD), BF16),
        ],
        in_specs=[IN_VMEM] * 3,
        out_specs=[IN_VMEM] * 3,
        scratch_shapes=[
            pltpu.VMEM((heads, tokens, HEAD), BF16),
            pltpu.VMEM((heads, tokens, HEAD), BF16),
        ],
        name="states",
        compiler_params=params(20),
    )(video, wk, wv)


def total_call(parts, other_parts):
    frames, heads = parts.shape[:2]
    half = HEAD // 2

    def kernel(parts, other_parts, out, sent):
        low = lax.axis_index("space") == 0
        for h in range(heads):
            total = None
            for f in range(frames):
                one = parts[f, h].astype(F32) + other_parts[f, h].astype(F32)
                total = one if total is None else total + one
            total = jnp.where(low, total[:half], total[half:])
            out[h] = total
            sent[h] = total.astype(BF16)

    dims = (heads, half, HEAD)
    return pl.pallas_call(
        kernel,
        out_shape=[shape(dims, F32), shape(dims, BF16)],
        in_specs=[IN_VMEM] * 2,
        out_specs=[IN_VMEM] * 2,
        name="total",
        compiler_params=params(4),
    )(parts, other_parts)


def add_call(mine, got):
    def kernel(mine, got, out, sent):
        total = mine[...] + got[...].astype(F32)
        out[...] = total
        sent[...] = total.astype(BF16)

    return pl.pallas_call(
        kernel,
        out_shape=[shape(mine.shape, F32), shape(mine.shape, BF16)],
        in_specs=[IN_VMEM] * 2,
        out_specs=[IN_VMEM] * 2,
        name="add",
        compiler_params=params(4),
    )(mine, got)


def query_call(video, w, first, width):
    def kernel(video, w, out):
        out[...] = features(matmul(video[...], w[:, first : first + width])).astype(BF16)

    return pl.pallas_call(
        kernel,
        out_shape=shape((video.shape[0], width), BF16),
        in_specs=[IN_VMEM] * 2,
        out_specs=IN_VMEM,
        name="query",
        compiler_params=params(16),
    )(video, w)


def attend(frames, queries, parts, other_parts, carry, other_carry, used, head_out):
    heads = carry.shape[0]
    per = head_out.shape[0] // frames
    low = lax.axis_index("space") == 0
    used[...] = jnp.zeros_like(used)
    for h in range(heads):
        mine, theirs = carry[h].astype(F32), other_carry[h].astype(F32)
        running = jnp.concatenate(
            [jnp.where(low, mine, theirs), jnp.where(low, theirs, mine)], axis=0
        )
        at = (h % 2) * HEAD
        for f in range(frames):
            running = running + parts[f, h].astype(F32) + other_parts[f, h].astype(F32)
            used[f, h // 2, at : at + HEAD, at : at + HEAD] = running.astype(BF16)
    for f in range(frames):
        rows = slice(f * per, (f + 1) * per)
        for p in range(pl.cdiv(heads, 2)):
            width = min(2, heads - 2 * p) * HEAD
            first = 2 * p * HEAD
            query, at = queries[0], first
            for piece in queries[1:]:
                if at < query.shape[1]:
                    break
                query, at = piece, at - query.shape[1]
            attended = matmul(query[rows, at : at + width], used[f, p, :width, :width])
            for h in range(width // HEAD):
                one = attended[:, h * HEAD : (h + 1) * HEAD]
                scale = lax.rsqrt(jnp.mean(one * one, axis=1, keepdims=True) + EPS)
                at = first + h * HEAD
                head_out[rows, at : at + HEAD] = (one * scale).astype(BF16)


def used_shape(frames, heads):
    return pltpu.VMEM((frames, pl.cdiv(heads, 2), 2 * HEAD, 2 * HEAD), BF16)


def partial_call(video, chunk, w_out, frames):
    tokens, d = video.shape
    heads = chunk[3].shape[0]

    queries, chunk = chunk[0], chunk[1:]
    n = len(queries)

    def kernel(video, *refs):
        parts, other_parts, carry, other_carry, w_out, out, used, head_out = refs[n:]
        attend(frames, refs[:n], parts, other_parts, carry, other_carry, used, head_out)
        per = tokens // frames
        for f in range(frames):
            rows = slice(f * per, (f + 1) * per)
            out[rows, :] = video[rows, :].astype(F32) + matmul(
                head_out[rows, :], w_out[: heads * HEAD, :]
            )

    return pl.pallas_call(
        kernel,
        out_shape=shape((tokens, d), F32),
        in_specs=[IN_VMEM] * (n + 6),
        out_specs=IN_VMEM,
        scratch_shapes=[used_shape(frames, heads), pltpu.VMEM((tokens, heads * HEAD), BF16)],
        name="partial",
        compiler_params=params(20),
    )(video, *queries, *chunk, w_out)


def attend_half(frames, half, query, parts, other_parts, carry, used, head_out):
    heads = carry.shape[0]
    per = head_out.shape[0] // frames
    used[...] = jnp.zeros_like(used)
    for h in range(heads):
        running = carry[h].astype(F32)
        at = (h % 2) * HEAD
        for f in range(frames):
            own = half * heads + h
            running = running + parts[f, own].astype(F32) + other_parts[f, own].astype(F32)
            used[f, h // 2, at : at + HEAD, at : at + HEAD] = running.astype(BF16)
    for f in range(frames):
        rows = slice(f * per, (f + 1) * per)
        for p in range(pl.cdiv(heads, 2)):
            width = min(2, heads - 2 * p) * HEAD
            first = 2 * p * HEAD
            cols = pl.ds(pl.multiple_of(half * heads * HEAD + first, HEAD), width)
            attended = matmul(query[rows, cols], used[f, p, :width, :width])
            for h in range(width // HEAD):
                one = attended[:, h * HEAD : (h + 1) * HEAD]
                scale = lax.rsqrt(jnp.mean(one * one, axis=1, keepdims=True) + EPS)
                at = first + h * HEAD
                head_out[rows, at : at + HEAD] = (one * scale).astype(BF16)


def half_rows(w_out, half, width):
    first = w_out.shape[0] - 2 * width
    return w_out[pl.ds(pl.multiple_of(first + half * width, HEAD), width), :]


def own_call(partial, chunk, w_out, frames):
    query, parts, other_parts, carry, _ = chunk
    tokens, d = partial.shape
    heads = carry.shape[0]
    width = heads * HEAD

    def kernel(partial, query, parts, other_parts, carry, w_out, out, used, head_out):
        half = lax.axis_index("space")
        attend_half(frames, half, query, parts, other_parts, carry, used, head_out)
        w = half_rows(w_out, half, width)
        per = tokens // frames
        for f in range(frames):
            rows = slice(f * per, (f + 1) * per)
            out[rows, :] = partial[rows, :] + matmul(head_out[rows, :], w)

    return pl.pallas_call(
        kernel,
        out_shape=shape((tokens, d), F32),
        in_specs=[IN_VMEM] * 6,
        out_specs=IN_VMEM,
        scratch_shapes=[used_shape(frames, heads), pltpu.VMEM((tokens, width), BF16)],
        name="own",
        compiler_params=params(20),
    )(partial, query, parts, other_parts, carry, w_out)


def latent_kernel(
    frames, columns, tiles, partial, query, parts, other_parts, carry,
    w_out, w_latent, out, used, head_out, latent,
):
    tokens, _ = partial.shape
    per = tokens // frames
    half = 1 - lax.axis_index("space")
    attend_half(frames, half, query, parts, other_parts, carry, used, head_out)
    w = half_rows(w_out, half, head_out.shape[1])
    for f in range(frames):
        rows = slice(f * per, (f + 1) * per)
        summed = partial[rows, :] + matmul(head_out[rows, :], w)
        scale = lax.rsqrt(jnp.mean(summed * summed, axis=1, keepdims=True) + EPS)
        latent[rows, :] = matmul(summed.astype(BF16), w_latent[...]) * scale

    own = columns // tiles
    grid_rows = per // columns
    main = grid_rows * frames * own
    for t in range(tiles):
        for r in range(grid_rows):
            block = [
                latent[pl.ds(f * per + r * columns + t * own, own), :] for f in range(frames)
            ]
            at = r * frames * own
            out[t, at : at + frames * own, :] = jnp.concatenate(block, axis=0).astype(BF16)
        sides = []
        for column in (t * own - 1, (t + 1) * own):
            for f in range(frames):
                if 0 <= column < columns:
                    at = f * per + column
                    sides.append(latent[pl.ds(at, grid_rows, stride=columns), :])
                else:
                    sides.append(jnp.zeros((grid_rows, out.shape[2]), F32))
        out[t, main:, :] = jnp.concatenate(sides, axis=0).astype(BF16)


def latent_call(partial, chunk, w_out, w_latent, frames, columns, tiles):
    query, parts, other_parts, _, other_carry = chunk
    tokens, _ = partial.shape
    channels = w_latent.shape[1]
    heads = other_carry.shape[0]
    rows = tokens // columns * (columns // tiles + 2)
    return pl.pallas_call(
        functools.partial(latent_kernel, frames, columns, tiles),
        out_shape=shape((tiles, rows, channels), BF16),
        in_specs=[IN_VMEM] * 7,
        out_specs=IN_VMEM,
        scratch_shapes=[
            used_shape(frames, heads),
            pltpu.VMEM((tokens, heads * HEAD), BF16),
            pltpu.VMEM((tokens, channels), F32),
        ],
        name="latent",
        compiler_params=params(20),
    )(partial, query, parts, other_parts, other_carry, w_out, w_latent)


def lay_rows(frames, tiles, grid_rows, own, rows, blocks, edge, left, middle, right):
    group = frames * own
    main = grid_rows * group
    channels = left.shape[-1]
    column = lax.broadcasted_iota(jnp.int32, (group, 1), 0) % own

    def lay(index, t, body, sides):
        at = slice(t * group, (t + 1) * group)
        first, last = (
            jnp.concatenate(
                [jnp.broadcast_to(sides[k : k + 1], (own, channels))
                 for k in range(side * frames, (side + 1) * frames)], axis=0
            )
            for side in range(2)
        )
        down = pltpu.roll(body, 1, 0)
        up = pltpu.roll(body, group - 1, 0)
        left[index, at, :] = jnp.where(column == 0, first, down).astype(BF16)
        middle[index, at, :] = body.astype(BF16)
        right[index, at, :] = jnp.where(column == own - 1, last, up).astype(BF16)

    for t in range(tiles):
        everything = blocks[t].astype(F32)
        beside = None if edge is None else edge[t].astype(F32)
        for index, row in enumerate(rows):
            if 0 <= row < grid_rows:
                sides = [
                    everything[main + k * grid_rows + row : main + k * grid_rows + row + 1]
                    for k in range(2 * frames)
                ]
                lay(index, t, everything[row * group : (row + 1) * group],
                    jnp.concatenate(sides, axis=0))
            else:
                present = lax.axis_index("space") == (1 if row < 0 else 0)
                there = jnp.where(present, beside, 0.0)
                lay(index, t, there[:group], there[group:])


def lay_taps(weight, taps):
    w = weight[...].astype(F32)
    channels = weight.shape[2]
    row_sets = (((0,), (1, 2)), ((0, 1), (2,)))
    for a in range(2):
        for b in range(2):
            for i, rows in enumerate(row_sets[a]):
                for j, cols in enumerate(row_sets[b]):
                    tap = sum(w[r, c] for r in rows for c in cols)
                    at = (2 * i + j) * channels
                    taps[2 * a + b, at : at + channels, :] = (0.5 * tap).astype(BF16)


def decode_row(own, index, bias, left, middle, right, taps, wide, staged, first):
    views = ((left, middle), (middle, right))
    half_bias = 0.5 * bias[...]
    lanes = wide.shape[-1]
    total = left.shape[1]
    for a in range(2):
        for b in range(2):
            lhs = jnp.concatenate(
                [v[index + a + k] for k in range(2) for v in views[b]], axis=1
            )
            h = matmul(lhs, taps[2 * a + b]) + half_bias
            value = h + h * jnp.tanh(h)
            for n in range(wide.shape[1]):
                wide[a, n, pl.ds(b, total, stride=2), :] = value[:, n * lanes : (n + 1) * lanes]
        for n in range(wide.shape[1]):
            shaped = wide[a, n].reshape(total // own, 2 * own, lanes)
            staged[:, first + a, :, n * lanes : (n + 1) * lanes] = shaped.astype(BF16)


def decode_scratch(rows, total, channels, width):
    return [pltpu.VMEM((rows, total, channels), BF16)] * 3 + [
        pltpu.VMEM((2, width // HEAD, 2 * total, HEAD), F32)
    ]


def interior_call(blocks, weight, bias, frames, tiles, grid_rows, own):
    channels, width = weight.shape[2:]
    total = tiles * frames * own

    def kernel(blocks, weight, bias, out, taps, left, middle, right, wide):
        lay_taps(weight, taps)
        lay_rows(frames, tiles, grid_rows, own, range(grid_rows), blocks, None,
                 left, middle, right)
        for r in range(1, grid_rows - 1):
            decode_row(own, r - 1, bias, left, middle, right, taps, wide, out, 2 * (r - 1))

    return pl.pallas_call(
        kernel,
        out_shape=[
            shape((tiles * frames, 2 * (grid_rows - 2), 2 * own, width), BF16),
            shape((4, 4 * channels, width), BF16),
        ],
        in_specs=[IN_VMEM] * 3,
        out_specs=[IN_VMEM] * 2,
        scratch_shapes=decode_scratch(grid_rows, total, channels, width),
        name="interior",
        compiler_params=params(24),
    )(blocks, weight, bias)


def border_call(blocks, edge, interior, taps, bias, frames, tiles, grid_rows, own):
    channels = blocks.shape[2]
    width = taps.shape[2]
    total = tiles * frames * own
    last = 2 * (grid_rows - 1)

    def kernel(blocks, edge, interior, taps, bias, out, left, middle, right, wide, staged, sem):
        copies = [pltpu.make_async_copy(interior, out.at[:, pl.ds(2, last - 2)], sem.at[2])]
        copies[0].start()
        rows = [-1, 0, 1, grid_rows - 2, grid_rows - 1, grid_rows]
        lay_rows(frames, tiles, grid_rows, own, rows, blocks, edge, left, middle, right)
        for i, (index, row) in enumerate(((0, 0), (3, last))):
            decode_row(own, index, bias, left, middle, right, taps, wide, staged, 2 * i)
            copies.append(
                pltpu.make_async_copy(
                    staged.at[:, pl.ds(2 * i, 2)], out.at[:, pl.ds(row, 2)], sem.at[i]
                )
            )
            copies[-1].start()
        for c in copies:
            c.wait()

    return pl.pallas_call(
        kernel,
        out_shape=shape((tiles * frames, 2 * grid_rows, 2 * own, width), BF16),
        in_specs=[IN_VMEM] * 5,
        out_specs=IN_HBM,
        scratch_shapes=decode_scratch(6, total, channels, width)
        + [
            pltpu.VMEM((tiles * frames, 4, 2 * own, width), BF16),
            pltpu.SemaphoreType.DMA((3,)),
        ],
        name="border",
        compiler_params=params(24),
    )(blocks, edge, interior, taps, bias)


def round_call(step, last, got, total, carry):
    def kernel(got, total, *refs):
        upper = (lax.axis_index("tm") // step) % 2 == 1
        received = got[...].astype(F32)
        before = jnp.where(upper, received, 0.0)
        if carry is not None:
            before = refs[0][...] + before
            refs = refs[1:]
        if last:
            refs[0][...] = before.astype(BF16)
        else:
            carry_out, total_out, sent_out = refs
            carry_out[...] = before
            both = total[...] + received
            total_out[...] = both
            sent_out[...] = both.astype(BF16)

    near = [got, total] + ([] if carry is None else [carry])
    kinds = [BF16] if last else [F32, F32, BF16]
    return pl.pallas_call(
        kernel,
        out_shape=[shape(total.shape, kind) for kind in kinds],
        in_specs=[IN_VMEM] * len(near),
        out_specs=[IN_VMEM] * len(kinds),
        name="round",
        compiler_params=params(4),
    )(*near)


def prefix_rounds(total, sent, tiles):
    carry = None
    step, number = 1, 0
    while step < tiles:
        last = 2 * step >= tiles
        got = lax.ppermute(sent, "tm", [(i, i ^ step) for i in range(tiles)])
        out = round_call(step, last, got, total, carry)
        if last:
            return out[0]
        carry, total, sent = out
        step *= 2
        number += 1
    return jnp.zeros_like(sent)


SWAP = [(0, 1), (1, 0)]


def body(video, w_query, w_key, w_value, w_out, w_latent, conv_weight, conv_bias):
    frames, grid_rows, columns, d = video.shape
    tiles = lax.axis_size("tm")
    own = columns // tiles
    flat = video.reshape(-1, d)
    heads = d // HEAD
    split = heads - heads // 4 * 2
    parts_a, near, wk_b, wv_b, near_query = first_states(
        flat, w_key, w_value, w_query, frames, split
    )
    other_a = lax.ppermute(parts_a, "space", SWAP)
    parts_b, mine_b, theirs_b = second_states(near, wk_b, wv_b, frames)
    got_b = lax.ppermute(theirs_b, "space", SWAP)
    other_b = lax.ppermute(parts_b, "space", SWAP)
    total_a = total_call(parts_a, other_a)
    total_b = add_call(mine_b, got_b)

    ready = {}
    for name, first, parts, other, (total, sent) in (
        ("a", 0, parts_a, other_a, total_a), ("b", split, parts_b, other_b, total_b),
    ):
        count = parts.shape[1]
        cuts = [first, first + 2, first + count] if name == "a" else [first, first + count]
        queries = []
        for low, high in zip(cuts, cuts[1:]):
            queries.append(
                query_call(near, near_query, low * HEAD, (high - low) * HEAD)
            )
        carry = prefix_rounds(total, sent, tiles)
        other_carry = lax.ppermute(carry, "space", SWAP)
        ready[name] = (queries, parts, other, carry, other_carry)

    partial = partial_call(near, ready["a"], w_out, frames)
    chunk_b = (ready["b"][0][0],) + ready["b"][1:]
    partial = own_call(partial, chunk_b, w_out, frames)
    blocks = latent_call(partial, chunk_b, w_out, w_latent, frames, columns, tiles)
    blocks = lax.all_to_all(blocks, "tm", 0, 0, tiled=True)
    return decode(blocks, conv_weight, conv_bias, frames, grid_rows, own, tiles)


def decode(blocks, conv_weight, conv_bias, frames, grid_rows, own, tiles):
    channels = conv_weight.shape[2]
    width = conv_weight.shape[3]
    group = frames * own
    main = grid_rows * group

    def edge_kernel(blocks, out):
        def take(r):
            for t in range(tiles):
                out[t, :group] = blocks[t, r * group : (r + 1) * group]
                sides = blocks[t, main:].astype(F32)
                out[t, group:] = jnp.concatenate(
                    [sides[k * grid_rows + r : k * grid_rows + r + 1] for k in range(2 * frames)],
                    axis=0,
                ).astype(BF16)

        upper = lax.axis_index("space") == 0

        @pl.when(upper)
        def _():
            take(grid_rows - 1)

        @pl.when(jnp.logical_not(upper))
        def _():
            take(0)

    mine = pl.pallas_call(
        edge_kernel,
        out_shape=shape((tiles, group + 2 * frames, channels), BF16),
        in_specs=[IN_VMEM],
        out_specs=IN_VMEM,
        name="edge",
        compiler_params=params(4),
    )(blocks)
    beside = lax.ppermute(mine, "space", SWAP)
    bias = conv_bias.reshape(1, width)
    interior, taps = interior_call(
        blocks, conv_weight, bias, frames, tiles, grid_rows, own
    )
    return border_call(blocks, beside, interior, taps, bias, frames, tiles, grid_rows, own)


def solution(mesh):
    assert mesh.shape["space"] == 2
    tiles = mesh.shape["tm"]
    assert tiles & (tiles - 1) == 0
    placed = (P(("groups", "tm"), "space", None, None), P(), P(), P(), P(), P(), P(), P())
    return jax.shard_map(
        body,
        mesh=mesh,
        in_specs=placed,
        out_specs=P("groups", "space", "tm", None),
        check_vma=False,
    )
```

```python
import functools

import jax
import jax.numpy as jnp
from jax import lax
from jax.experimental import pallas as pl
from jax.experimental.pallas import tpu as pltpu
from jax.sharding import PartitionSpec as P


HEAD = 128
EPS = 1e-06
BF16 = jnp.bfloat16
F32 = jnp.float32


IN_HBM = pl.BlockSpec(memory_space=pltpu.HBM)
IN_VMEM = pl.BlockSpec(memory_space=pltpu.VMEM)


def shape(dims, dtype):
    return jax.ShapeDtypeStruct(dims, dtype)


def params(megabytes):
    return pltpu.CompilerParams(vmem_limit_bytes=megabytes << 20)


def in_hbm(x):
    return pltpu.with_memory_space_constraint(x, pltpu.HBM)


def matmul(a, b):
    return jnp.dot(a, b, preferred_element_type=F32)


def features(x):
    return jnp.where(x > 0.0, x + 1.0, jnp.exp(jnp.minimum(x, 0.0)))


def states_kernel(frames, heads, fetched, video_in, wk_hbm, wv_hbm, *refs):
    if fetched:
        parts_out, mine_out, theirs_out, key, value = refs
        video, wk, wv = video_in, wk_hbm, wv_hbm
        late = []
    else:
        (wq_hbm, parts_out, video, wk_out, wv_out, wq_out, wk, wv, key, value,
         wk_sem, wv_sem, video_sem, late_sem) = refs
        rest = wk_out.shape[1]
        source = pl.ds(heads * HEAD, rest)
        late = [
            pltpu.make_async_copy(wq_hbm, wq_out, late_sem.at[0]),
            pltpu.make_async_copy(wk_hbm.at[:, source], wk_out, late_sem.at[1]),
            pltpu.make_async_copy(wv_hbm.at[:, source], wv_out, late_sem.at[2]),
        ]
    per = video.shape[0] // frames

    def weight_copies(h):
        cols = pl.ds(pl.multiple_of(h * HEAD, HEAD), HEAD)
        return (
            pltpu.make_async_copy(wk_hbm.at[:, cols], wk.at[:, cols], wk_sem.at[h]),
            pltpu.make_async_copy(wv_hbm.at[:, cols], wv.at[:, cols], wv_sem.at[h]),
        )

    def video_copy(f):
        rows = pl.ds(f * per, per)
        return pltpu.make_async_copy(video_in.at[rows], video.at[rows], video_sem.at[f])

    if not fetched:
        soon = min(2, heads)
        for f in range(frames):
            video_copy(f).start()
        for h in range(soon):
            for c in weight_copies(h):
                c.start()
        for f in range(frames):
            video_copy(f).wait()
        for h in range(soon, heads):
            for c in weight_copies(h):
                c.start()
        for c in late:
            c.start()

    def one_head(h, carry):
        if not fetched:
            for c in weight_copies(h):
                c.wait()
        cols = pl.ds(pl.multiple_of(h * HEAD, HEAD), HEAD)
        both = jnp.concatenate([wk[:, cols], wv[:, cols]], axis=1)
        for f in range(frames):
            rows = slice(f * per, (f + 1) * per)
            kv = matmul(video[rows, :], both)
            key[h, rows, :] = features(kv[:, :HEAD]).astype(BF16)
            value[h, rows, :] = kv[:, HEAD:].astype(BF16)
        return carry

    lax.fori_loop(0, heads, one_head, 0)

    totals = []
    for h in range(heads):
        total = None
        for f in range(frames):
            rows = slice(f * per, (f + 1) * per)
            state = lax.dot_general(
                key[h, rows, :], value[h, rows, :], (((0,), (0,)), ((), ())),
                preferred_element_type=F32,
            )
            parts_out[f, h] = state.astype(BF16)
            total = state if total is None else total + state
        totals.append(total)
    if fetched:
        lower = lax.axis_index("space") == 0
        half = heads // 2
        for h in range(half):
            mine_out[h] = jnp.where(lower, totals[h], totals[half + h])
            theirs_out[h] = jnp.where(lower, totals[half + h], totals[h]).astype(BF16)
    for c in late:
        c.wait()


def first_states(video, wk, wv, wq, frames, heads):
    tokens, d = video.shape
    width = heads * HEAD
    return pl.pallas_call(
        functools.partial(states_kernel, frames, heads, False),
        out_shape=[
            shape((frames, heads, HEAD, HEAD), BF16),
            shape((tokens, d), BF16),
            shape((d, d - width), BF16),
            shape((d, d - width), BF16),
            shape((d, d), BF16),
        ],
        in_specs=[IN_HBM] * 4,
        out_specs=[IN_VMEM] * 5,
        scratch_shapes=[
            pltpu.VMEM((d, width), BF16),
            pltpu.VMEM((d, width), BF16),
            pltpu.VMEM((heads, tokens, HEAD), BF16),
            pltpu.VMEM((heads, tokens, HEAD), BF16),
            pltpu.SemaphoreType.DMA((heads,)),
            pltpu.SemaphoreType.DMA((heads,)),
            pltpu.SemaphoreType.DMA((frames,)),
            pltpu.SemaphoreType.DMA((3,)),
        ],
        name="states",
        compiler_params=params(20),
    )(in_hbm(video), in_hbm(wk), in_hbm(wv), in_hbm(wq))


def second_states(video, wk, wv, frames):
    tokens, _ = video.shape
    heads = wk.shape[1] // HEAD
    return pl.pallas_call(
        functools.partial(states_kernel, frames, heads, True),
        out_shape=[
            shape((frames, heads, HEAD, HEAD), BF16),
            shape((heads // 2, HEAD, HEAD), F32),
            shape((heads // 2, HEAD, HEAD), BF16),
        ],
        in_specs=[IN_VMEM] * 3,
        out_specs=[IN_VMEM] * 3,
        scratch_shapes=[
            pltpu.VMEM((heads, tokens, HEAD), BF16),
            pltpu.VMEM((heads, tokens, HEAD), BF16),
        ],
        name="states",
        compiler_params=params(20),
    )(video, wk, wv)


def total_call(parts, other_parts):
    frames, heads = parts.shape[:2]
    half = HEAD // 2

    def kernel(parts, other_parts, out, sent):
        low = lax.axis_index("space") == 0
        for h in range(heads):
            total = None
            for f in range(frames):
                one = parts[f, h].astype(F32) + other_parts[f, h].astype(F32)
                total = one if total is None else total + one
            total = jnp.where(low, total[:half], total[half:])
            out[h] = total
            sent[h] = total.astype(BF16)

    dims = (heads, half, HEAD)
    return pl.pallas_call(
        kernel,
        out_shape=[shape(dims, F32), shape(dims, BF16)],
        in_specs=[IN_VMEM] * 2,
        out_specs=[IN_VMEM] * 2,
        name="total",
        compiler_params=params(4),
    )(parts, other_parts)


def add_call(mine, got):
    def kernel(mine, got, out, sent):
        total = mine[...] + got[...].astype(F32)
        out[...] = total
        sent[...] = total.astype(BF16)

    return pl.pallas_call(
        kernel,
        out_shape=[shape(mine.shape, F32), shape(mine.shape, BF16)],
        in_specs=[IN_VMEM] * 2,
        out_specs=[IN_VMEM] * 2,
        name="add",
        compiler_params=params(4),
    )(mine, got)


def query_call(video, w, first, width):
    def kernel(video, w, out):
        out[...] = features(matmul(video[...], w[:, first : first + width])).astype(BF16)

    return pl.pallas_call(
        kernel,
        out_shape=shape((video.shape[0], width), BF16),
        in_specs=[IN_VMEM] * 2,
        out_specs=IN_VMEM,
        name="query",
        compiler_params=params(16),
    )(video, w)


def attend(frames, queries, parts, other_parts, carry, other_carry, used, head_out):
    heads = carry.shape[0]
    per = head_out.shape[0] // frames
    low = lax.axis_index("space") == 0
    used[...] = jnp.zeros_like(used)
    for h in range(heads):
        mine, theirs = carry[h].astype(F32), other_carry[h].astype(F32)
        running = jnp.concatenate(
            [jnp.where(low, mine, theirs), jnp.where(low, theirs, mine)], axis=0
        )
        at = (h % 2) * HEAD
        for f in range(frames):
            running = running + parts[f, h].astype(F32) + other_parts[f, h].astype(F32)
            used[f, h // 2, at : at + HEAD, at : at + HEAD] = running.astype(BF16)
    for f in range(frames):
        rows = slice(f * per, (f + 1) * per)
        for p in range(pl.cdiv(heads, 2)):
            width = min(2, heads - 2 * p) * HEAD
            first = 2 * p * HEAD
            query, at = queries[0], first
            for piece in queries[1:]:
                if at < query.shape[1]:
                    break
                query, at = piece, at - query.shape[1]
            attended = matmul(query[rows, at : at + width], used[f, p, :width, :width])
            for h in range(width // HEAD):
                one = attended[:, h * HEAD : (h + 1) * HEAD]
                scale = lax.rsqrt(jnp.mean(one * one, axis=1, keepdims=True) + EPS)
                at = first + h * HEAD
                head_out[rows, at : at + HEAD] = (one * scale).astype(BF16)


def used_shape(frames, heads):
    return pltpu.VMEM((frames, pl.cdiv(heads, 2), 2 * HEAD, 2 * HEAD), BF16)


def partial_call(video, chunk, w_out, frames):
    tokens, d = video.shape
    heads = chunk[3].shape[0]

    queries, chunk = chunk[0], chunk[1:]
    n = len(queries)

    def kernel(video, *refs):
        parts, other_parts, carry, other_carry, w_out, out, used, head_out = refs[n:]
        attend(frames, refs[:n], parts, other_parts, carry, other_carry, used, head_out)
        per = tokens // frames
        for f in range(frames):
            rows = slice(f * per, (f + 1) * per)
            out[rows, :] = video[rows, :].astype(F32) + matmul(
                head_out[rows, :], w_out[: heads * HEAD, :]
            )

    return pl.pallas_call(
        kernel,
        out_shape=shape((tokens, d), F32),
        in_specs=[IN_VMEM] * (n + 6),
        out_specs=IN_VMEM,
        scratch_shapes=[used_shape(frames, heads), pltpu.VMEM((tokens, heads * HEAD), BF16)],
        name="partial",
        compiler_params=params(20),
    )(video, *queries, *chunk, w_out)


def attend_half(frames, half, query, parts, other_parts, carry, used, head_out):
    heads = carry.shape[0]
    per = head_out.shape[0] // frames
    used[...] = jnp.zeros_like(used)
    for h in range(heads):
        running = carry[h].astype(F32)
        at = (h % 2) * HEAD
        for f in range(frames):
            own = half * heads + h
            running = running + parts[f, own].astype(F32) + other_parts[f, own].astype(F32)
            used[f, h // 2, at : at + HEAD, at : at + HEAD] = running.astype(BF16)
    for f in range(frames):
        rows = slice(f * per, (f + 1) * per)
        for p in range(pl.cdiv(heads, 2)):
            width = min(2, heads - 2 * p) * HEAD
            first = 2 * p * HEAD
            cols = pl.ds(pl.multiple_of(half * heads * HEAD + first, HEAD), width)
            attended = matmul(query[rows, cols], used[f, p, :width, :width])
            for h in range(width // HEAD):
                one = attended[:, h * HEAD : (h + 1) * HEAD]
                scale = lax.rsqrt(jnp.mean(one * one, axis=1, keepdims=True) + EPS)
                at = first + h * HEAD
                head_out[rows, at : at + HEAD] = (one * scale).astype(BF16)


def half_rows(w_out, half, width):
    first = w_out.shape[0] - 2 * width
    return w_out[pl.ds(pl.multiple_of(first + half * width, HEAD), width), :]


def own_call(partial, chunk, w_out, frames):
    query, parts, other_parts, carry, _ = chunk
    tokens, d = partial.shape
    heads = carry.shape[0]
    width = heads * HEAD

    def kernel(partial, query, parts, other_parts, carry, w_out, out, used, head_out):
        half = lax.axis_index("space")
        attend_half(frames, half, query, parts, other_parts, carry, used, head_out)
        w = half_rows(w_out, half, width)
        per = tokens // frames
        for f in range(frames):
            rows = slice(f * per, (f + 1) * per)
            out[rows, :] = partial[rows, :] + matmul(head_out[rows, :], w)

    return pl.pallas_call(
        kernel,
        out_shape=shape((tokens, d), F32),
        in_specs=[IN_VMEM] * 6,
        out_specs=IN_VMEM,
        scratch_shapes=[used_shape(frames, heads), pltpu.VMEM((tokens, width), BF16)],
        name="own",
        compiler_params=params(20),
    )(partial, query, parts, other_parts, carry, w_out)


def latent_kernel(
    frames, columns, tiles, partial, query, parts, other_parts, carry,
    w_out, w_latent, out, used, head_out, latent,
):
    tokens, _ = partial.shape
    per = tokens // frames
    half = 1 - lax.axis_index("space")
    attend_half(frames, half, query, parts, other_parts, carry, used, head_out)
    w = half_rows(w_out, half, head_out.shape[1])
    for f in range(frames):
        rows = slice(f * per, (f + 1) * per)
        summed = partial[rows, :] + matmul(head_out[rows, :], w)
        scale = lax.rsqrt(jnp.mean(summed * summed, axis=1, keepdims=True) + EPS)
        latent[rows, :] = matmul(summed.astype(BF16), w_latent[...]) * scale

    own = columns // tiles
    grid_rows = per // columns
    main = grid_rows * frames * own
    for t in range(tiles):
        for r in range(grid_rows):
            block = [
                latent[pl.ds(f * per + r * columns + t * own, own), :] for f in range(frames)
            ]
            at = r * frames * own
            out[t, at : at + frames * own, :] = jnp.concatenate(block, axis=0).astype(BF16)
        sides = []
        for column in (t * own - 1, (t + 1) * own):
            for f in range(frames):
                if 0 <= column < columns:
                    at = f * per + column
                    sides.append(latent[pl.ds(at, grid_rows, stride=columns), :])
                else:
                    sides.append(jnp.zeros((grid_rows, out.shape[2]), F32))
        out[t, main:, :] = jnp.concatenate(sides, axis=0).astype(BF16)


def latent_call(partial, chunk, w_out, w_latent, frames, columns, tiles):
    query, parts, other_parts, _, other_carry = chunk
    tokens, _ = partial.shape
    channels = w_latent.shape[1]
    heads = other_carry.shape[0]
    rows = tokens // columns * (columns // tiles + 2)
    return pl.pallas_call(
        functools.partial(latent_kernel, frames, columns, tiles),
        out_shape=shape((tiles, rows, channels), BF16),
        in_specs=[IN_VMEM] * 7,
        out_specs=IN_VMEM,
        scratch_shapes=[
            used_shape(frames, heads),
            pltpu.VMEM((tokens, heads * HEAD), BF16),
            pltpu.VMEM((tokens, channels), F32),
        ],
        name="latent",
        compiler_params=params(20),
    )(partial, query, parts, other_parts, other_carry, w_out, w_latent)


def lay_rows(frames, tiles, grid_rows, own, rows, blocks, edge, left, middle, right):
    group = frames * own
    main = grid_rows * group
    channels = left.shape[-1]
    column = lax.broadcasted_iota(jnp.int32, (group, 1), 0) % own

    def lay(index, t, body, sides):
        at = slice(t * group, (t + 1) * group)
        first, last = (
            jnp.concatenate(
                [jnp.broadcast_to(sides[k : k + 1], (own, channels))
                 for k in range(side * frames, (side + 1) * frames)], axis=0
            )
            for side in range(2)
        )
        down = pltpu.roll(body, 1, 0)
        up = pltpu.roll(body, group - 1, 0)
        left[index, at, :] = jnp.where(column == 0, first, down).astype(BF16)
        middle[index, at, :] = body.astype(BF16)
        right[index, at, :] = jnp.where(column == own - 1, last, up).astype(BF16)

    for t in range(tiles):
        everything = blocks[t].astype(F32)
        beside = None if edge is None else edge[t].astype(F32)
        for index, row in enumerate(rows):
            if 0 <= row < grid_rows:
                sides = [
                    everything[main + k * grid_rows + row : main + k * grid_rows + row + 1]
                    for k in range(2 * frames)
                ]
                lay(index, t, everything[row * group : (row + 1) * group],
                    jnp.concatenate(sides, axis=0))
            else:
                present = lax.axis_index("space") == (1 if row < 0 else 0)
                there = jnp.where(present, beside, 0.0)
                lay(index, t, there[:group], there[group:])


def lay_taps(weight, taps):
    w = weight[...].astype(F32)
    channels = weight.shape[2]
    row_sets = (((0,), (1, 2)), ((0, 1), (2,)))
    for a in range(2):
        for b in range(2):
            for i, rows in enumerate(row_sets[a]):
                for j, cols in enumerate(row_sets[b]):
                    tap = sum(w[r, c] for r in rows for c in cols)
                    at = (2 * i + j) * channels
                    taps[2 * a + b, at : at + channels, :] = (0.5 * tap).astype(BF16)


def decode_rows(own, index, count, bias, left, middle, right, taps, wide, staged, first):
    views = ((left, middle), (middle, right))
    half_bias = 0.5 * bias[...]
    lanes = wide.shape[-1]
    total, channels = left.shape[1:]
    size = count * total
    for a in range(2):
        for b in range(2):
            lhs = jnp.concatenate(
                [v[index + a + k : index + a + k + count].reshape(size, channels)
                 for k in range(2) for v in views[b]], axis=1
            )
            h = matmul(lhs, taps[2 * a + b]) + half_bias
            value = h + h * jnp.tanh(h)
            for n in range(wide.shape[1]):
                wide[a, n, pl.ds(b, size, stride=2), :] = value[:, n * lanes : (n + 1) * lanes]
        for n in range(wide.shape[1]):
            shaped = wide[a, n].reshape(count, total // own, 2 * own, lanes)
            for r in range(count):
                staged[:, first + 2 * r + a, :, n * lanes : (n + 1) * lanes] = (
                    shaped[r].astype(BF16)
                )


def decode_scratch(rows, count, total, channels, width):
    return [pltpu.VMEM((rows, total, channels), BF16)] * 3 + [
        pltpu.VMEM((2, width // HEAD, 2 * count * total, HEAD), F32)
    ]


def interior_call(blocks, weight, bias, frames, tiles, grid_rows, own):
    channels, width = weight.shape[2:]
    total = tiles * frames * own
    count = 3 if (grid_rows - 2) % 3 == 0 else 1

    def kernel(blocks, weight, bias, out, taps, left, middle, right, wide):
        lay_taps(weight, taps)
        lay_rows(frames, tiles, grid_rows, own, range(grid_rows), blocks, None,
                 left, middle, right)
        for i in range(0, grid_rows - 2, count):
            decode_rows(own, i, count, bias, left, middle, right, taps, wide, out, 2 * i)

    return pl.pallas_call(
        kernel,
        out_shape=[
            shape((tiles * frames, 2 * (grid_rows - 2), 2 * own, width), BF16),
            shape((4, 4 * channels, width), BF16),
        ],
        in_specs=[IN_VMEM] * 3,
        out_specs=[IN_VMEM] * 2,
        scratch_shapes=decode_scratch(grid_rows, count, total, channels, width),
        name="interior",
        compiler_params=params(24),
    )(blocks, weight, bias)


def border_call(blocks, edge, interior, taps, bias, frames, tiles, grid_rows, own):
    channels = blocks.shape[2]
    width = taps.shape[2]
    total = tiles * frames * own
    last = 2 * (grid_rows - 1)

    def kernel(blocks, edge, interior, taps, bias, out, left, middle, right, wide, staged, sem):
        copies = [pltpu.make_async_copy(interior, out.at[:, pl.ds(2, last - 2)], sem.at[2])]
        copies[0].start()
        rows = [-1, 0, 1, grid_rows - 2, grid_rows - 1, grid_rows]
        lay_rows(frames, tiles, grid_rows, own, rows, blocks, edge, left, middle, right)
        for i, (index, row) in enumerate(((0, 0), (3, last))):
            decode_rows(own, index, 1, bias, left, middle, right, taps, wide, staged, 2 * i)
            copies.append(
                pltpu.make_async_copy(
                    staged.at[:, pl.ds(2 * i, 2)], out.at[:, pl.ds(row, 2)], sem.at[i]
                )
            )
            copies[-1].start()
        for c in copies:
            c.wait()

    return pl.pallas_call(
        kernel,
        out_shape=shape((tiles * frames, 2 * grid_rows, 2 * own, width), BF16),
        in_specs=[IN_VMEM] * 5,
        out_specs=IN_HBM,
        scratch_shapes=decode_scratch(6, 1, total, channels, width)
        + [
            pltpu.VMEM((tiles * frames, 4, 2 * own, width), BF16),
            pltpu.SemaphoreType.DMA((3,)),
        ],
        name="border",
        compiler_params=params(24),
    )(blocks, edge, interior, taps, bias)


def round_call(step, last, got, total, carry):
    def kernel(got, total, *refs):
        upper = (lax.axis_index("tm") // step) % 2 == 1
        received = got[...].astype(F32)
        before = jnp.where(upper, received, 0.0)
        if carry is not None:
            before = refs[0][...] + before
            refs = refs[1:]
        if last:
            refs[0][...] = before.astype(BF16)
        else:
            carry_out, total_out, sent_out = refs
            carry_out[...] = before
            both = total[...] + received
            total_out[...] = both
            sent_out[...] = both.astype(BF16)

    near = [got, total] + ([] if carry is None else [carry])
    kinds = [BF16] if last else [F32, F32, BF16]
    return pl.pallas_call(
        kernel,
        out_shape=[shape(total.shape, kind) for kind in kinds],
        in_specs=[IN_VMEM] * len(near),
        out_specs=[IN_VMEM] * len(kinds),
        name="round",
        compiler_params=params(4),
    )(*near)


def prefix_rounds(total, sent, tiles):
    carry = None
    step, number = 1, 0
    while step < tiles:
        last = 2 * step >= tiles
        got = lax.ppermute(sent, "tm", [(i, i ^ step) for i in range(tiles)])
        out = round_call(step, last, got, total, carry)
        if last:
            return out[0]
        carry, total, sent = out
        step *= 2
        number += 1
    return jnp.zeros_like(sent)


SWAP = [(0, 1), (1, 0)]


def body(video, w_query, w_key, w_value, w_out, w_latent, conv_weight, conv_bias):
    frames, grid_rows, columns, d = video.shape
    tiles = lax.axis_size("tm")
    own = columns // tiles
    flat = video.reshape(-1, d)
    heads = d // HEAD
    split = heads - heads // 4 * 2
    parts_a, near, wk_b, wv_b, near_query = first_states(
        flat, w_key, w_value, w_query, frames, split
    )
    other_a = lax.ppermute(parts_a, "space", SWAP)
    parts_b, mine_b, theirs_b = second_states(near, wk_b, wv_b, frames)
    got_b = lax.ppermute(theirs_b, "space", SWAP)
    other_b = lax.ppermute(parts_b, "space", SWAP)
    total_a = total_call(parts_a, other_a)
    total_b = add_call(mine_b, got_b)

    ready = {}
    for name, first, parts, other, (total, sent) in (
        ("a", 0, parts_a, other_a, total_a), ("b", split, parts_b, other_b, total_b),
    ):
        count = parts.shape[1]
        cuts = [first, first + 2, first + count] if name == "a" else [first, first + count]
        queries = []
        for low, high in zip(cuts, cuts[1:]):
            queries.append(
                query_call(near, near_query, low * HEAD, (high - low) * HEAD)
            )
        carry = prefix_rounds(total, sent, tiles)
        other_carry = lax.ppermute(carry, "space", SWAP)
        ready[name] = (queries, parts, other, carry, other_carry)

    partial = partial_call(near, ready["a"], w_out, frames)
    chunk_b = (ready["b"][0][0],) + ready["b"][1:]
    partial = own_call(partial, chunk_b, w_out, frames)
    blocks = latent_call(partial, chunk_b, w_out, w_latent, frames, columns, tiles)
    blocks = lax.all_to_all(blocks, "tm", 0, 0, tiled=True)
    return decode(blocks, conv_weight, conv_bias, frames, grid_rows, own, tiles)


def decode(blocks, conv_weight, conv_bias, frames, grid_rows, own, tiles):
    channels = conv_weight.shape[2]
    width = conv_weight.shape[3]
    group = frames * own
    main = grid_rows * group

    def edge_kernel(blocks, out):
        def take(r):
            for t in range(tiles):
                out[t, :group] = blocks[t, r * group : (r + 1) * group]
                sides = blocks[t, main:].astype(F32)
                out[t, group:] = jnp.concatenate(
                    [sides[k * grid_rows + r : k * grid_rows + r + 1] for k in range(2 * frames)],
                    axis=0,
                ).astype(BF16)

        upper = lax.axis_index("space") == 0

        @pl.when(upper)
        def _():
            take(grid_rows - 1)

        @pl.when(jnp.logical_not(upper))
        def _():
            take(0)

    mine = pl.pallas_call(
        edge_kernel,
        out_shape=shape((tiles, group + 2 * frames, channels), BF16),
        in_specs=[IN_VMEM],
        out_specs=IN_VMEM,
        name="edge",
        compiler_params=params(4),
    )(blocks)
    beside = lax.ppermute(mine, "space", SWAP)
    bias = conv_bias.reshape(1, width)
    interior, taps = interior_call(
        blocks, conv_weight, bias, frames, tiles, grid_rows, own
    )
    return border_call(blocks, beside, interior, taps, bias, frames, tiles, grid_rows, own)


def solution(mesh):
    assert mesh.shape["space"] == 2
    tiles = mesh.shape["tm"]
    assert tiles & (tiles - 1) == 0
    placed = (P(("groups", "tm"), "space", None, None), P(), P(), P(), P(), P(), P(), P())
    return jax.shard_map(
        body,
        mesh=mesh,
        in_specs=placed,
        out_specs=P("groups", "space", "tm", None),
        check_vma=False,
    )
```

```python
import functools

import jax
import jax.numpy as jnp
from jax import lax
from jax.experimental import pallas as pl
from jax.experimental.pallas import tpu as pltpu
from jax.sharding import PartitionSpec as P


HEAD = 128
EPS = 1e-06
BF16 = jnp.bfloat16
F32 = jnp.float32


IN_HBM = pl.BlockSpec(memory_space=pltpu.HBM)
IN_VMEM = pl.BlockSpec(memory_space=pltpu.VMEM)


def shape(dims, dtype):
    return jax.ShapeDtypeStruct(dims, dtype)


def params(megabytes):
    return pltpu.CompilerParams(vmem_limit_bytes=megabytes << 20)


def in_hbm(x):
    return pltpu.with_memory_space_constraint(x, pltpu.HBM)


def matmul(a, b):
    return jnp.dot(a, b, preferred_element_type=F32)


def features(x):
    return jnp.where(x > 0.0, x + 1.0, jnp.exp(jnp.minimum(x, 0.0)))


def states_kernel(frames, heads, fetched, video_in, wk_hbm, wv_hbm, *refs):
    if fetched:
        parts_out, mine_out, theirs_out, key, value = refs
        video, wk, wv = video_in, wk_hbm, wv_hbm
        late = []
    else:
        (wq_hbm, parts_out, video, wk_out, wv_out, wq_out, wk, wv, key, value,
         wk_sem, wv_sem, video_sem, late_sem) = refs
        rest = wk_out.shape[1]
        source = pl.ds(heads * HEAD, rest)
        late = [
            pltpu.make_async_copy(wk_hbm.at[:, source], wk_out, late_sem.at[1]),
            pltpu.make_async_copy(wv_hbm.at[:, source], wv_out, late_sem.at[2]),
            pltpu.make_async_copy(wq_hbm, wq_out, late_sem.at[0]),
        ]
    per = video.shape[0] // frames

    def weight_copies(h):
        cols = pl.ds(pl.multiple_of(h * HEAD, HEAD), HEAD)
        return (
            pltpu.make_async_copy(wk_hbm.at[:, cols], wk.at[:, cols], wk_sem.at[h]),
            pltpu.make_async_copy(wv_hbm.at[:, cols], wv.at[:, cols], wv_sem.at[h]),
        )

    def video_copy(f):
        rows = pl.ds(f * per, per)
        return pltpu.make_async_copy(video_in.at[rows], video.at[rows], video_sem.at[f])

    if not fetched:
        soon = min(2, heads)
        for f in range(frames):
            video_copy(f).start()
        for h in range(soon):
            for c in weight_copies(h):
                c.start()
        for f in range(frames):
            video_copy(f).wait()
        for h in range(soon, heads):
            for c in weight_copies(h):
                c.start()
        for c in late:
            c.start()

    def one_head(h, carry):
        if not fetched:
            for c in weight_copies(h):
                c.wait()
        cols = pl.ds(pl.multiple_of(h * HEAD, HEAD), HEAD)
        both = jnp.concatenate([wk[:, cols], wv[:, cols]], axis=1)
        for f in range(frames):
            rows = slice(f * per, (f + 1) * per)
            kv = matmul(video[rows, :], both)
            key[h, rows, :] = features(kv[:, :HEAD]).astype(BF16)
            value[h, rows, :] = kv[:, HEAD:].astype(BF16)
        return carry

    lax.fori_loop(0, heads, one_head, 0, unroll=2 if heads % 2 == 0 else 1)

    totals = []
    for h in range(heads):
        total = None
        for f in range(frames):
            rows = slice(f * per, (f + 1) * per)
            state = lax.dot_general(
                key[h, rows, :], value[h, rows, :], (((0,), (0,)), ((), ())),
                preferred_element_type=F32,
            )
            parts_out[f, h] = state.astype(BF16)
            total = state if total is None else total + state
        totals.append(total)
    if fetched:
        lower = lax.axis_index("space") == 0
        half = heads // 2
        for h in range(half):
            mine_out[h] = jnp.where(lower, totals[h], totals[half + h])
            theirs_out[h] = jnp.where(lower, totals[half + h], totals[h]).astype(BF16)
    for c in late:
        c.wait()


def first_states(video, wk, wv, wq, frames, heads):
    tokens, d = video.shape
    width = heads * HEAD
    return pl.pallas_call(
        functools.partial(states_kernel, frames, heads, False),
        out_shape=[
            shape((frames, heads, HEAD, HEAD), BF16),
            shape((tokens, d), BF16),
            shape((d, d - width), BF16),
            shape((d, d - width), BF16),
            shape((d, d), BF16),
        ],
        in_specs=[IN_HBM] * 4,
        out_specs=[IN_VMEM] * 5,
        scratch_shapes=[
            pltpu.VMEM((d, width), BF16),
            pltpu.VMEM((d, width), BF16),
            pltpu.VMEM((heads, tokens, HEAD), BF16),
            pltpu.VMEM((heads, tokens, HEAD), BF16),
            pltpu.SemaphoreType.DMA((heads,)),
            pltpu.SemaphoreType.DMA((heads,)),
            pltpu.SemaphoreType.DMA((frames,)),
            pltpu.SemaphoreType.DMA((3,)),
        ],
        name="states",
        compiler_params=params(20),
    )(in_hbm(video), in_hbm(wk), in_hbm(wv), in_hbm(wq))


def second_states(video, wk, wv, frames):
    tokens, _ = video.shape
    heads = wk.shape[1] // HEAD
    return pl.pallas_call(
        functools.partial(states_kernel, frames, heads, True),
        out_shape=[
            shape((frames, heads, HEAD, HEAD), BF16),
            shape((heads // 2, HEAD, HEAD), F32),
            shape((heads // 2, HEAD, HEAD), BF16),
        ],
        in_specs=[IN_VMEM] * 3,
        out_specs=[IN_VMEM] * 3,
        scratch_shapes=[
            pltpu.VMEM((heads, tokens, HEAD), BF16),
            pltpu.VMEM((heads, tokens, HEAD), BF16),
        ],
        name="states",
        compiler_params=params(20),
    )(video, wk, wv)


def total_call(parts, other_parts):
    frames, heads = parts.shape[:2]
    half = HEAD // 2

    def kernel(parts, other_parts, out, sent):
        low = lax.axis_index("space") == 0
        for h in range(heads):
            total = None
            for f in range(frames):
                one = parts[f, h].astype(F32) + other_parts[f, h].astype(F32)
                total = one if total is None else total + one
            total = jnp.where(low, total[:half], total[half:])
            out[h] = total
            sent[h] = total.astype(BF16)

    dims = (heads, half, HEAD)
    return pl.pallas_call(
        kernel,
        out_shape=[shape(dims, F32), shape(dims, BF16)],
        in_specs=[IN_VMEM] * 2,
        out_specs=[IN_VMEM] * 2,
        name="total",
        compiler_params=params(4),
    )(parts, other_parts)


def add_call(mine, got):
    def kernel(mine, got, out, sent):
        total = mine[...] + got[...].astype(F32)
        out[...] = total
        sent[...] = total.astype(BF16)

    return pl.pallas_call(
        kernel,
        out_shape=[shape(mine.shape, F32), shape(mine.shape, BF16)],
        in_specs=[IN_VMEM] * 2,
        out_specs=[IN_VMEM] * 2,
        name="add",
        compiler_params=params(4),
    )(mine, got)


def query_call(video, w, first, width):
    def kernel(video, w, out):
        out[...] = features(matmul(video[...], w[:, first : first + width])).astype(BF16)

    return pl.pallas_call(
        kernel,
        out_shape=shape((video.shape[0], width), BF16),
        in_specs=[IN_VMEM] * 2,
        out_specs=IN_VMEM,
        name="query",
        compiler_params=params(16),
    )(video, w)


def attend(frames, queries, parts, other_parts, carry, other_carry, used, head_out):
    heads = carry.shape[0]
    per = head_out.shape[0] // frames
    low = lax.axis_index("space") == 0
    used[...] = jnp.zeros_like(used)
    for h in range(heads):
        mine, theirs = carry[h].astype(F32), other_carry[h].astype(F32)
        running = jnp.concatenate(
            [jnp.where(low, mine, theirs), jnp.where(low, theirs, mine)], axis=0
        )
        at = (h % 2) * HEAD
        for f in range(frames):
            running = running + parts[f, h].astype(F32) + other_parts[f, h].astype(F32)
            used[f, h // 2, at : at + HEAD, at : at + HEAD] = running.astype(BF16)
    for f in range(frames):
        rows = slice(f * per, (f + 1) * per)
        for p in range(pl.cdiv(heads, 2)):
            width = min(2, heads - 2 * p) * HEAD
            first = 2 * p * HEAD
            query, at = queries[0], first
            for piece in queries[1:]:
                if at < query.shape[1]:
                    break
                query, at = piece, at - query.shape[1]
            attended = matmul(query[rows, at : at + width], used[f, p, :width, :width])
            for h in range(width // HEAD):
                one = attended[:, h * HEAD : (h + 1) * HEAD]
                scale = lax.rsqrt(jnp.mean(one * one, axis=1, keepdims=True) + EPS)
                at = first + h * HEAD
                head_out[rows, at : at + HEAD] = (one * scale).astype(BF16)


def used_shape(frames, heads):
    return pltpu.VMEM((frames, pl.cdiv(heads, 2), 2 * HEAD, 2 * HEAD), BF16)


def partial_call(video, chunk, w_out, frames):
    tokens, d = video.shape
    heads = chunk[3].shape[0]

    queries, chunk = chunk[0], chunk[1:]
    n = len(queries)

    def kernel(video, *refs):
        parts, other_parts, carry, other_carry, w_out, out, used, head_out = refs[n:]
        attend(frames, refs[:n], parts, other_parts, carry, other_carry, used, head_out)
        per = tokens // frames
        for f in range(frames):
            rows = slice(f * per, (f + 1) * per)
            out[rows, :] = video[rows, :].astype(F32) + matmul(
                head_out[rows, :], w_out[: heads * HEAD, :]
            )

    return pl.pallas_call(
        kernel,
        out_shape=shape((tokens, d), F32),
        in_specs=[IN_VMEM] * (n + 6),
        out_specs=IN_VMEM,
        scratch_shapes=[used_shape(frames, heads), pltpu.VMEM((tokens, heads * HEAD), BF16)],
        name="partial",
        compiler_params=params(20),
    )(video, *queries, *chunk, w_out)


def attend_half(frames, half, query, parts, other_parts, carry, used, head_out):
    heads = carry.shape[0]
    per = head_out.shape[0] // frames
    used[...] = jnp.zeros_like(used)
    for h in range(heads):
        running = carry[h].astype(F32)
        at = (h % 2) * HEAD
        for f in range(frames):
            own = half * heads + h
            running = running + parts[f, own].astype(F32) + other_parts[f, own].astype(F32)
            used[f, h // 2, at : at + HEAD, at : at + HEAD] = running.astype(BF16)
    for f in range(frames):
        rows = slice(f * per, (f + 1) * per)
        for p in range(pl.cdiv(heads, 2)):
            width = min(2, heads - 2 * p) * HEAD
            first = 2 * p * HEAD
            cols = pl.ds(pl.multiple_of(half * heads * HEAD + first, HEAD), width)
            attended = matmul(query[rows, cols], used[f, p, :width, :width])
            for h in range(width // HEAD):
                one = attended[:, h * HEAD : (h + 1) * HEAD]
                scale = lax.rsqrt(jnp.mean(one * one, axis=1, keepdims=True) + EPS)
                at = first + h * HEAD
                head_out[rows, at : at + HEAD] = (one * scale).astype(BF16)


def half_rows(w_out, half, width):
    first = w_out.shape[0] - 2 * width
    return w_out[pl.ds(pl.multiple_of(first + half * width, HEAD), width), :]


def own_call(partial, chunk, w_out, frames):
    query, parts, other_parts, carry, _ = chunk
    tokens, d = partial.shape
    heads = carry.shape[0]
    width = heads * HEAD

    def kernel(partial, query, parts, other_parts, carry, w_out, out, used, head_out):
        half = lax.axis_index("space")
        attend_half(frames, half, query, parts, other_parts, carry, used, head_out)
        w = half_rows(w_out, half, width)
        per = tokens // frames
        for f in range(frames):
            rows = slice(f * per, (f + 1) * per)
            out[rows, :] = partial[rows, :] + matmul(head_out[rows, :], w)

    return pl.pallas_call(
        kernel,
        out_shape=shape((tokens, d), F32),
        in_specs=[IN_VMEM] * 6,
        out_specs=IN_VMEM,
        scratch_shapes=[used_shape(frames, heads), pltpu.VMEM((tokens, width), BF16)],
        name="own",
        compiler_params=params(20),
    )(partial, query, parts, other_parts, carry, w_out)


def latent_kernel(
    frames, columns, tiles, partial, query, parts, other_parts, carry,
    w_out, w_latent, out, used, head_out, latent,
):
    tokens, _ = partial.shape
    per = tokens // frames
    half = 1 - lax.axis_index("space")
    attend_half(frames, half, query, parts, other_parts, carry, used, head_out)
    w = half_rows(w_out, half, head_out.shape[1])
    piece = per // 2
    for i in range(2 * frames):
        rows = slice(i * piece, (i + 1) * piece)
        summed = partial[rows, :] + matmul(head_out[rows, :], w)
        scale = lax.rsqrt(jnp.mean(summed * summed, axis=1, keepdims=True) + EPS)
        latent[rows, :] = matmul(summed.astype(BF16), w_latent[...]) * scale

    own = columns // tiles
    grid_rows = per // columns
    main = grid_rows * frames * own
    for t in range(tiles):
        for r in range(grid_rows):
            block = [
                latent[pl.ds(f * per + r * columns + t * own, own), :] for f in range(frames)
            ]
            at = r * frames * own
            out[t, at : at + frames * own, :] = jnp.concatenate(block, axis=0).astype(BF16)
        sides = []
        for column in (t * own - 1, (t + 1) * own):
            for f in range(frames):
                if 0 <= column < columns:
                    at = f * per + column
                    sides.append(latent[pl.ds(at, grid_rows, stride=columns), :])
                else:
                    sides.append(jnp.zeros((grid_rows, out.shape[2]), F32))
        out[t, main:, :] = jnp.concatenate(sides, axis=0).astype(BF16)


def latent_call(partial, chunk, w_out, w_latent, frames, columns, tiles):
    query, parts, other_parts, _, other_carry = chunk
    tokens, _ = partial.shape
    channels = w_latent.shape[1]
    heads = other_carry.shape[0]
    rows = tokens // columns * (columns // tiles + 2)
    return pl.pallas_call(
        functools.partial(latent_kernel, frames, columns, tiles),
        out_shape=shape((tiles, rows, channels), BF16),
        in_specs=[IN_VMEM] * 7,
        out_specs=IN_VMEM,
        scratch_shapes=[
            used_shape(frames, heads),
            pltpu.VMEM((tokens, heads * HEAD), BF16),
            pltpu.VMEM((tokens, channels), F32),
        ],
        name="latent",
        compiler_params=params(20),
    )(partial, query, parts, other_parts, other_carry, w_out, w_latent)


def lay_rows(frames, tiles, grid_rows, own, rows, blocks, edge, left, middle, right):
    group = frames * own
    main = grid_rows * group
    channels = left.shape[-1]
    column = lax.broadcasted_iota(jnp.int32, (group, 1), 0) % own

    def lay(index, t, body, sides):
        at = slice(t * group, (t + 1) * group)
        first, last = (
            jnp.concatenate(
                [jnp.broadcast_to(sides[k : k + 1], (own, channels))
                 for k in range(side * frames, (side + 1) * frames)], axis=0
            )
            for side in range(2)
        )
        down = pltpu.roll(body, 1, 0)
        up = pltpu.roll(body, group - 1, 0)
        left[index, at, :] = jnp.where(column == 0, first, down).astype(BF16)
        middle[index, at, :] = body.astype(BF16)
        right[index, at, :] = jnp.where(column == own - 1, last, up).astype(BF16)

    for t in range(tiles):
        everything = blocks[t].astype(F32)
        beside = None if edge is None else edge[t].astype(F32)
        for index, row in enumerate(rows):
            if 0 <= row < grid_rows:
                sides = [
                    everything[main + k * grid_rows + row : main + k * grid_rows + row + 1]
                    for k in range(2 * frames)
                ]
                lay(index, t, everything[row * group : (row + 1) * group],
                    jnp.concatenate(sides, axis=0))
            else:
                present = lax.axis_index("space") == (1 if row < 0 else 0)
                there = jnp.where(present, beside, 0.0)
                lay(index, t, there[:group], there[group:])


def lay_taps(weight, taps):
    w = weight[...].astype(F32)
    channels = weight.shape[2]
    row_sets = (((0,), (1, 2)), ((0, 1), (2,)))
    for a in range(2):
        for b in range(2):
            for i, rows in enumerate(row_sets[a]):
                for j, cols in enumerate(row_sets[b]):
                    tap = sum(w[r, c] for r in rows for c in cols)
                    at = (2 * i + j) * channels
                    taps[2 * a + b, at : at + channels, :] = (0.5 * tap).astype(BF16)


def decode_rows(own, index, count, bias, left, middle, right, taps, wide, staged, first):
    views = ((left, middle), (middle, right))
    half_bias = 0.5 * bias[...]
    lanes = wide.shape[-1]
    total, channels = left.shape[1:]
    size = count * total
    for a in range(2):
        for b in range(2):
            lhs = jnp.concatenate(
                [v[index + a + k : index + a + k + count].reshape(size, channels)
                 for k in range(2) for v in views[b]], axis=1
            )
            h = matmul(lhs, taps[2 * a + b]) + half_bias
            value = h + h * jnp.tanh(h)
            for n in range(wide.shape[1]):
                wide[a, n, pl.ds(b, size, stride=2), :] = value[:, n * lanes : (n + 1) * lanes]
        for n in range(wide.shape[1]):
            shaped = wide[a, n].reshape(count, total // own, 2 * own, lanes)
            for r in range(count):
                staged[:, first + 2 * r + a, :, n * lanes : (n + 1) * lanes] = (
                    shaped[r].astype(BF16)
                )


def decode_scratch(rows, count, total, channels, width):
    return [pltpu.VMEM((rows, total, channels), BF16)] * 3 + [
        pltpu.VMEM((2, width // HEAD, 2 * count * total, HEAD), F32)
    ]


def interior_call(blocks, weight, bias, frames, tiles, grid_rows, own):
    channels, width = weight.shape[2:]
    total = tiles * frames * own
    count = 3 if (grid_rows - 2) % 3 == 0 else 1

    def kernel(blocks, weight, bias, out, taps, left, middle, right, wide):
        lay_taps(weight, taps)
        lay_rows(frames, tiles, grid_rows, own, range(grid_rows), blocks, None,
                 left, middle, right)
        for i in range(0, grid_rows - 2, count):
            decode_rows(own, i, count, bias, left, middle, right, taps, wide, out, 2 * i)

    return pl.pallas_call(
        kernel,
        out_shape=[
            shape((tiles * frames, 2 * (grid_rows - 2), 2 * own, width), BF16),
            shape((4, 4 * channels, width), BF16),
        ],
        in_specs=[IN_VMEM] * 3,
        out_specs=[IN_VMEM] * 2,
        scratch_shapes=decode_scratch(grid_rows, count, total, channels, width),
        name="interior",
        compiler_params=params(24),
    )(blocks, weight, bias)


def border_call(blocks, edge, interior, taps, bias, frames, tiles, grid_rows, own):
    channels = blocks.shape[2]
    width = taps.shape[2]
    total = tiles * frames * own
    last = 2 * (grid_rows - 1)

    def kernel(blocks, edge, interior, taps, bias, out, left, middle, right, wide, staged, sem):
        copies = [pltpu.make_async_copy(interior, out.at[:, pl.ds(2, last - 2)], sem.at[2])]
        copies[0].start()
        rows = [-1, 0, 1, grid_rows - 2, grid_rows - 1, grid_rows]
        lay_rows(frames, tiles, grid_rows, own, rows, blocks, edge, left, middle, right)
        for i, (index, row) in enumerate(((0, 0), (3, last))):
            decode_rows(own, index, 1, bias, left, middle, right, taps, wide, staged, 2 * i)
            copies.append(
                pltpu.make_async_copy(
                    staged.at[:, pl.ds(2 * i, 2)], out.at[:, pl.ds(row, 2)], sem.at[i]
                )
            )
            copies[-1].start()
        for c in copies:
            c.wait()

    return pl.pallas_call(
        kernel,
        out_shape=shape((tiles * frames, 2 * grid_rows, 2 * own, width), BF16),
        in_specs=[IN_VMEM] * 5,
        out_specs=IN_HBM,
        scratch_shapes=decode_scratch(6, 1, total, channels, width)
        + [
            pltpu.VMEM((tiles * frames, 4, 2 * own, width), BF16),
            pltpu.SemaphoreType.DMA((3,)),
        ],
        name="border",
        compiler_params=params(24),
    )(blocks, edge, interior, taps, bias)


def round_call(step, last, got, total, carry):
    def kernel(got, total, *refs):
        upper = (lax.axis_index("tm") // step) % 2 == 1
        received = got[...].astype(F32)
        before = jnp.where(upper, received, 0.0)
        if carry is not None:
            before = refs[0][...] + before
            refs = refs[1:]
        if last:
            refs[0][...] = before.astype(BF16)
        else:
            carry_out, total_out, sent_out = refs
            carry_out[...] = before
            both = total[...] + received
            total_out[...] = both
            sent_out[...] = both.astype(BF16)

    near = [got, total] + ([] if carry is None else [carry])
    kinds = [BF16] if last else [F32, F32, BF16]
    return pl.pallas_call(
        kernel,
        out_shape=[shape(total.shape, kind) for kind in kinds],
        in_specs=[IN_VMEM] * len(near),
        out_specs=[IN_VMEM] * len(kinds),
        name="round",
        compiler_params=params(4),
    )(*near)


def prefix_rounds(total, sent, tiles):
    carry = None
    step, number = 1, 0
    while step < tiles:
        last = 2 * step >= tiles
        got = lax.ppermute(sent, "tm", [(i, i ^ step) for i in range(tiles)])
        out = round_call(step, last, got, total, carry)
        if last:
            return out[0]
        carry, total, sent = out
        step *= 2
        number += 1
    return jnp.zeros_like(sent)


SWAP = [(0, 1), (1, 0)]


def body(video, w_query, w_key, w_value, w_out, w_latent, conv_weight, conv_bias):
    frames, grid_rows, columns, d = video.shape
    tiles = lax.axis_size("tm")
    own = columns // tiles
    flat = video.reshape(-1, d)
    heads = d // HEAD
    split = heads - heads // 4 * 2
    parts_a, near, wk_b, wv_b, near_query = first_states(
        flat, w_key, w_value, w_query, frames, split
    )
    other_a = lax.ppermute(parts_a, "space", SWAP)
    parts_b, mine_b, theirs_b = second_states(near, wk_b, wv_b, frames)
    got_b = lax.ppermute(theirs_b, "space", SWAP)
    other_b = lax.ppermute(parts_b, "space", SWAP)
    total_a = total_call(parts_a, other_a)
    total_b = add_call(mine_b, got_b)

    ready = {}
    for name, first, parts, other, (total, sent) in (
        ("a", 0, parts_a, other_a, total_a), ("b", split, parts_b, other_b, total_b),
    ):
        count = parts.shape[1]
        cuts = [first, first + 2, first + count] if name == "a" else [first, first + count]
        queries = []
        for low, high in zip(cuts, cuts[1:]):
            queries.append(
                query_call(near, near_query, low * HEAD, (high - low) * HEAD)
            )
        carry = prefix_rounds(total, sent, tiles)
        other_carry = lax.ppermute(carry, "space", SWAP)
        ready[name] = (queries, parts, other, carry, other_carry)

    partial = partial_call(near, ready["a"], w_out, frames)
    chunk_b = (ready["b"][0][0],) + ready["b"][1:]
    partial = own_call(partial, chunk_b, w_out, frames)
    blocks = latent_call(partial, chunk_b, w_out, w_latent, frames, columns, tiles)
    blocks = lax.all_to_all(blocks, "tm", 0, 0, tiled=True)
    return decode(blocks, conv_weight, conv_bias, frames, grid_rows, own, tiles)


def decode(blocks, conv_weight, conv_bias, frames, grid_rows, own, tiles):
    channels = conv_weight.shape[2]
    width = conv_weight.shape[3]
    group = frames * own
    main = grid_rows * group

    def edge_kernel(blocks, out):
        def take(r):
            for t in range(tiles):
                out[t, :group] = blocks[t, r * group : (r + 1) * group]
                sides = blocks[t, main:].astype(F32)
                out[t, group:] = jnp.concatenate(
                    [sides[k * grid_rows + r : k * grid_rows + r + 1] for k in range(2 * frames)],
                    axis=0,
                ).astype(BF16)

        upper = lax.axis_index("space") == 0

        @pl.when(upper)
        def _():
            take(grid_rows - 1)

        @pl.when(jnp.logical_not(upper))
        def _():
            take(0)

    mine = pl.pallas_call(
        edge_kernel,
        out_shape=shape((tiles, group + 2 * frames, channels), BF16),
        in_specs=[IN_VMEM],
        out_specs=IN_VMEM,
        name="edge",
        compiler_params=params(4),
    )(blocks)
    beside = lax.ppermute(mine, "space", SWAP)
    bias = conv_bias.reshape(1, width)
    interior, taps = interior_call(
        blocks, conv_weight, bias, frames, tiles, grid_rows, own
    )
    return border_call(blocks, beside, interior, taps, bias, frames, tiles, grid_rows, own)


def solution(mesh):
    assert mesh.shape["space"] == 2
    tiles = mesh.shape["tm"]
    assert tiles & (tiles - 1) == 0
    placed = (P(("groups", "tm"), "space", None, None), P(), P(), P(), P(), P(), P(), P())
    return jax.shard_map(
        body,
        mesh=mesh,
        in_specs=placed,
        out_specs=P("groups", "space", "tm", None),
        check_vma=False,
    )
```

```python
import functools

import jax
import jax.numpy as jnp
from jax import lax
from jax.experimental import pallas as pl
from jax.experimental.pallas import tpu as pltpu
from jax.sharding import PartitionSpec as P


HEAD = 128
EPS = 1e-06
BF16 = jnp.bfloat16
F32 = jnp.float32


IN_HBM = pl.BlockSpec(memory_space=pltpu.HBM)
IN_VMEM = pl.BlockSpec(memory_space=pltpu.VMEM)


def shape(dims, dtype):
    return jax.ShapeDtypeStruct(dims, dtype)


def params(megabytes):
    return pltpu.CompilerParams(vmem_limit_bytes=megabytes << 20)


def in_hbm(x):
    return pltpu.with_memory_space_constraint(x, pltpu.HBM)


def matmul(a, b):
    return jnp.dot(a, b, preferred_element_type=F32)


def features(x):
    return jnp.where(x > 0.0, x + 1.0, jnp.exp(jnp.minimum(x, 0.0)))


def states_kernel(frames, heads, fetched, video_in, wk_hbm, wv_hbm, *refs):
    if fetched:
        parts_out, mine_out, theirs_out, key, value = refs
        video, wk, wv = video_in, wk_hbm, wv_hbm
        late = []
    else:
        (wq_hbm, parts_out, video, wk_out, wv_out, wq_out, wk, wv, key, value,
         wk_sem, wv_sem, video_sem, late_sem) = refs
        rest = wk_out.shape[1]
        source = pl.ds(heads * HEAD, rest)
        late = [
            pltpu.make_async_copy(wq_hbm, wq_out, late_sem.at[0]),
            pltpu.make_async_copy(wk_hbm.at[:, source], wk_out, late_sem.at[1]),
            pltpu.make_async_copy(wv_hbm.at[:, source], wv_out, late_sem.at[2]),
        ]
    per = video.shape[0] // frames

    def weight_copies(h):
        cols = pl.ds(pl.multiple_of(h * HEAD, HEAD), HEAD)
        return (
            pltpu.make_async_copy(wk_hbm.at[:, cols], wk.at[:, cols], wk_sem.at[h]),
            pltpu.make_async_copy(wv_hbm.at[:, cols], wv.at[:, cols], wv_sem.at[h]),
        )

    def video_copy(f):
        rows = pl.ds(f * per, per)
        return pltpu.make_async_copy(video_in.at[rows], video.at[rows], video_sem.at[f])

    if not fetched:
        soon = min(2, heads)
        for f in range(frames):
            video_copy(f).start()
        for h in range(soon):
            for c in weight_copies(h):
                c.start()
        for f in range(frames):
            video_copy(f).wait()
        for h in range(soon, heads):
            for c in weight_copies(h):
                c.start()
        for c in late:
            c.start()

    def one_head(h, carry):
        if not fetched:
            for c in weight_copies(h):
                c.wait()
        cols = pl.ds(pl.multiple_of(h * HEAD, HEAD), HEAD)
        both = jnp.concatenate([wk[:, cols], wv[:, cols]], axis=1)
        for f in range(frames):
            rows = slice(f * per, (f + 1) * per)
            kv = matmul(video[rows, :], both)
            key[h, rows, :] = features(kv[:, :HEAD]).astype(BF16)
            value[h, rows, :] = kv[:, HEAD:].astype(BF16)
        return carry

    lax.fori_loop(0, heads, one_head, 0)

    totals = []
    for h in range(heads):
        total = None
        for f in range(frames):
            rows = slice(f * per, (f + 1) * per)
            state = lax.dot_general(
                key[h, rows, :], value[h, rows, :], (((0,), (0,)), ((), ())),
                preferred_element_type=F32,
            )
            parts_out[f, h] = state.astype(BF16)
            total = state if total is None else total + state
        totals.append(total)
    if fetched:
        lower = lax.axis_index("space") == 0
        half = heads // 2
        for h in range(half):
            mine_out[h] = jnp.where(lower, totals[h], totals[half + h])
            theirs_out[h] = jnp.where(lower, totals[half + h], totals[h]).astype(BF16)
    for c in late:
        c.wait()


def first_states(video, wk, wv, wq, frames, heads):
    tokens, d = video.shape
    width = heads * HEAD
    return pl.pallas_call(
        functools.partial(states_kernel, frames, heads, False),
        out_shape=[
            shape((frames, heads, HEAD, HEAD), BF16),
            shape((tokens, d), BF16),
            shape((d, d - width), BF16),
            shape((d, d - width), BF16),
            shape((d, d), BF16),
        ],
        in_specs=[IN_HBM] * 4,
        out_specs=[IN_VMEM] * 5,
        scratch_shapes=[
            pltpu.VMEM((d, width), BF16),
            pltpu.VMEM((d, width), BF16),
            pltpu.VMEM((heads, tokens, HEAD), BF16),
            pltpu.VMEM((heads, tokens, HEAD), BF16),
            pltpu.SemaphoreType.DMA((heads,)),
            pltpu.SemaphoreType.DMA((heads,)),
            pltpu.SemaphoreType.DMA((frames,)),
            pltpu.SemaphoreType.DMA((3,)),
        ],
        name="states",
        compiler_params=params(20),
    )(in_hbm(video), in_hbm(wk), in_hbm(wv), in_hbm(wq))


def second_states(video, wk, wv, frames):
    tokens, _ = video.shape
    heads = wk.shape[1] // HEAD
    return pl.pallas_call(
        functools.partial(states_kernel, frames, heads, True),
        out_shape=[
            shape((frames, heads, HEAD, HEAD), BF16),
            shape((heads // 2, HEAD, HEAD), F32),
            shape((heads // 2, HEAD, HEAD), BF16),
        ],
        in_specs=[IN_VMEM] * 3,
        out_specs=[IN_VMEM] * 3,
        scratch_shapes=[
            pltpu.VMEM((heads, tokens, HEAD), BF16),
            pltpu.VMEM((heads, tokens, HEAD), BF16),
        ],
        name="states",
        compiler_params=params(20),
    )(video, wk, wv)


def total_call(parts, other_parts):
    frames, heads = parts.shape[:2]
    half = HEAD // 2

    def kernel(parts, other_parts, out, sent):
        low = lax.axis_index("space") == 0
        for h in range(heads):
            total = None
            for f in range(frames):
                one = parts[f, h].astype(F32) + other_parts[f, h].astype(F32)
                total = one if total is None else total + one
            total = jnp.where(low, total[:half], total[half:])
            out[h] = total
            sent[h] = total.astype(BF16)

    dims = (heads, half, HEAD)
    return pl.pallas_call(
        kernel,
        out_shape=[shape(dims, F32), shape(dims, BF16)],
        in_specs=[IN_VMEM] * 2,
        out_specs=[IN_VMEM] * 2,
        name="total",
        compiler_params=params(4),
    )(parts, other_parts)


def add_call(mine, got):
    def kernel(mine, got, out, sent):
        total = mine[...] + got[...].astype(F32)
        out[...] = total
        sent[...] = total.astype(BF16)

    return pl.pallas_call(
        kernel,
        out_shape=[shape(mine.shape, F32), shape(mine.shape, BF16)],
        in_specs=[IN_VMEM] * 2,
        out_specs=[IN_VMEM] * 2,
        name="add",
        compiler_params=params(4),
    )(mine, got)


def query_call(video, w, first, width):
    def kernel(video, w, out):
        out[...] = features(matmul(video[...], w[:, first : first + width])).astype(BF16)

    return pl.pallas_call(
        kernel,
        out_shape=shape((video.shape[0], width), BF16),
        in_specs=[IN_VMEM] * 2,
        out_specs=IN_VMEM,
        name="query",
        compiler_params=params(16),
    )(video, w)


def attend(frames, queries, parts, other_parts, carry, other_carry, used, head_out):
    heads = carry.shape[0]
    per = head_out.shape[0] // frames
    low = lax.axis_index("space") == 0
    used[...] = jnp.zeros_like(used)
    for h in range(heads):
        mine, theirs = carry[h].astype(F32), other_carry[h].astype(F32)
        running = jnp.concatenate(
            [jnp.where(low, mine, theirs), jnp.where(low, theirs, mine)], axis=0
        )
        at = (h % 2) * HEAD
        for f in range(frames):
            running = running + parts[f, h].astype(F32) + other_parts[f, h].astype(F32)
            used[f, h // 2, at : at + HEAD, at : at + HEAD] = running.astype(BF16)
    for f in range(frames):
        rows = slice(f * per, (f + 1) * per)
        for p in range(pl.cdiv(heads, 2)):
            width = min(2, heads - 2 * p) * HEAD
            first = 2 * p * HEAD
            query, at = queries[0], first
            for piece in queries[1:]:
                if at < query.shape[1]:
                    break
                query, at = piece, at - query.shape[1]
            attended = matmul(query[rows, at : at + width], used[f, p, :width, :width])
            for h in range(width // HEAD):
                one = attended[:, h * HEAD : (h + 1) * HEAD]
                scale = lax.rsqrt(jnp.mean(one * one, axis=1, keepdims=True) + EPS)
                at = first + h * HEAD
                head_out[rows, at : at + HEAD] = (one * scale).astype(BF16)


def used_shape(frames, heads):
    return pltpu.VMEM((frames, pl.cdiv(heads, 2), 2 * HEAD, 2 * HEAD), BF16)


def partial_call(video, chunk, w_out, frames):
    tokens, d = video.shape
    heads = chunk[3].shape[0]

    queries, chunk = chunk[0], chunk[1:]
    n = len(queries)

    def kernel(video, *refs):
        parts, other_parts, carry, other_carry, w_out, out, used, head_out = refs[n:]
        attend(frames, refs[:n], parts, other_parts, carry, other_carry, used, head_out)
        per = tokens // frames
        for f in range(frames):
            rows = slice(f * per, (f + 1) * per)
            out[rows, :] = video[rows, :].astype(F32) + matmul(
                head_out[rows, :], w_out[: heads * HEAD, :]
            )

    return pl.pallas_call(
        kernel,
        out_shape=shape((tokens, d), F32),
        in_specs=[IN_VMEM] * (n + 6),
        out_specs=IN_VMEM,
        scratch_shapes=[used_shape(frames, heads), pltpu.VMEM((tokens, heads * HEAD), BF16)],
        name="partial",
        compiler_params=params(20),
    )(video, *queries, *chunk, w_out)


def attend_half(frames, half, query, parts, other_parts, carry, used, head_out):
    heads = carry.shape[0]
    per = head_out.shape[0] // frames
    used[...] = jnp.zeros_like(used)
    for h in range(heads):
        running = carry[h].astype(F32)
        at = (h % 2) * HEAD
        for f in range(frames):
            own = half * heads + h
            running = running + parts[f, own].astype(F32) + other_parts[f, own].astype(F32)
            used[f, h // 2, at : at + HEAD, at : at + HEAD] = running.astype(BF16)
    for f in range(frames):
        rows = slice(f * per, (f + 1) * per)
        for p in range(pl.cdiv(heads, 2)):
            width = min(2, heads - 2 * p) * HEAD
            first = 2 * p * HEAD
            cols = pl.ds(pl.multiple_of(half * heads * HEAD + first, HEAD), width)
            attended = matmul(query[rows, cols], used[f, p, :width, :width])
            for h in range(width // HEAD):
                one = attended[:, h * HEAD : (h + 1) * HEAD]
                scale = lax.rsqrt(jnp.mean(one * one, axis=1, keepdims=True) + EPS)
                at = first + h * HEAD
                head_out[rows, at : at + HEAD] = (one * scale).astype(BF16)


def half_rows(w_out, half, width):
    first = w_out.shape[0] - 2 * width
    return w_out[pl.ds(pl.multiple_of(first + half * width, HEAD), width), :]


def own_call(partial, chunk, w_out, frames):
    query, parts, other_parts, carry, _ = chunk
    tokens, d = partial.shape
    heads = carry.shape[0]
    width = heads * HEAD

    def kernel(partial, query, parts, other_parts, carry, w_out, out, used, head_out):
        half = lax.axis_index("space")
        attend_half(frames, half, query, parts, other_parts, carry, used, head_out)
        w = half_rows(w_out, half, width)
        per = tokens // frames
        for f in range(frames):
            rows = slice(f * per, (f + 1) * per)
            out[rows, :] = partial[rows, :] + matmul(head_out[rows, :], w)

    return pl.pallas_call(
        kernel,
        out_shape=shape((tokens, d), F32),
        in_specs=[IN_VMEM] * 6,
        out_specs=IN_VMEM,
        scratch_shapes=[used_shape(frames, heads), pltpu.VMEM((tokens, width), BF16)],
        name="own",
        compiler_params=params(20),
    )(partial, query, parts, other_parts, carry, w_out)


def latent_kernel(
    frames, columns, tiles, partial, query, parts, other_parts, carry,
    w_out, w_latent, out, used, head_out, latent,
):
    tokens, _ = partial.shape
    per = tokens // frames
    half = 1 - lax.axis_index("space")
    attend_half(frames, half, query, parts, other_parts, carry, used, head_out)
    w = half_rows(w_out, half, head_out.shape[1])
    for f in range(frames):
        rows = slice(f * per, (f + 1) * per)
        summed = partial[rows, :] + matmul(head_out[rows, :], w)
        scale = lax.rsqrt(jnp.mean(summed * summed, axis=1, keepdims=True) + EPS)
        latent[rows, :] = matmul(summed.astype(BF16), w_latent[...]) * scale

    own = columns // tiles
    grid_rows = per // columns
    main = grid_rows * frames * own
    for t in range(tiles):
        for r in range(grid_rows):
            block = [
                latent[pl.ds(f * per + r * columns + t * own, own), :] for f in range(frames)
            ]
            at = r * frames * own
            out[t, at : at + frames * own, :] = jnp.concatenate(block, axis=0).astype(BF16)
        sides = []
        for column in (t * own - 1, (t + 1) * own):
            for f in range(frames):
                if 0 <= column < columns:
                    at = f * per + column
                    sides.append(latent[pl.ds(at, grid_rows, stride=columns), :])
                else:
                    sides.append(jnp.zeros((grid_rows, out.shape[2]), F32))
        out[t, main:, :] = jnp.concatenate(sides, axis=0).astype(BF16)


def latent_call(partial, chunk, w_out, w_latent, frames, columns, tiles):
    query, parts, other_parts, _, other_carry = chunk
    tokens, _ = partial.shape
    channels = w_latent.shape[1]
    heads = other_carry.shape[0]
    rows = tokens // columns * (columns // tiles + 2)
    return pl.pallas_call(
        functools.partial(latent_kernel, frames, columns, tiles),
        out_shape=shape((tiles, rows, channels), BF16),
        in_specs=[IN_VMEM] * 7,
        out_specs=IN_VMEM,
        scratch_shapes=[
            used_shape(frames, heads),
            pltpu.VMEM((tokens, heads * HEAD), BF16),
            pltpu.VMEM((tokens, channels), F32),
        ],
        name="latent",
        compiler_params=params(20),
    )(partial, query, parts, other_parts, other_carry, w_out, w_latent)


def lay_rows(frames, tiles, grid_rows, own, rows, blocks, edge, left, middle, right):
    group = frames * own
    main = grid_rows * group
    channels = left.shape[-1]
    column = lax.broadcasted_iota(jnp.int32, (group, 1), 0) % own

    def lay(index, t, body, sides):
        at = slice(t * group, (t + 1) * group)
        first, last = (
            jnp.concatenate(
                [jnp.broadcast_to(sides[k : k + 1], (own, channels))
                 for k in range(side * frames, (side + 1) * frames)], axis=0
            )
            for side in range(2)
        )
        down = pltpu.roll(body, 1, 0)
        up = pltpu.roll(body, group - 1, 0)
        left[index, at, :] = jnp.where(column == 0, first, down).astype(BF16)
        middle[index, at, :] = body.astype(BF16)
        right[index, at, :] = jnp.where(column == own - 1, last, up).astype(BF16)

    for t in range(tiles):
        everything = blocks[t].astype(F32)
        beside = None if edge is None else edge[t].astype(F32)
        for index, row in enumerate(rows):
            if 0 <= row < grid_rows:
                sides = [
                    everything[main + k * grid_rows + row : main + k * grid_rows + row + 1]
                    for k in range(2 * frames)
                ]
                lay(index, t, everything[row * group : (row + 1) * group],
                    jnp.concatenate(sides, axis=0))
            else:
                present = lax.axis_index("space") == (1 if row < 0 else 0)
                there = jnp.where(present, beside, 0.0)
                lay(index, t, there[:group], there[group:])


def lay_taps(weight, taps):
    w = weight[...].astype(F32)
    channels = weight.shape[2]
    row_sets = (((0,), (1, 2)), ((0, 1), (2,)))
    for a in range(2):
        for b in range(2):
            for i, rows in enumerate(row_sets[a]):
                for j, cols in enumerate(row_sets[b]):
                    tap = sum(w[r, c] for r in rows for c in cols)
                    at = (2 * i + j) * channels
                    taps[2 * a + b, at : at + channels, :] = (0.5 * tap).astype(BF16)


def decode_rows(own, index, count, bias, left, middle, right, taps, wide, staged, first):
    views = ((left, middle), (middle, right))
    half_bias = 0.5 * bias[...]
    lanes = wide.shape[-1]
    total, channels = left.shape[1:]
    size = count * total
    for a in range(2):
        for b in range(2):
            lhs = jnp.concatenate(
                [v[index + a + k : index + a + k + count].reshape(size, channels)
                 for k in range(2) for v in views[b]], axis=1
            )
            h = matmul(lhs, taps[2 * a + b]) + half_bias
            value = h + h * jnp.tanh(h)
            for n in range(wide.shape[1]):
                wide[a, n, pl.ds(b, size, stride=2), :] = value[:, n * lanes : (n + 1) * lanes]
        for n in range(wide.shape[1]):
            shaped = wide[a, n].reshape(count, total // own, 2 * own, lanes)
            for r in range(count):
                staged[:, first + 2 * r + a, :, n * lanes : (n + 1) * lanes] = (
                    shaped[r].astype(BF16)
                )


def decode_scratch(rows, count, total, channels, width):
    return [pltpu.VMEM((rows, total, channels), BF16)] * 3 + [
        pltpu.VMEM((2, width // HEAD, 2 * count * total, HEAD), F32)
    ]


def taps_call(weight):
    channels, width = weight.shape[2:]
    return pl.pallas_call(
        lay_taps,
        out_shape=shape((4, 4 * channels, width), BF16),
        in_specs=[IN_VMEM],
        out_specs=IN_VMEM,
        name="taps",
        compiler_params=params(8),
    )(weight)


def interior_call(blocks, taps, bias, frames, tiles, grid_rows, own):
    channels, width = blocks.shape[2], taps.shape[2]
    total = tiles * frames * own
    count = 3 if (grid_rows - 2) % 3 == 0 else 1

    def kernel(blocks, taps, bias, out, left, middle, right, wide):
        lay_rows(frames, tiles, grid_rows, own, range(grid_rows), blocks, None,
                 left, middle, right)
        for i in range(0, grid_rows - 2, count):
            decode_rows(own, i, count, bias, left, middle, right, taps, wide, out, 2 * i)

    return pl.pallas_call(
        kernel,
        out_shape=shape((tiles * frames, 2 * (grid_rows - 2), 2 * own, width), BF16),
        in_specs=[IN_VMEM] * 3,
        out_specs=IN_VMEM,
        scratch_shapes=decode_scratch(grid_rows, count, total, channels, width),
        name="interior",
        compiler_params=params(24),
    )(blocks, taps, bias)


def border_call(blocks, edge, interior, taps, bias, frames, tiles, grid_rows, own):
    channels = blocks.shape[2]
    width = taps.shape[2]
    total = tiles * frames * own
    last = 2 * (grid_rows - 1)

    def kernel(blocks, edge, interior, taps, bias, out, left, middle, right, wide, staged, sem):
        copies = [pltpu.make_async_copy(interior, out.at[:, pl.ds(2, last - 2)], sem.at[2])]
        copies[0].start()
        rows = [-1, 0, 1, grid_rows - 2, grid_rows - 1, grid_rows]
        lay_rows(frames, tiles, grid_rows, own, rows, blocks, edge, left, middle, right)
        for i, (index, row) in enumerate(((0, 0), (3, last))):
            decode_rows(own, index, 1, bias, left, middle, right, taps, wide, staged, 2 * i)
            copies.append(
                pltpu.make_async_copy(
                    staged.at[:, pl.ds(2 * i, 2)], out.at[:, pl.ds(row, 2)], sem.at[i]
                )
            )
            copies[-1].start()
        for c in copies:
            c.wait()

    return pl.pallas_call(
        kernel,
        out_shape=shape((tiles * frames, 2 * grid_rows, 2 * own, width), BF16),
        in_specs=[IN_VMEM] * 5,
        out_specs=IN_HBM,
        scratch_shapes=decode_scratch(6, 1, total, channels, width)
        + [
            pltpu.VMEM((tiles * frames, 4, 2 * own, width), BF16),
            pltpu.SemaphoreType.DMA((3,)),
        ],
        name="border",
        compiler_params=params(24),
    )(blocks, edge, interior, taps, bias)


def round_call(step, last, got, total, carry):
    def kernel(got, total, *refs):
        upper = (lax.axis_index("tm") // step) % 2 == 1
        received = got[...].astype(F32)
        before = jnp.where(upper, received, 0.0)
        if carry is not None:
            before = refs[0][...] + before
            refs = refs[1:]
        if last:
            refs[0][...] = before.astype(BF16)
        else:
            carry_out, total_out, sent_out = refs
            carry_out[...] = before
            both = total[...] + received
            total_out[...] = both
            sent_out[...] = both.astype(BF16)

    near = [got, total] + ([] if carry is None else [carry])
    kinds = [BF16] if last else [F32, F32, BF16]
    return pl.pallas_call(
        kernel,
        out_shape=[shape(total.shape, kind) for kind in kinds],
        in_specs=[IN_VMEM] * len(near),
        out_specs=[IN_VMEM] * len(kinds),
        name="round",
        compiler_params=params(4),
    )(*near)


def prefix_rounds(total, sent, tiles):
    carry = None
    step, number = 1, 0
    while step < tiles:
        last = 2 * step >= tiles
        got = lax.ppermute(sent, "tm", [(i, i ^ step) for i in range(tiles)])
        out = round_call(step, last, got, total, carry)
        if last:
            return out[0]
        carry, total, sent = out
        step *= 2
        number += 1
    return jnp.zeros_like(sent)


SWAP = [(0, 1), (1, 0)]


def body(video, w_query, w_key, w_value, w_out, w_latent, conv_weight, conv_bias):
    frames, grid_rows, columns, d = video.shape
    tiles = lax.axis_size("tm")
    own = columns // tiles
    flat = video.reshape(-1, d)
    heads = d // HEAD
    split = heads - heads // 4 * 2
    parts_a, near, wk_b, wv_b, near_query = first_states(
        flat, w_key, w_value, w_query, frames, split
    )
    other_a = lax.ppermute(parts_a, "space", SWAP)
    parts_b, mine_b, theirs_b = second_states(near, wk_b, wv_b, frames)
    got_b = lax.ppermute(theirs_b, "space", SWAP)
    other_b = lax.ppermute(parts_b, "space", SWAP)
    total_a = total_call(parts_a, other_a)
    total_b = add_call(mine_b, got_b)

    ready = {}
    for name, first, parts, other, (total, sent) in (
        ("a", 0, parts_a, other_a, total_a), ("b", split, parts_b, other_b, total_b),
    ):
        count = parts.shape[1]
        cuts = [first, first + 2, first + count] if name == "a" else [first, first + count]
        queries = []
        for low, high in zip(cuts, cuts[1:]):
            queries.append(
                query_call(near, near_query, low * HEAD, (high - low) * HEAD)
            )
        carry = prefix_rounds(total, sent, tiles)
        other_carry = lax.ppermute(carry, "space", SWAP)
        ready[name] = (queries, parts, other, carry, other_carry)

    taps = taps_call(conv_weight)
    partial = partial_call(near, ready["a"], w_out, frames)
    chunk_b = (ready["b"][0][0],) + ready["b"][1:]
    partial = own_call(partial, chunk_b, w_out, frames)
    blocks = latent_call(partial, chunk_b, w_out, w_latent, frames, columns, tiles)
    blocks = lax.all_to_all(blocks, "tm", 0, 0, tiled=True)
    return decode(blocks, taps, conv_weight, conv_bias, frames, grid_rows, own, tiles)


def decode(blocks, taps, conv_weight, conv_bias, frames, grid_rows, own, tiles):
    channels = conv_weight.shape[2]
    width = conv_weight.shape[3]
    group = frames * own
    main = grid_rows * group

    def edge_kernel(blocks, out):
        def take(r):
            for t in range(tiles):
                out[t, :group] = blocks[t, r * group : (r + 1) * group]
                sides = blocks[t, main:].astype(F32)
                out[t, group:] = jnp.concatenate(
                    [sides[k * grid_rows + r : k * grid_rows + r + 1] for k in range(2 * frames)],
                    axis=0,
                ).astype(BF16)

        upper = lax.axis_index("space") == 0

        @pl.when(upper)
        def _():
            take(grid_rows - 1)

        @pl.when(jnp.logical_not(upper))
        def _():
            take(0)

    mine = pl.pallas_call(
        edge_kernel,
        out_shape=shape((tiles, group + 2 * frames, channels), BF16),
        in_specs=[IN_VMEM],
        out_specs=IN_VMEM,
        name="edge",
        compiler_params=params(4),
    )(blocks)
    beside = lax.ppermute(mine, "space", SWAP)
    bias = conv_bias.reshape(1, width)
    interior = interior_call(blocks, taps, bias, frames, tiles, grid_rows, own)
    return border_call(blocks, beside, interior, taps, bias, frames, tiles, grid_rows, own)


def solution(mesh):
    assert mesh.shape["space"] == 2
    tiles = mesh.shape["tm"]
    assert tiles & (tiles - 1) == 0
    placed = (P(("groups", "tm"), "space", None, None), P(), P(), P(), P(), P(), P(), P())
    return jax.shard_map(
        body,
        mesh=mesh,
        in_specs=placed,
        out_specs=P("groups", "space", "tm", None),
        check_vma=False,
    )
```
